32 devices in a mesh: dp: 8 (over y, x, core), expert: 4 (over z).
Axes of the slice: x: 2, y: 2, z: 4, core: 2. Of those that a mesh axis runs over, the one named last changes fastest.
Arguments:
- hidden_in: bfloat16 [32, 128, 2048], P(('dp', 'expert')), may hold values from -6 to 6
- out_grad: bfloat16 [32, 128, 2048], P(('dp', 'expert')), may hold values from -6 to 6
- seq_lengths: int32 [32], P('dp'), may hold values from 72 to 128, as said below
- attn_choice: int32 [32, 128, 2], P('dp'), may hold values from 0 to 3, as said below
- moe_choice: int32 [32, 128, 2], P('dp'), may hold values from 0 to 3, as said below
- attn_gain: float32 [2048], P('dp'), may hold values from 0.5 to 1.5
- moe_gain: float32 [2048], P('dp'), may hold values from 0.5 to 1.5
- attn_router: float32 [2048, 4], P('dp'), may hold values from -0.25 to 0.25
- moe_router: float32 [2048, 4], P('dp'), may hold values from -0.25 to 0.25
- key_weight: float32 [2048, 2048], P('dp'), may hold values from -0.125 to 0.125
- value_weight: float32 [2048, 2048], P('dp'), may hold values from -0.125 to 0.125
- query_weight: float32 [4, 2048, 2048], P('expert', 'dp'), may hold values from -0.125 to 0.125
- output_weight: float32 [4, 2048, 2048], P('expert', 'dp'), may hold values from -0.5 to 0.5
- gate_weight: float32 [4, 2048, 5632], P('expert', None, 'dp'), may hold values from -0.125 to 0.125
- up_weight: float32 [4, 2048, 5632], P('expert', None, 'dp'), may hold values from -0.125 to 0.125
- down_weight: float32 [4, 5632, 2048], P('expert', 'dp'), may hold values from -0.078125 to 0.078125
Outputs:
- block_out: bfloat16 [32, 128, 2048], P(('dp', 'expert'))
- input_grad: bfloat16 [32, 128, 2048], P(('dp', 'expert'))
- attn_gain_grad: float32 [2048], P(('dp', 'expert'))
- moe_gain_grad: float32 [2048], P(('dp', 'expert'))
- attn_router_grad: float32 [2048, 4], P(('dp', 'expert'))
- moe_router_grad: float32 [2048, 4], P(('dp', 'expert'))
- key_grad: float32 [2048, 2048], P(('dp', 'expert'))
- value_grad: float32 [2048, 2048], P(('dp', 'expert'))
- query_grad: float32 [4, 2048, 2048], P('expert', 'dp')
- output_grad: float32 [4, 2048, 2048], P('expert', 'dp')
- gate_grad: float32 [4, 2048, 5632], P('expert', None, 'dp')
- up_grad: float32 [4, 2048, 5632], P('expert', None, 'dp')
- down_grad: float32 [4, 5632, 2048], P('expert', 'dp')
The draws below stay inside these ranges and needn't reach their ends.
Inputs may be any that keep to these rules, and one draw needn't show every extreme that they name: `seq_lengths`: every aligned block of 4 sequences holds one of length 128. `attn_choice`: each token names 2 different experts. Over the positions below its sequence's length, no expert is named by more than 72 tokens of one sequence, and in every aligned block of 4 sequences some expert is named by exactly 72 live tokens of each of them. Entries at padded positions carry no meaning. `moe_choice`: as for attn_choice, drawn independently.
All inputs are finite; a program needn't handle non-finite values.
Results may differ from the reference program's by a relative error of at most 0.019.
The reference program's roundings to bfloat16 on the way count: a program that leaves them out, or rounds other values in their place, can miss the bound.
Values may be sent and summed in bfloat16 or wider, within the bound.
A program may use at most 384 MiB of HBM per device.

```python
import jax
import jax.numpy as jnp
from jax import lax

D = 2048
FF = 5632
HEADS = 16
HEAD = 128
LEN = 128
EXPERTS = 4
SEQS = 32
CAP = 72
MINLEN = 72


def lengths_common(key):
    drawn = jax.random.randint(jax.random.fold_in(key, 11), (SEQS,), MINLEN, LEN + 1)
    full_at = jax.random.randint(jax.random.fold_in(key, 12), (SEQS // EXPERTS,), 0, EXPERTS)
    group_of = jnp.arange(SEQS, dtype=jnp.int32) // EXPERTS
    inside = jnp.arange(SEQS, dtype=jnp.int32) % EXPERTS
    return jnp.where(inside == full_at[group_of], LEN, drawn).astype(jnp.int32)


def route_one(seq_key, length_value, hot_expert):
    order_key = jax.random.fold_in(seq_key, 1)
    label_key = jax.random.fold_in(seq_key, 2)
    swap_key = jax.random.fold_in(seq_key, 3)
    shuffled = jax.random.permutation(order_key, LEN).astype(jnp.int32)
    places = jnp.arange(LEN, dtype=jnp.int32)
    ranking = shuffled + LEN * (places >= length_value).astype(jnp.int32)
    ranks = jnp.argsort(jnp.argsort(ranking)).astype(jnp.int32)
    labels = jax.random.permutation(label_key, EXPERTS).astype(jnp.int32)
    hot_at = jnp.argmax(labels == hot_expert).astype(jnp.int32)
    others = EXPERTS - 1
    first_index = jnp.where(ranks < CAP, 0, 1 + jnp.remainder(ranks - CAP, others))
    second_index = 1 + jnp.remainder(ranks - CAP + 1, others)
    first_id = labels[jnp.remainder(hot_at + first_index, EXPERTS)]
    second_id = labels[jnp.remainder(hot_at + second_index, EXPERTS)]
    swapped = jax.random.randint(swap_key, (LEN,), 0, 2)
    return jnp.stack([jnp.where(swapped == 1, second_id, first_id), jnp.where(swapped == 1, first_id, second_id)], axis=-1).astype(jnp.int32)


def draw_routes(key, salt):
    lengths_all = lengths_common(key)
    route_key = jax.random.fold_in(key, salt)
    hot_groups = jax.random.randint(jax.random.fold_in(route_key, 1), (SEQS // EXPERTS,), 0, EXPERTS)
    hot_each = hot_groups[jnp.arange(SEQS, dtype=jnp.int32) // EXPERTS].astype(jnp.int32)
    seq_keys = jax.random.split(jax.random.fold_in(route_key, 2), SEQS)
    return jax.vmap(route_one)(seq_keys, lengths_all, hot_each)


def draw_seq_lengths(key, part):
    return lengths_common(key)


def draw_attn_choice(key, part):
    return draw_routes(key, 101)


def draw_moe_choice(key, part):
    return draw_routes(key, 202)


def raised(values, rng, source, target, shards_of, factor):
    def block_of(position):
        return (jnp.arange(values.shape[position]) // (values.shape[position] // shards_of)).reshape((-1,) + (1,) * (values.ndim - 1 - position))

    first = jax.random.permutation(rng, shards_of)[block_of(target)]
    second = (block_of(target) + shards_of // 2) % shards_of
    return jnp.where((block_of(source) == first) | (block_of(source) == second), factor * values, values)


def levels(stream_key, dims, shards, least, high):
    factor_of = 1.0
    for axis_at, parts in shards:
        draws = jax.random.uniform(jax.random.fold_in(jax.random.fold_in(stream_key, 6), axis_at), (parts,), jnp.float32, least / len(shards), high / len(shards))
        factor_of = factor_of * jnp.repeat(jnp.exp(draws), dims[axis_at] // parts).reshape((-1,) + (1,) * (len(dims) - 1 - axis_at))
    return factor_of


def centred(stream_key, dims, spread, reach, pieces=(), kind=jnp.bfloat16):
    values = jax.random.normal(stream_key, dims, jnp.float32) * spread
    if len(pieces) > 0:
        values = levels(stream_key, dims, pieces, -0.22, 0.18) * values
    return jnp.clip(values, min=-reach, max=reach).astype(kind)


def noise_with(stream_key, extent, scale, most, cuts, heavy, kind=jnp.bfloat16):
    result = scale * jax.random.normal(stream_key, extent, jnp.float32)
    if cuts:
        result = result * levels(stream_key, extent, cuts, -0.22, 0.18)
    return jnp.clip(raised(result, jax.random.fold_in(stream_key, 3), *heavy), -most, most).astype(kind)


def setup_inputs(seed: int = 0) -> dict:
    seeds = jax.random.split(jax.random.key(seed), 17)
    hidden_in = noise_with(seeds[0], (SEQS, LEN, D), 1.0, 6.0, ((0, 32),), (0, 2, 32, 2.75))
    out_grad = centred(seeds[1], (SEQS, LEN, D), 1.0, 6.0, ((0, 32),))
    seq_lengths = draw_seq_lengths(jax.random.fold_in(seeds[16], 71), 0)
    attn_choice = draw_attn_choice(jax.random.fold_in(seeds[16], 71), 0)
    moe_choice = draw_moe_choice(jax.random.fold_in(seeds[16], 71), 0)
    attn_gain = jnp.clip(1.0 + 0.1 * jax.random.normal(seeds[5], (D,), jnp.float32), 0.5, 1.5)
    moe_gain = jnp.clip(1.0 + 0.1 * jax.random.normal(seeds[6], (D,), jnp.float32), 0.5, 1.5)
    attn_router = centred(seeds[7], (D, EXPERTS), (D // 4) ** -0.5, 0.25, ((0, 8),), jnp.float32)
    moe_router = centred(seeds[8], (D, EXPERTS), (D // 4) ** -0.5, 0.25, ((0, 8),), jnp.float32)
    key_weight = centred(seeds[9], (D, HEADS * HEAD), D ** -0.5, 0.125, ((0, 8),), jnp.float32)
    value_weight = centred(seeds[10], (D, HEADS * HEAD), D ** -0.5, 0.125, ((0, 8),), jnp.float32)
    query_weight = centred(seeds[11], (EXPERTS, D, HEADS * HEAD), D ** -0.5, 0.125, ((0, 4), (1, 8)), jnp.float32)
    output_weight = centred(seeds[12], (EXPERTS, HEADS * HEAD, D), (HEADS * HEAD // 16) ** -0.5, 0.5, ((0, 4), (1, 8)), jnp.float32)
    gate_weight = centred(seeds[13], (EXPERTS, D, FF), D ** -0.5, 0.125, ((0, 4), (2, 8)), jnp.float32)
    up_weight = centred(seeds[14], (EXPERTS, D, FF), D ** -0.5, 0.125, ((0, 4), (2, 8)), jnp.float32)
    down_weight = centred(seeds[15], (EXPERTS, FF, D), FF ** -0.5, 0.078125, ((0, 4), (1, 8)), jnp.float32)
    return dict(hidden_in=hidden_in, out_grad=out_grad, seq_lengths=seq_lengths, attn_choice=attn_choice, moe_choice=moe_choice, attn_gain=attn_gain, moe_gain=moe_gain, attn_router=attn_router, moe_router=moe_router, key_weight=key_weight, value_weight=value_weight, query_weight=query_weight, output_weight=output_weight, gate_weight=gate_weight, up_weight=up_weight, down_weight=down_weight)


@jax.custom_vjp
def low(v):
    return lax.optimization_barrier(v.astype(jnp.bfloat16)).astype(jnp.float32)

@jax.custom_vjp
def low_back(v):
    return v

def low_keep(v):
    return (low(v), None)

def low_pass(kept, grad):
    return (grad,)

def back_keep(v):
    return (v, None)

def back_low(kept, grad):
    return (low(grad),)
low.defvjp(low_keep, low_pass)
low_back.defvjp(back_keep, back_low)
eps = 1e-06
theta = 10000.0
highest = lax.Precision.HIGHEST

def rope_tables(positions, head_size):
    half_size = head_size // 2
    frequency = theta ** (-(jnp.arange(half_size, dtype=jnp.float32) * 2.0 / head_size))
    angles = positions.astype(jnp.float32)[:, None] * frequency[None, :]
    return (jnp.cos(angles), jnp.sin(angles))

def rotate(value, cosine, sine, direction):
    half_size = value.shape[-1] // 2
    former = value[..., :half_size]
    latter = value[..., half_size:]
    cosine = cosine[:, None, :]
    sine = direction * sine[:, None, :]
    return jnp.concatenate([former * cosine - latter * sine, latter * cosine + former * sine], axis=-1)

def project(left, right):
    return jnp.einsum('...d,de->...e', left, right, precision=highest)

def norm_apply(value, gain_value):
    scale_value = lax.rsqrt(lax.optimization_barrier(jnp.mean(value * value, axis=-1, keepdims=True)) + eps)
    return value * scale_value * gain_value

def softmax_rows(values):
    peak = lax.optimization_barrier(jnp.max(values, axis=-1, keepdims=True))
    powers = jnp.exp(values - peak)
    return powers / lax.optimization_barrier(jnp.sum(powers, axis=-1, keepdims=True))

def dense_gates(logits, choices, live_rows):
    onehot = (choices[..., None] == jnp.arange(EXPERTS, dtype=jnp.int32)).astype(jnp.float32)
    chosen = lax.optimization_barrier(jnp.sum(logits[..., None, :] * onehot, axis=-1))
    shares = softmax_rows(chosen) * live_rows[..., None]
    return lax.optimization_barrier(jnp.sum(shares[..., None] * onehot, axis=-2))

def reference(hidden_in, out_grad, seq_lengths, attn_choice, moe_choice, attn_gain, moe_gain, attn_router, moe_router, key_weight, value_weight, query_weight, output_weight, gate_weight, up_weight, down_weight):
    places = jnp.arange(LEN, dtype=jnp.int32)
    live_rows = (places[None, :] < seq_lengths[:, None]).astype(jnp.float32)
    visible = (places[None, :] <= places[:, None])[None, None] & (places[None, None, None, :] < seq_lengths[:, None, None, None])
    cosine, sine = rope_tables(places, HEAD)
    score_scale = HEAD ** (-0.5)

    def forward(inputs_f, gain_one, gain_two, router_one, router_two, key_full, value_full, query_full, output_full, gate_full, up_full, down_full):
        gain_one = low(gain_one)
        gain_two = low(gain_two)
        router_one = low(router_one)
        router_two = low(router_two)
        key_full = low(key_full)
        value_full = low(value_full)
        query_full = low(query_full)
        output_full = low(output_full)
        gate_full = low(gate_full)
        up_full = low(up_full)
        down_full = low(down_full)
        normed_one = low(norm_apply(inputs_f, gain_one))
        key_pre = low_back(project(normed_one, key_full))
        keys = low(rotate(key_pre.reshape(SEQS, LEN, HEADS, HEAD), cosine, sine, 1.0))
        values = low_back(low(project(normed_one, value_full))).reshape(SEQS, LEN, HEADS, HEAD)
        gates_one = dense_gates(project(normed_one, router_one), attn_choice, live_rows)
        attn_sum = jnp.zeros_like(inputs_f)
        for expert in range(EXPERTS):
            expert_rows = low_back(normed_one)
            query_pre = low_back(project(expert_rows, query_full[expert]))
            queries = low(rotate(query_pre.reshape(SEQS, LEN, HEADS, HEAD), cosine, sine, 1.0))
            scores = low_back(jnp.einsum('sqhd,skhd->shqk', queries, keys, precision=highest) * score_scale)
            weights_attn = low(softmax_rows(jnp.where(visible, scores, -1e+30)))
            mixture = jnp.einsum('shqk,skhd->sqhd', weights_attn, values, precision=highest)
            heads_out = low_back(low(mixture.reshape(SEQS, LEN, HEADS * HEAD)))
            branch = low_back(low(project(heads_out, output_full[expert])))
            attn_sum = attn_sum + gates_one[..., expert:expert + 1] * branch
        middle = inputs_f + attn_sum
        normed_two = low(norm_apply(middle, gain_two))
        gates_two = dense_gates(project(normed_two, router_two), moe_choice, live_rows)
        moe_sum = jnp.zeros_like(inputs_f)
        for expert in range(EXPERTS):
            expert_rows = low_back(normed_two)
            gate_pre = low_back(project(expert_rows, gate_full[expert]))
            up_pre = low_back(project(expert_rows, up_full[expert]))
            activated = gate_pre * (1.0 / (1.0 + jnp.exp(-gate_pre)))
            hidden_rows = low(activated * up_pre)
            branch = low_back(low(project(hidden_rows, down_full[expert])))
            moe_sum = moe_sum + gates_two[..., expert:expert + 1] * branch
        return live_rows[..., None] * (middle + moe_sum)
    block_out, pullback = jax.vjp(forward, hidden_in.astype(jnp.float32), attn_gain, moe_gain, attn_router, moe_router, key_weight, value_weight, query_weight, output_weight, gate_weight, up_weight, down_weight)
    grads = pullback(out_grad.astype(jnp.float32))
    return (block_out.astype(jnp.bfloat16), grads[0].astype(jnp.bfloat16), grads[1], grads[2], grads[3], grads[4], grads[5], grads[6], grads[7], grads[8], grads[9], grads[10], grads[11])
```

```python
from functools import partial

import jax
import jax.numpy as jnp
from jax import lax
from jax.experimental import pallas as pl
from jax.experimental.pallas import tpu as pltpu
from jax.sharding import PartitionSpec as P

HEADS = 16
HEAD = 128
MESH = pl.DeviceIdType.MESH
ANY = pl.BlockSpec(memory_space=pl.ANY)

eps = 1e-06
theta = 10000.0
highest = lax.Precision.HIGHEST
f32 = jnp.float32
bf16 = jnp.bfloat16


def rope_tables(positions, head_size):
    half_size = head_size // 2
    frequency = theta ** (-(jnp.arange(half_size, dtype=f32) * 2.0 / head_size))
    angles = positions.astype(f32)[:, None] * frequency[None, :]
    return (jnp.cos(angles), jnp.sin(angles))


def signed_tables(positions):
    cosine, sine = rope_tables(positions, HEAD)
    return (jnp.concatenate([cosine, cosine], 1), jnp.concatenate([-sine, sine], 1))


def turned_back(value, tables):
    half_size = HEAD // 2
    swapped = jnp.concatenate([value[:, half_size:], value[:, :half_size]], axis=1)
    return value * tables[0] - swapped * tables[1]


def norm_scale(value):
    return lax.rsqrt(jnp.mean(value * value, axis=-1, keepdims=True) + eps)


def norm_backward(grad_normed, value, scale_value, gain_value):
    scaled_grad = grad_normed * gain_value
    gain_part = jnp.sum(grad_normed * value * scale_value, axis=0)
    grad_value = scale_value * scaled_grad - value * scale_value**3 * jnp.mean(
        scaled_grad * value, axis=-1, keepdims=True
    )
    return (grad_value, gain_part)


def softmax_rows(values):
    peak = jnp.max(values, axis=-1, keepdims=True)
    powers = jnp.exp(values - peak)
    return powers / jnp.sum(powers, axis=-1, keepdims=True)


def router_gates(logits, choices, live_rows, experts):
    onehot = (choices[:, :, None] == jnp.arange(experts, dtype=jnp.int32)[None, None, :]).astype(
        f32
    )
    chosen = jnp.sum(logits[:, None, :] * onehot, axis=-1)
    shares = softmax_rows(chosen)
    dense = jnp.sum((shares * live_rows[:, None])[:, :, None] * onehot, axis=1)
    return (onehot, shares, dense)


def gates_backward(grad_dense, onehot, shares, live_rows):
    grad_shares = jnp.sum(grad_dense[:, None, :] * onehot, axis=-1) * live_rows[:, None]
    grad_chosen = shares * (grad_shares - jnp.sum(shares * grad_shares, axis=-1, keepdims=True))
    return jnp.sum(grad_chosen[:, :, None] * onehot, axis=1)


def route_table(choices, length_value, experts, capacity):
    places = jnp.arange(choices.shape[0], dtype=jnp.int32)
    living = (places < length_value).astype(jnp.int32)
    picked = (
        jnp.sum(
            (choices[:, :, None] == jnp.arange(experts, dtype=jnp.int32)[None, None, :]).astype(
                jnp.int32
            ),
            axis=1,
        )
        * living[:, None]
    )
    slot_of = jnp.cumsum(picked, axis=0) - 1
    slot_ids = jnp.arange(capacity, dtype=jnp.int32)
    return (slot_of.T[:, None, :] == slot_ids[None, :, None]) & (picked.T[:, None, :] == 1)


def flip(index, bit):
    return index + bit * (1 - 2 * ((index // bit) % 2))


def flips(index, mask, bits):
    for bit in bits:
        if mask & bit:
            index = flip(index, bit)
    return index


def span(bits):
    masks = [0]
    for bit in bits:
        masks = masks + [mask | bit for mask in masks]
    return masks


def bit_orders(size):
    bits = [1 << k for k in range(size.bit_length() - 1)]
    high = bits[1:]
    return (high + bits[:1], high[::-1] + bits[:1])


def barrier(targets):
    semaphore = pltpu.get_barrier_semaphore()
    for target in targets:
        pl.semaphore_signal(semaphore, inc=1, device_id=target, device_id_type=MESH)
    pl.semaphore_wait(semaphore, len(targets))


def gather_kernel(groups, experts, splits, axes, *refs):
    count = len(splits)
    shards, home = refs[:count], refs[count]
    fulls, home_all = refs[count + 1 : 2 * count + 1], refs[2 * count + 1]
    local_sem, send_sem, recv_sem, home_send, home_recv = refs[2 * count + 2 :]
    group = lax.axis_index("dp")
    mine = lax.axis_index("expert")
    orders = bit_orders(groups)
    bits = sorted(orders[0])
    others = [(mine + step) % experts for step in range(1, experts)]
    barrier([(flip(group, bit), mine) for bit in bits] + [(group, other) for other in others])

    home_copies = []
    for step, other in enumerate(others):
        copy = pltpu.make_async_remote_copy(
            src_ref=home,
            dst_ref=home_all.at[mine],
            send_sem=home_send.at[step],
            recv_sem=home_recv.at[step],
            device_id=(group, other),
            device_id_type=MESH,
        )
        copy.start()
        home_copies.append(copy)

    def part(ref, which, block, half):
        pieces, axis = splits[which], axes[which]
        extent = shards[which].shape[axis]
        size = extent // pieces
        start = half * size if block is None else block * extent + half * size
        if block is not None:
            start = pl.multiple_of(start, size)
        where = pl.ds(start, size)
        return ref.at[where] if axis == 0 else ref.at[:, where]

    stages = {}
    slot = 0
    for which in range(count):
        for half in range(splits[which]):
            order = orders[half]
            for stage, bit in enumerate(order):
                copies = []
                for mask in span(order[:stage]):
                    block = flips(group, mask, bits)
                    target = part(fulls[which], which, block, half)
                    source = part(shards[which], which, None, half) if mask == 0 else target
                    copies.append(
                        pltpu.make_async_remote_copy(
                            src_ref=source,
                            dst_ref=target,
                            send_sem=send_sem.at[slot],
                            recv_sem=recv_sem.at[slot],
                            device_id=(flip(group, bit), mine),
                            device_id_type=MESH,
                        )
                    )
                    slot += 1
                stages[which, half, stage] = copies
    keys = [(which, half) for which in range(count) for half in range(splits[which])]
    for which, half in keys:
        for copy in stages[which, half, 0]:
            copy.start()
    local = [pltpu.make_async_copy(home, home_all.at[mine], local_sem.at[count])]
    for which in range(count):
        extent = shards[which].shape[axes[which]]
        where = pl.ds(pl.multiple_of(group * extent, extent), extent)
        target = fulls[which].at[where] if axes[which] == 0 else fulls[which].at[:, where]
        local.append(pltpu.make_async_copy(shards[which], target, local_sem.at[which]))
    for copy in local:
        copy.start()
    for stage in range(len(bits)):
        for which, half in keys:
            for copy in stages[which, half, stage]:
                copy.wait_recv()
            if stage + 1 < len(bits):
                for copy in stages[which, half, stage + 1]:
                    copy.start()
    for copies in stages.values():
        for copy in copies:
            copy.wait_send()
    for copy in home_copies:
        copy.wait()
    for copy in local:
        copy.wait()


def gather_all(arrays, splits, axes, home):
    groups = lax.axis_size("dp")
    experts = lax.axis_size("expert")
    shapes = []
    for array, axis in zip(arrays, axes):
        shape = list(array.shape)
        shape[axis] *= groups
        shapes.append(jax.ShapeDtypeStruct(tuple(shape), array.dtype))
    shapes.append(jax.ShapeDtypeStruct((experts,) + home.shape, home.dtype))
    slots = sum(splits) * (groups - 1)
    return pl.pallas_call(
        partial(gather_kernel, groups, experts, splits, axes),
        out_shape=shapes,
        in_specs=[ANY] * (len(arrays) + 1),
        out_specs=[ANY] * (len(arrays) + 1),
        scratch_shapes=[
            pltpu.SemaphoreType.DMA((len(arrays) + 1,)),
            pltpu.SemaphoreType.DMA((slots,)),
            pltpu.SemaphoreType.DMA((slots,)),
            pltpu.SemaphoreType.DMA((experts - 1,)),
            pltpu.SemaphoreType.DMA((experts - 1,)),
        ],
        compiler_params=pltpu.CompilerParams(collective_id=0, has_side_effects=True),
        name="gather_all",
    )(*arrays, home)


def total_kernel(groups, experts, parts, total, held, send_sem, recv_sem):
    devices = groups * experts
    me = lax.axis_index("dp") * experts + lax.axis_index("expert")
    semaphore = pltpu.get_barrier_semaphore()

    def greet(step, carry):
        other = (me + step) % devices
        pl.semaphore_signal(
            semaphore,
            inc=1,
            device_id=(other // experts, other % experts),
            device_id_type=MESH,
        )
        return carry

    lax.fori_loop(1, devices, greet, 0)
    pl.semaphore_wait(semaphore, devices - 1)

    def copy_of(step):
        other = (me + step) % devices
        return pltpu.make_async_remote_copy(
            src_ref=parts.at[other],
            dst_ref=held.at[step],
            send_sem=send_sem.at[step],
            recv_sem=recv_sem.at[step],
            device_id=(other // experts, other % experts),
            device_id_type=MESH,
        )

    def send(step, carry):
        copy_of(step).start()
        return carry

    lax.fori_loop(1, devices, send, 0)
    held[0] = parts[me]

    def finish(step, carry):
        copy_of(step).wait()
        return carry

    lax.fori_loop(1, devices, finish, 0)
    total[...] = jnp.sum(held[...], axis=0)


def total_small(rows):
    groups = lax.axis_size("dp")
    experts = lax.axis_size("expert")
    devices = groups * experts
    kinds, width = rows.shape
    share = width // devices
    packed = rows.reshape(kinds, devices, share).transpose(1, 0, 2).reshape(devices, kinds * share)
    room = -(-kinds * share // 1024) * 1024
    packed = jnp.pad(packed, ((0, 0), (0, room - kinds * share))).reshape(
        devices, room // 128, 128
    )
    summed = pl.pallas_call(
        partial(total_kernel, groups, experts),
        out_shape=jax.ShapeDtypeStruct((room // 128, 128), f32),
        in_specs=[pl.BlockSpec(memory_space=pltpu.VMEM)],
        out_specs=pl.BlockSpec(memory_space=pltpu.VMEM),
        scratch_shapes=[
            pltpu.VMEM((devices, room // 128, 128), f32),
            pltpu.SemaphoreType.DMA((devices,)),
            pltpu.SemaphoreType.DMA((devices,)),
        ],
        compiler_params=pltpu.CompilerParams(collective_id=1, has_side_effects=True),
        name="total_small",
    )(packed)
    return summed.reshape(-1)[: kinds * share].reshape(kinds, share)


def turn(value, cosine, sine):
    return value * cosine + pltpu.roll(value, HEAD // 2, 1) * sine


def softmax_all(scores, seen):
    masked = jnp.where(seen, scores * (HEAD ** (-0.5)), -1e30)
    powers = jnp.exp(masked - jnp.max(masked, axis=-1, keepdims=True))
    return powers / jnp.sum(powers, axis=-1, keepdims=True)


def blocks_of(experts, rows, tokens, width):
    capacity, seq_len = rows // experts, tokens // experts
    return [
        (
            slice(seq * capacity, (seq + 1) * capacity),
            slice(seq * seq_len, (seq + 1) * seq_len),
            slice(head * HEAD, (head + 1) * HEAD),
        )
        for head in range(width // HEAD)
        for seq in range(experts)
    ]


def attend_kernel(
    experts,
    inputs_ref,
    small_ref,
    table_ref,
    place_ref,
    cos_far,
    sin_far,
    cos_near,
    sin_near,
    query_weight,
    key_weight,
    value_weight,
    normed_out,
    rows_out,
    query_out,
    key_out,
    value_out,
    mixture_out,
    query_hold,
):
    @pl.when(pl.program_id(0) == 0)
    def _():
        gain = small_ref[0:1].astype(f32)

        def norm_part(step, carry):
            at = pl.ds(pl.multiple_of(step * 32, 32), 32)
            value = inputs_ref[at].astype(f32)
            normed_out[at] = (value * norm_scale(value) * gain).astype(bf16)
            return carry

        lax.fori_loop(0, inputs_ref.shape[0] // 32, norm_part, 0)
        rows_out[...] = jnp.dot(
            table_ref[...], normed_out[...], preferred_element_type=f32
        ).astype(bf16)

    capacity = rows_out.shape[0] // experts
    seq_len = normed_out.shape[0] // experts
    width = key_out.shape[1]
    key = jnp.dot(normed_out[...], key_weight[...], preferred_element_type=f32)
    value_out[...] = jnp.dot(
        normed_out[...], value_weight[...], preferred_element_type=f32
    ).astype(bf16)
    query = jnp.dot(rows_out[...], query_weight[...], preferred_element_type=f32)
    for head in range(width // HEAD):
        cut = slice(head * HEAD, (head + 1) * HEAD)
        key_out[:, cut] = turn(key[:, cut], cos_near[...], sin_near[...]).astype(bf16)
        query_hold[:, cut] = turn(query[:, cut], cos_far[...], sin_far[...])
    query_out[...] = query_hold[...].astype(bf16)
    blocks = blocks_of(experts, rows_out.shape[0], normed_out.shape[0], width)
    contract = (((1,), (1,)), ((), ()))
    scores = jnp.concatenate(
        [
            lax.dot_general(
                query_hold[rows, cut].astype(bf16),
                key_out[keys, cut],
                contract,
                preferred_element_type=f32,
            )
            for rows, keys, cut in blocks
        ],
        axis=0,
    )
    spots = lax.broadcasted_iota(jnp.int32, (rows_out.shape[0], seq_len), 1)
    seen = spots <= place_ref[...]
    probs = softmax_all(scores, jnp.concatenate([seen] * (width // HEAD), axis=0))
    for number, (rows, keys, cut) in enumerate(blocks):
        query_hold[rows, cut] = jnp.dot(
            probs[number * capacity : (number + 1) * capacity].astype(bf16),
            value_out[keys, cut],
            preferred_element_type=f32,
        )
    mixture_out[...] = query_hold[...].astype(bf16)


def attend(experts, inputs, small, table, places, far, near, query_w, key_w, value_w):
    tokens, depth = inputs.shape
    rows = table.shape[0]
    heads_width = query_w.shape[1]
    tile = 256

    def full(shape):
        return pl.BlockSpec(shape, lambda step: (0, 0))

    def cut(height):
        return pl.BlockSpec((height, tile), lambda step: (0, step))

    def shaped(height, width):
        return jax.ShapeDtypeStruct((height, width), bf16)

    return pl.pallas_call(
        partial(attend_kernel, experts),
        grid=(heads_width // tile,),
        out_shape=[
            shaped(tokens, depth),
            shaped(rows, depth),
            shaped(rows, heads_width),
            shaped(tokens, heads_width),
            shaped(tokens, heads_width),
            shaped(rows, heads_width),
        ],
        in_specs=[
            full((tokens, depth)),
            full(small.shape),
            full(table.shape),
            full(places.shape),
            full((rows, HEAD)),
            full((rows, HEAD)),
            full((tokens, HEAD)),
            full((tokens, HEAD)),
            cut(depth),
            cut(depth),
            cut(depth),
        ],
        out_specs=[
            full((tokens, depth)),
            full((rows, depth)),
            cut(rows),
            cut(tokens),
            cut(tokens),
            cut(rows),
        ],
        scratch_shapes=[pltpu.VMEM((rows, tile), f32)],
        compiler_params=pltpu.CompilerParams(vmem_limit_bytes=48 * 1024 * 1024),
        cost_estimate=pl.CostEstimate(
            flops=2 * depth * heads_width * (2 * tokens + rows),
            bytes_accessed=6 * depth * heads_width + 8 * tokens * depth,
            transcendentals=rows * heads_width,
        ),
        name="attend",
    )(inputs, small, table, places, *far, *near, query_w, key_w, value_w)


def attend_back_kernel(
    experts,
    grad_ref,
    place_ref,
    cos_far,
    sin_far,
    weight_ref,
    query_ref,
    key_ref,
    value_ref,
    mixture_ref,
    query_out,
    key_out,
    value_out,
    output_out,
    grad_hold,
    query_hold,
    back_hold,
):
    contract = (((1,), (1,)), ((), ()))
    stack = (((0,), (0,)), ((), ()))
    rows_all = grad_ref.shape[0]
    capacity = rows_all // experts
    width = query_ref.shape[1]
    seq_len = key_ref.shape[0] // experts
    scale = HEAD ** (-0.5)
    grad_hold[...] = (
        lax.dot_general(grad_ref[...], weight_ref[...], contract, preferred_element_type=f32)
        .astype(bf16)
        .astype(f32)
    )
    output_out[...] = lax.dot_general(
        mixture_ref[...], grad_ref[...], stack, preferred_element_type=f32
    ).astype(bf16)
    query_hold[...] = query_ref[...].astype(f32)
    blocks = blocks_of(experts, rows_all, key_ref.shape[0], width)
    queries = [query_hold[rows, cut].astype(bf16) for rows, keys, cut in blocks]
    grads = [grad_hold[rows, cut].astype(bf16) for rows, keys, cut in blocks]
    scores = jnp.concatenate(
        [
            lax.dot_general(query, key_ref[keys, cut], contract, preferred_element_type=f32)
            for query, (rows, keys, cut) in zip(queries, blocks)
        ],
        axis=0,
    )
    grad_probs = jnp.concatenate(
        [
            lax.dot_general(grad, value_ref[keys, cut], contract, preferred_element_type=f32)
            for grad, (rows, keys, cut) in zip(grads, blocks)
        ],
        axis=0,
    )
    spots = lax.broadcasted_iota(jnp.int32, (rows_all, seq_len), 1)
    seen = spots <= place_ref[...]
    probs = softmax_all(scores, jnp.concatenate([seen] * (width // HEAD), axis=0))
    inner = jnp.sum(probs * grad_probs, axis=-1, keepdims=True)
    slopes = probs * (grad_probs - inner)
    for number, (rows, keys, cut) in enumerate(blocks):
        own = slice(number * capacity, (number + 1) * capacity)
        slope = slopes[own].astype(bf16)
        value_out[0, keys, cut] = lax.dot_general(
            probs[own].astype(bf16), grads[number], stack, preferred_element_type=f32
        ).astype(bf16)
        key_out[0, keys, cut] = (
            lax.dot_general(slope, queries[number], stack, preferred_element_type=f32) * scale
        ).astype(bf16)
        back_hold[rows, cut] = (
            jnp.dot(slope, key_ref[keys, cut], preferred_element_type=f32) * scale
        )
    for head in range(width // HEAD):
        cut = slice(head * HEAD, (head + 1) * HEAD)
        query_out[:, cut] = turn(back_hold[:, cut], cos_far[...], -sin_far[...]).astype(bf16)


def attend_back(experts, grad_rows, places, far, output_w, query, key, value, mixture):
    rows, depth = grad_rows.shape
    tokens, heads_width = key.shape
    tile = 256
    own_width = heads_width // experts
    steps = own_width // tile

    def full(shape):
        return pl.BlockSpec(shape, lambda step: (0, 0))

    def cut(height):
        return pl.BlockSpec((height, tile), lambda step: (0, step))

    by_heads = pl.BlockSpec((1, tokens, tile), lambda step: (step // steps, 0, step % steps))
    return pl.pallas_call(
        partial(attend_back_kernel, experts),
        grid=(heads_width // tile,),
        out_shape=[
            jax.ShapeDtypeStruct((rows, heads_width), bf16),
            jax.ShapeDtypeStruct((experts, tokens, own_width), bf16),
            jax.ShapeDtypeStruct((experts, tokens, own_width), bf16),
            jax.ShapeDtypeStruct((heads_width, depth), bf16),
        ],
        in_specs=[
            full((rows, depth)),
            full(places.shape),
            full((rows, HEAD)),
            full((rows, HEAD)),
            pl.BlockSpec((tile, depth), lambda step: (step, 0)),
            cut(rows),
            cut(tokens),
            cut(tokens),
            cut(rows),
        ],
        out_specs=[
            cut(rows),
            by_heads,
            by_heads,
            pl.BlockSpec((tile, depth), lambda step: (step, 0)),
        ],
        scratch_shapes=[pltpu.VMEM((rows, tile), f32)] * 3,
        compiler_params=pltpu.CompilerParams(vmem_limit_bytes=48 * 1024 * 1024),
        cost_estimate=pl.CostEstimate(
            flops=4 * rows * depth * heads_width,
            bytes_accessed=4 * depth * heads_width + 8 * tokens * heads_width,
            transcendentals=rows * heads_width,
        ),
        name="attend_back",
    )(grad_rows, places, *far, output_w, query, key, value, mixture)


def halves(ref, block, rows, half):
    size = rows // 2
    return ref.at[pl.ds(pl.multiple_of(block * rows + half * size, size), size)]


def whole(ref, block, rows):
    return ref.at[pl.ds(pl.multiple_of(block * rows, rows), rows)]


def ffn_kernel(
    rows,
    own_ref,
    slope_ref,
    pick_ref,
    router_ref,
    gate_ref,
    up_ref,
    down_ref,
    rows_out,
    hidden_out,
    grad_gate_out,
    grad_up_out,
    out_out,
    grad_out,
    held,
    pulled,
    hidden,
    scaled,
    grad_gate,
    grad_up,
    made,
    grads,
    near,
    far,
    dense,
    dense_far,
    dense_hold,
    far_send,
    far_recv,
    near_send,
    near_recv,
    sum_send,
    sum_recv,
    dense_send,
    dense_recv,
    load_sem,
    save_sem,
):
    group = lax.axis_index("dp")
    mine = lax.axis_index("expert")
    depth = held.shape[1]
    width = hidden.shape[1]
    pair = 2 * rows
    bits = (1, 2, 4)
    peers = {mask: (flips(group, mask, bits), mine) for mask in range(1, 8)}
    barrier([peers[mask] for mask in range(1, 8)])

    def remote(source, target, send, recv, mask):
        return pltpu.make_async_remote_copy(
            src_ref=source,
            dst_ref=target,
            send_sem=send,
            recv_sem=recv,
            device_id=peers[mask],
            device_id_type=MESH,
        )

    def own_half(half):
        size = rows // 2
        return own_ref.at[pl.ds(half * size, size)]

    sends = {}
    for slot, (mask, half) in enumerate(((2, 0), (4, 1), (2, 1), (4, 0))):
        sends[mask, half] = remote(
            own_half(half),
            halves(held, mask, rows, half),
            far_send.at[slot],
            far_recv.at[slot],
            mask,
        )
    sends[6, 0] = remote(
        halves(held, 2, rows, 0), halves(held, 6, rows, 0), far_send.at[4], far_recv.at[4], 4
    )
    sends[6, 1] = remote(
        halves(held, 4, rows, 1), halves(held, 6, rows, 1), far_send.at[5], far_recv.at[5], 2
    )
    across = {}
    for chip in range(4):
        across[chip] = remote(
            own_ref if chip == 0 else whole(held, 2 * chip, rows),
            whole(held, 2 * chip + 1, rows),
            near_send.at[chip],
            near_recv.at[chip],
            1,
        )
    sends[2, 0].start()
    sends[4, 1].start()
    across[0].start()
    sends[2, 1].start()
    sends[4, 0].start()
    seat = pltpu.make_async_copy(own_ref, whole(held, 0, rows), load_sem.at[2])
    seat.start()

    def pull(chip, slot, which):
        block = group_of(2 * chip + which)
        return pltpu.make_async_copy(
            slope_ref.at[block], whole(pulled, 2 * slot + which, rows), load_sem.at[which]
        )

    def group_of(index):
        result = group
        for bit in bits:
            on = (index // bit) % 2
            turned = bit * (1 - 2 * ((group // bit) % 2))
            result = result + on * turned
        return result

    def saves(chip):
        copies = []
        for which in range(2):
            block = group_of(2 * chip + which)
            for number, (source, target) in enumerate(
                (
                    (whole(held, 2 * chip + which, rows), rows_out.at[block]),
                    (whole(scaled, which, rows), hidden_out.at[block]),
                    (whole(grad_gate, which, rows), grad_gate_out.at[block]),
                    (whole(grad_up, which, rows), grad_up_out.at[block]),
                    (whole(made, which, rows), out_out.at[block]),
                )
            ):
                copies.append(
                    pltpu.make_async_copy(source, target, save_sem.at[5 * which + number])
                )
        return copies

    def across_sum(chip):
        return remote(
            whole(grads, 2 * chip + 1, rows),
            whole(near, chip, rows),
            near_send.at[4 + chip],
            near_recv.at[4 + chip],
            1,
        )

    hops = {}
    for slot, (key, block, half, mask) in enumerate(
        (
            ("x2", 2, 0, 2),
            ("x6", 6, 0, 2),
            ("y4", 4, 1, 4),
            ("y6", 6, 1, 4),
            ("then_y", 4, 0, 4),
            ("then_x", 2, 1, 2),
        )
    ):
        size = rows // 2
        hops[key] = remote(
            halves(grads, block, rows, half),
            far.at[pl.ds(slot * size, size)],
            sum_send.at[slot],
            sum_recv.at[slot],
            mask,
        )
    far_slots = {"x2": 0, "x6": 1, "y4": 2, "y6": 3, "then_y": 4, "then_x": 5}

    def dense_hop(mask):
        return remote(
            dense.at[mask],
            dense_far.at[mask],
            dense_send.at[mask],
            dense_recv.at[mask],
            mask,
        )

    def join(chip):
        across_sum(chip).wait_recv()
        block = 2 * chip

        def add(step, carry):
            at = pl.ds(pl.multiple_of(block * rows + step * 48, 16), 48)
            other = pl.ds(pl.multiple_of(chip * rows + step * 48, 16), 48)
            grads[at] = (grads[at].astype(f32) + near[other].astype(f32)).astype(bf16)
            return carry

        lax.fori_loop(0, rows // 48, add, 0)

    def add_far(block, half, key):
        size = rows // 2
        hops[key].wait_recv()

        def add(step, carry):
            at = pl.ds(pl.multiple_of(block * rows + half * size + step * 48, 16), 48)
            other = pl.ds(far_slots[key] * size + pl.multiple_of(step * 48, 16), 48)
            grads[at] = (grads[at].astype(f32) + far[other].astype(f32)).astype(bf16)
            return carry

        lax.fori_loop(0, size // 48, add, 0)

    for which in range(2):
        pull(0, 0, which).start()
    seat.wait()

    def step(chip, carry):
        @pl.when(chip == 0)
        def _():
            across[0].wait_recv()

        @pl.when(chip == 1)
        def _():
            sends[2, 0].wait_recv()
            sends[6, 0].start()
            sends[4, 1].wait_recv()
            sends[6, 1].start()
            sends[2, 1].wait_recv()
            across[1].start()
            sends[4, 0].wait_recv()
            across[2].start()
            across[1].wait_recv()

        @pl.when(chip == 2)
        def _():
            sends[6, 0].wait_recv()
            sends[6, 1].wait_recv()
            across[3].start()
            across[2].wait_recv()

        @pl.when(chip == 3)
        def _():
            across[3].wait_recv()

        slot = chip % 2
        for which in range(2):
            pull(chip, slot, which).wait()

        @pl.when(chip < 3)
        def _():
            for which in range(2):
                pull(chip + 1, 1 - slot, which).start()

        @pl.when(chip > 0)
        def _():
            for copy in saves(chip - 1):
                copy.wait()

        base = pl.multiple_of(chip * pair, pair)
        at = pl.ds(base, pair)
        logits = lax.dot_general(
            held[at], router_ref[...], (((1,), (1,)), ((), ())), preferred_element_type=f32
        )
        apart = []
        for which in range(2):
            block = group_of(2 * chip + which)
            picks = pick_ref[pl.ds(pl.multiple_of(block * rows, rows), rows)]
            apart.append(
                jnp.sum(
                    logits[which * rows : (which + 1) * rows] * picks, axis=-1, keepdims=True
                )
            )
        weight = 1.0 / (1.0 + jnp.exp(jnp.concatenate(apart, axis=0)))
        loads = pl.ds(pl.multiple_of(slot * pair, pair), pair)
        tile = 256
        partial_dense = jnp.zeros((pair, 128), f32)

        def units(number, total):
            cut = pl.ds(pl.multiple_of(number * tile, tile), tile)
            contract = (((1,), (1,)), ((), ()))
            gate = lax.dot_general(
                held[at], gate_ref[cut], contract, preferred_element_type=f32
            )
            up = lax.dot_general(held[at], up_ref[cut], contract, preferred_element_type=f32)
            sigmoid = 1.0 / (1.0 + jnp.exp(-gate))
            active = gate * sigmoid
            value = (active * up).astype(bf16)
            wide = value.astype(f32)
            plain = pulled[loads, cut]
            hidden[:, cut] = value
            scaled[:, cut] = (weight * wide).astype(bf16)
            inner = weight * plain
            grad_gate[:, cut] = (inner * up * (sigmoid * (1.0 + gate * (1.0 - sigmoid)))).astype(
                bf16
            )
            grad_up[:, cut] = (inner * active).astype(bf16)
            both = wide * plain
            return total + both[:, :128] + both[:, 128:]

        partial_dense = lax.fori_loop(0, width // tile, units, partial_dense)
        ones = jnp.ones((8, 128), f32)
        for which in range(2):
            dense[2 * chip + which] = lax.dot_general(
                ones,
                partial_dense[which * rows : (which + 1) * rows],
                (((1,), (1,)), ((), ())),
                precision=highest,
                preferred_element_type=f32,
            )

        @pl.when(chip == 1)
        def _():
            join(0)

        @pl.when(chip == 2)
        def _():
            join(1)
            hops["x2"].start()

        @pl.when(chip == 3)
        def _():
            join(2)
            hops["y4"].start()

        def columns(number, carry):
            cut = pl.ds(pl.multiple_of(number * tile, tile), tile)
            made[:, cut] = jnp.dot(
                hidden[...], down_ref[:, cut], preferred_element_type=f32
            ).astype(bf16)
            grads[at, cut] = (
                jnp.dot(grad_gate[...], gate_ref[:, cut], preferred_element_type=f32)
                + jnp.dot(grad_up[...], up_ref[:, cut], preferred_element_type=f32)
            ).astype(bf16)
            return carry

        lax.fori_loop(0, depth // tile, columns, 0)
        across_sum(chip).start()
        for copy in saves(chip):
            copy.start()
        return carry

    lax.fori_loop(0, 4, step, 0)
    join(3)
    hops["x6"].start()
    hops["y6"].start()
    for mask in range(1, 8):
        dense_hop(mask).start()
    add_far(0, 0, "x2")
    add_far(0, 1, "y4")
    add_far(4, 0, "x6")
    hops["then_y"].start()
    add_far(2, 1, "y6")
    hops["then_x"].start()
    total = dense[0]
    for mask in range(1, 8):
        dense_hop(mask).wait_recv()
        total = total + dense_far[mask]
    for copy in saves(3):
        copy.wait()
    pick = (lax.broadcasted_iota(jnp.int32, (8, 128), 0) == 0).astype(f32)
    column = lax.dot_general(
        total, pick, (((0,), (0,)), ((), ())), precision=highest, preferred_element_type=f32
    )
    upper = column.astype(bf16)
    lower = (column - upper.astype(f32)).astype(bf16)
    lane = lax.broadcasted_iota(jnp.int32, column.shape, 1)
    dense_hold[...] = jnp.where(lane == 0, upper, jnp.where(lane == 1, lower, 0.0)).astype(bf16)
    add_far(0, 0, "then_y")
    add_far(0, 1, "then_x")
    tail = pltpu.make_async_copy(dense_hold, grad_out.at[:, pl.ds(depth, 128)], load_sem.at[0])
    tail.start()
    last = pltpu.make_async_copy(
        whole(grads, 0, rows), grad_out.at[:, pl.ds(0, depth)], load_sem.at[2]
    )
    last.start()
    for copy in list(sends.values()) + list(across.values()) + list(hops.values()):
        copy.wait_send()
    for chip in range(4):
        across_sum(chip).wait_send()
    for mask in range(1, 8):
        dense_hop(mask).wait_send()
    last.wait()
    tail.wait()


def ffn_call(own, slopes, picks, router, gate, up, down):
    rows, depth = own.shape
    width = gate.shape[0]
    vmem = pl.BlockSpec(memory_space=pltpu.VMEM)
    return pl.pallas_call(
        partial(ffn_kernel, rows),
        out_shape=[
            jax.ShapeDtypeStruct((8, rows, depth), bf16),
            jax.ShapeDtypeStruct((8, rows, width), bf16),
            jax.ShapeDtypeStruct((8, rows, width), bf16),
            jax.ShapeDtypeStruct((8, rows, width), bf16),
            jax.ShapeDtypeStruct((8, rows, depth), bf16),
            jax.ShapeDtypeStruct((rows, depth + 128), bf16),
        ],
        in_specs=[ANY, ANY, vmem, vmem, vmem, vmem, vmem],
        out_specs=[ANY] * 6,
        scratch_shapes=[
            pltpu.VMEM((8 * rows, depth), bf16),
            pltpu.VMEM((4 * rows, width), f32),
            pltpu.VMEM((2 * rows, width), bf16),
            pltpu.VMEM((2 * rows, width), bf16),
            pltpu.VMEM((2 * rows, width), bf16),
            pltpu.VMEM((2 * rows, width), bf16),
            pltpu.VMEM((2 * rows, depth), bf16),
            pltpu.VMEM((8 * rows, depth), bf16),
            pltpu.VMEM((4 * rows, depth), bf16),
            pltpu.VMEM((3 * rows, depth), bf16),
            pltpu.VMEM((8, 8, rows), f32),
            pltpu.VMEM((8, 8, rows), f32),
            pltpu.VMEM((rows, 128), bf16),
            pltpu.SemaphoreType.DMA((6,)),
            pltpu.SemaphoreType.DMA((6,)),
            pltpu.SemaphoreType.DMA((8,)),
            pltpu.SemaphoreType.DMA((8,)),
            pltpu.SemaphoreType.DMA((6,)),
            pltpu.SemaphoreType.DMA((6,)),
            pltpu.SemaphoreType.DMA((8,)),
            pltpu.SemaphoreType.DMA((8,)),
            pltpu.SemaphoreType.DMA((3,)),
            pltpu.SemaphoreType.DMA((10,)),
        ],
        compiler_params=pltpu.CompilerParams(
            collective_id=2, has_side_effects=True, vmem_limit_bytes=61 * 1024 * 1024
        ),
        name="ffn",
    )(own, slopes, picks, router, gate, up, down)


class ChipSums:
    def __init__(self, remote, blocks, near, far, sems, rows):
        self.blocks, self.near, self.far, self.rows = blocks, near, far, rows
        self.remote = remote
        self.near_send, self.near_recv, self.sum_send, self.sum_recv = sems
        self.hops = {}
        size = rows // 2
        for slot, (key, block, half, mask) in enumerate(
            (
                ("x2", 2, 0, 2),
                ("x6", 6, 0, 2),
                ("y4", 4, 1, 4),
                ("y6", 6, 1, 4),
                ("then_y", 4, 0, 4),
                ("then_x", 2, 1, 2),
            )
        ):
            self.hops[key] = (
                remote(
                    halves(blocks, block, rows, half),
                    far.at[pl.ds(slot * size, size)],
                    self.sum_send.at[slot],
                    self.sum_recv.at[slot],
                    mask,
                ),
                slot * size,
            )

    def across(self, chip):
        return self.remote(
            whole(self.blocks, 2 * chip + 1, self.rows),
            whole(self.near, chip, self.rows),
            self.near_send.at[chip],
            self.near_recv.at[chip],
            1,
        )

    def add(self, start, other, other_start, count):
        piece = 48 if count % 48 == 0 else 32

        def one(step, carry):
            at = pl.ds(pl.multiple_of(start + step * piece, 16), piece)
            have = pl.ds(pl.multiple_of(other_start + step * piece, 16), piece)
            self.blocks[at] = (self.blocks[at].astype(f32) + other[have].astype(f32)).astype(bf16)
            return carry

        lax.fori_loop(0, count // piece, one, 0)

    def join(self, chip):
        self.across(chip).wait_recv()
        self.add(2 * chip * self.rows, self.near, chip * self.rows, self.rows)

    def begin(self, key):
        self.hops[key][0].start()

    def settle(self, chip):
        self.join(chip)

        @pl.when(chip == 1)
        def _():
            self.begin("x2")

        @pl.when(chip == 2)
        def _():
            self.begin("y4")

        @pl.when(chip == 3)
        def _():
            self.begin("x6")
            self.begin("y6")

    def add_far(self, block, half, key):
        size = self.rows // 2
        copy, place = self.hops[key]
        copy.wait_recv()
        self.add(block * self.rows + half * size, self.far, place, size)

    def cross(self):
        self.add_far(4, 0, "x6")
        self.begin("then_y")
        self.add_far(2, 1, "y6")
        self.begin("then_x")
        self.add_far(0, 0, "x2")
        self.add_far(0, 1, "y4")

    def close(self):
        self.add_far(0, 0, "then_y")
        self.add_far(0, 1, "then_x")

    def drain(self):
        for copy, place in self.hops.values():
            copy.wait_send()
        for chip in range(4):
            self.across(chip).wait_send()


def turned_pair(index, other, bits):
    result = index
    for bit in bits:
        on = (other // bit) % 2
        result = result + on * bit * (1 - 2 * ((index // bit) % 2))
    return result


def back_kernel(
    grad_ref,
    rows_ref,
    place_ref,
    cos_far,
    sin_far,
    cos_near,
    sin_near,
    weight_ref,
    query_ref,
    key_ref,
    value_ref,
    mixture_ref,
    query_out,
    key_out,
    value_out,
    output_sum,
    query_sum,
    grad_hold,
    query_hold,
    back_hold,
    weights,
    key_part,
    value_part,
    key_got,
    value_got,
    key_pass,
    value_pass,
    total_hold,
    output_blocks,
    output_near,
    output_far,
    query_blocks,
    query_near,
    query_far,
    output_near_send,
    output_near_recv,
    output_sum_send,
    output_sum_recv,
    query_near_send,
    query_near_recv,
    query_sum_send,
    query_sum_recv,
    got_send,
    got_recv,
    pass_send,
    pass_recv,
    load_sem,
):
    group = lax.axis_index("dp")
    mine = lax.axis_index("expert")
    experts = 4
    side = mine // 2
    edge = ((mine + 1) % experts) // 2 == 0
    bits = (1, 2, 4)
    peers = {mask: (flips(group, mask, bits), mine) for mask in (1, 2, 4)}
    barrier(
        [peers[mask] for mask in (1, 2, 4)]
        + [(group, (mine + step) % experts) for step in range(1, experts)]
    )

    def remote(source, target, send, recv, mask):
        return pltpu.make_async_remote_copy(
            src_ref=source,
            dst_ref=target,
            send_sem=send,
            recv_sem=recv,
            device_id=peers[mask],
            device_id_type=MESH,
        )

    rows_all, depth = grad_ref.shape
    tokens = key_ref.shape[0]
    capacity = rows_all // experts
    seq_len = tokens // experts
    tile = 256
    contract = (((1,), (1,)), ((), ()))
    stack = (((0,), (0,)), ((), ()))
    scale = HEAD ** (-0.5)
    outputs = ChipSums(
        remote,
        output_blocks,
        output_near,
        output_far,
        (output_near_send, output_near_recv, output_sum_send, output_sum_recv),
        tile,
    )
    queries_sum = ChipSums(
        remote,
        query_blocks,
        query_near,
        query_far,
        (query_near_send, query_near_recv, query_sum_send, query_sum_recv),
        tile,
    )

    def owner_of(number):
        return jnp.where(
            number == 0,
            2 - side,
            jnp.where(number == 1, 3 - 3 * side, jnp.where(number == 2, 1 + 4 * side - mine, mine)),
        )

    def chip_of(owner):
        return turned_pair(owner, group // 2, (1, 2))

    def load(step):
        at = pl.multiple_of((2 * owner_of(step // 2) + step % 2) * tile, tile)
        return pltpu.make_async_copy(
            weight_ref.at[pl.ds(at, tile)], weights.at[step % 2], load_sem.at[step % 2]
        )

    def part_at(owner):
        return pl.ds(pl.multiple_of(owner * tokens, tokens), tokens)

    def give(owner):
        return [
            pltpu.make_async_remote_copy(
                src_ref=part.at[part_at(owner)],
                dst_ref=got.at[part_at(mine)],
                send_sem=got_send.at[owner, number],
                recv_sem=got_recv.at[mine, number],
                device_id=(group, owner),
                device_id_type=MESH,
            )
            for number, (part, got) in enumerate(
                ((key_part, key_got), (value_part, value_got))
            )
        ]

    def got_from(source):
        return [
            pltpu.make_async_remote_copy(
                src_ref=part.at[part_at(source)],
                dst_ref=got.at[part_at(source)],
                send_sem=got_send.at[source, number],
                recv_sem=got_recv.at[source, number],
                device_id=(group, source),
                device_id_type=MESH,
            )
            for number, (part, got) in enumerate(
                ((key_part, key_got), (value_part, value_got))
            )
        ]

    def hand_on(target):
        return [
            pltpu.make_async_remote_copy(
                src_ref=part.at[part_at(2 - side)],
                dst_ref=pile,
                send_sem=pass_send.at[number],
                recv_sem=pass_recv.at[number],
                device_id=(group, target),
                device_id_type=MESH,
            )
            for number, (part, pile) in enumerate(
                ((key_part, key_pass), (value_part, value_pass))
            )
        ]

    load(0).start()
    block_slices = blocks_of(experts, rows_all, tokens, tile)
    spots = lax.broadcasted_iota(jnp.int32, (rows_all, seq_len), 1)

    def one(step, carry):
        owner = owner_of(step // 2)
        parity = step % 2
        number = 2 * owner + parity
        chip = chip_of(owner)
        load(step).wait()

        @pl.when(step < 7)
        def _():
            load(step + 1).start()

        columns = pl.ds(pl.multiple_of(number * tile, tile), tile)
        block = turned_pair(number, group, bits)
        block_at = pl.ds(pl.multiple_of(block * tile, tile), tile)
        grad_hold[...] = (
            lax.dot_general(
                grad_ref[...], weights[parity], contract, preferred_element_type=f32
            )
            .astype(bf16)
            .astype(f32)
        )
        output_blocks[block_at] = lax.dot_general(
            mixture_ref[:, columns], grad_ref[...], stack, preferred_element_type=f32
        ).astype(bf16)

        @pl.when((parity == 1) & (step > 1))
        def _():
            outputs.settle(chip_of(owner_of(step // 2 - 1)))

        query_hold[...] = query_ref[:, columns].astype(f32)
        keys_tile = key_ref[:, columns]
        values_tile = value_ref[:, columns]
        queries = [query_hold[rows, cut].astype(bf16) for rows, keys, cut in block_slices]
        grads = [grad_hold[rows, cut].astype(bf16) for rows, keys, cut in block_slices]
        scores = jnp.concatenate(
            [
                lax.dot_general(query, keys_tile[keys, cut], contract, preferred_element_type=f32)
                for query, (rows, keys, cut) in zip(queries, block_slices)
            ],
            axis=0,
        )
        grad_probs = jnp.concatenate(
            [
                lax.dot_general(grad, values_tile[keys, cut], contract, preferred_element_type=f32)
                for grad, (rows, keys, cut) in zip(grads, block_slices)
            ],
            axis=0,
        )
        seen = spots <= place_ref[...]
        probs = softmax_all(scores, jnp.concatenate([seen] * (tile // HEAD), axis=0))
        inner = jnp.sum(probs * grad_probs, axis=-1, keepdims=True)
        slopes = probs * (grad_probs - inner)
        for count, (rows, keys, cut) in enumerate(block_slices):
            own = slice(count * capacity, (count + 1) * capacity)
            slope = slopes[own].astype(bf16)
            token_at = pl.ds(
                pl.multiple_of(owner * tokens + keys.start, seq_len), seq_len
            )
            lanes = pl.ds(pl.multiple_of(parity * tile + cut.start, HEAD), HEAD)
            value_part[token_at, lanes] = lax.dot_general(
                probs[own].astype(bf16), grads[count], stack, preferred_element_type=f32
            ).astype(bf16)
            key_part[token_at, lanes] = (
                lax.dot_general(slope, queries[count], stack, preferred_element_type=f32) * scale
            ).astype(bf16)
            back_hold[rows, cut] = (
                jnp.dot(slope, keys_tile[keys, cut], preferred_element_type=f32) * scale
            )
        for head in range(tile // HEAD):
            cut = slice(head * HEAD, (head + 1) * HEAD)
            lanes = pl.ds(pl.multiple_of(number * tile + head * HEAD, HEAD), HEAD)
            query_out[:, lanes] = turn(back_hold[:, cut], cos_far[...], -sin_far[...]).astype(bf16)

        @pl.when(parity == 1)
        def _():
            outputs.across(chip).start()

            @pl.when(step == 1)
            def _():
                @pl.when(edge)
                def _():
                    for copy in hand_on(1 + side):
                        copy.start()

            @pl.when((step == 3) | (step == 5))
            def _():
                for copy in give(owner):
                    copy.start()

        return carry

    lax.fori_loop(0, 8, one, 0)

    def project(block, carry):
        number = turned_pair(block, group, bits)
        columns = pl.ds(pl.multiple_of(number * tile, tile), tile)
        block_at = pl.ds(pl.multiple_of(block * tile, tile), tile)
        query_blocks[block_at] = lax.dot_general(
            rows_ref[:, columns], query_out[...], stack, preferred_element_type=f32
        ).astype(bf16)

        @pl.when(block % 2 == 1)
        def _():
            queries_sum.across(block // 2).start()

        return carry

    lax.fori_loop(0, 8, project, 0)
    outputs.settle(chip_of(mine))
    piece = 32

    @pl.when(jnp.logical_not(edge))
    def _():
        for (part, pile), copy in zip(
            ((key_part, key_pass), (value_part, value_pass)), hand_on(1 + side)
        ):
            copy.wait_recv()

            def add(step, carry):
                at = pl.ds(pl.multiple_of((2 - side) * tokens + step * piece, piece), piece)
                other = pl.ds(pl.multiple_of(step * piece, piece), piece)
                part[at] = (part[at].astype(f32) + pile[other].astype(f32)).astype(bf16)
                return carry

            lax.fori_loop(0, tokens // piece, add, 0)
        for copy in give(2 - side):
            copy.start()

    for chip in range(4):
        queries_sum.settle(chip)
    outputs.cross()
    outputs.close()
    result = pltpu.make_async_copy(whole(output_blocks, 0, tile), output_sum, load_sem.at[0])
    result.start()
    queries_sum.cross()
    queries_sum.close()
    second = pltpu.make_async_copy(whole(query_blocks, 0, tile), query_sum, load_sem.at[1])
    second.start()

    def expected(source):
        far_end = (mine + 2) % experts
        middle = ((mine + 1) % experts) // 2 == 1
        return jnp.logical_not(middle & (source == far_end))

    def gather(number, part, got):
        def first(step, carry):
            at = pl.ds(pl.multiple_of(mine * tokens + step * piece, piece), piece)
            where = pl.ds(pl.multiple_of(step * piece, piece), piece)
            total_hold[where] = part[at].astype(f32)
            return carry

        lax.fori_loop(0, tokens // piece, first, 0)
        for hop in range(1, experts):
            source = (mine + hop) % experts

            @pl.when(expected(source))
            def _():
                got_from(source)[number].wait_recv()

                def add(step, carry):
                    at = pl.ds(pl.multiple_of(source * tokens + step * piece, piece), piece)
                    where = pl.ds(pl.multiple_of(step * piece, piece), piece)
                    total_hold[where] = total_hold[where] + got[at].astype(f32)
                    return carry

                lax.fori_loop(0, tokens // piece, add, 0)

    gather(1, value_part, value_got)
    value_out[...] = total_hold[...].astype(bf16)
    gather(0, key_part, key_got)
    for head in range(key_out.shape[1] // HEAD):
        cut = slice(head * HEAD, (head + 1) * HEAD)
        key_out[:, cut] = turn(total_hold[:, cut], cos_near[...], -sin_near[...]).astype(bf16)

    @pl.when(edge)
    def _():
        for copy in hand_on(1 + side):
            copy.wait_send()

    @pl.when(jnp.logical_not(edge))
    def _():
        for copy in give(2 - side):
            copy.wait_send()

    for number in (1, 2):
        for copy in give(owner_of(number)):
            copy.wait_send()
    outputs.drain()
    queries_sum.drain()
    result.wait()
    second.wait()


def back_call(grad_rows, rows_flat, places, far, near, output_w, query, key, value, mixture):
    rows, depth = grad_rows.shape
    tokens, heads_width = key.shape
    own = heads_width // 4
    tile = 256
    vmem = pl.BlockSpec(memory_space=pltpu.VMEM)

    def dma(*shape):
        return pltpu.SemaphoreType.DMA(shape)

    def blocks(count):
        return pltpu.VMEM((count * tile, depth), bf16)

    return pl.pallas_call(
        back_kernel,
        out_shape=[
            jax.ShapeDtypeStruct((rows, heads_width), bf16),
            jax.ShapeDtypeStruct((tokens, own), bf16),
            jax.ShapeDtypeStruct((tokens, own), bf16),
            jax.ShapeDtypeStruct((tile, depth), bf16),
            jax.ShapeDtypeStruct((tile, depth), bf16),
        ],
        in_specs=[vmem] * 7 + [ANY] + [vmem] * 4,
        out_specs=[vmem] * 3 + [ANY] * 2,
        scratch_shapes=[
            pltpu.VMEM((rows, tile), f32),
            pltpu.VMEM((rows, tile), f32),
            pltpu.VMEM((rows, tile), f32),
            pltpu.VMEM((2, tile, depth), bf16),
            pltpu.VMEM((4 * tokens, own), bf16),
            pltpu.VMEM((4 * tokens, own), bf16),
            pltpu.VMEM((4 * tokens, own), bf16),
            pltpu.VMEM((4 * tokens, own), bf16),
            pltpu.VMEM((tokens, own), bf16),
            pltpu.VMEM((tokens, own), bf16),
            pltpu.VMEM((tokens, own), f32),
            blocks(8),
            blocks(4),
            blocks(3),
            blocks(8),
            blocks(4),
            blocks(3),
            dma(4),
            dma(4),
            dma(6),
            dma(6),
            dma(4),
            dma(4),
            dma(6),
            dma(6),
            dma(4, 2),
            dma(4, 2),
            dma(2),
            dma(2),
            dma(2),
        ],
        compiler_params=pltpu.CompilerParams(
            collective_id=3, has_side_effects=True, vmem_limit_bytes=61 * 1024 * 1024
        ),
        cost_estimate=pl.CostEstimate(
            flops=60_000_000_000, bytes_accessed=200_000_000, transcendentals=0
        ),
        name="attend_back_sums",
    )(grad_rows, rows_flat, places, *far, *near, output_w, query, key, value, mixture)


def start_kernel(
    home,
    attn_gain,
    moe_gain,
    attn_router,
    moe_router,
    attn_choice,
    moe_choice,
    lengths,
    cos_home,
    sin_home,
    given,
    value_shard,
    key_shard,
    query_shard,
    output_shard,
    small_full,
    told_full,
    table_out,
    place_out,
    cos_far,
    sin_far,
    attn_table,
    moe_table,
    normed_out,
    rows_out,
    query_out,
    key_out,
    value_out,
    mixture_out,
    branch_out,
    value_own,
    key_own,
    query_full,
    output_full,
    given_out,
    inputs,
    small_own,
    told_own,
    small_hold,
    normed,
    rows_hold,
    query_hold,
    query_low,
    keys,
    values,
    chances,
    mixture,
    branch,
    given_hold,
    value_stage,
    key_stage,
    query_stage,
    output_stage,
    value_buf,
    key_buf,
    query_buf,
    output_buf,
    load_sem,
    far_send,
    far_recv,
    near_send,
    near_recv,
    home_send,
    home_recv,
    small_send,
    small_recv,
    told_send,
    told_recv,
    heads_send,
    heads_recv,
    given_send,
    given_recv,
    save_sem,
):
    group = lax.axis_index("dp")
    mine = lax.axis_index("expert")
    experts = 4
    bits = (1, 2, 4)
    peers = {mask: (flips(group, mask, bits), mine) for mask in range(1, 8)}
    others = [(mine + hop) % experts for hop in range(1, experts)]
    seq_len, depth = home.shape
    expert_rows = rows_out.shape[0]
    capacity = expert_rows // experts
    tokens = experts * seq_len
    extent = key_shard.shape[0]
    half_extent = extent // 2
    own_width = value_buf.shape[1]
    heads_width = key_buf.shape[1]
    tile = 256
    shards = (value_shard, key_shard, query_shard, output_shard)
    stages = (value_stage, key_stage, query_stage, output_stage)
    buffers = (value_buf, key_buf, query_buf, output_buf)
    loads = []
    for which in range(4):
        source = shards[which]
        if which == 0:
            source = source.at[:, pl.ds(pl.multiple_of(mine * own_width, own_width), own_width)]
        loads.append(pltpu.make_async_copy(source, stages[which], load_sem.at[which]))
    seat = pltpu.make_async_copy(home, inputs.at[mine], load_sem.at[4])
    for copy in loads:
        copy.start()
    seat.start()

    small_hold[...] = jnp.zeros_like(small_hold)
    small_hold[0:1] = attn_gain[...]
    small_hold[1:2] = moe_gain[...]
    small_hold[2 : 2 + experts] = attn_router[...]
    small_hold[2 + experts : 2 + 2 * experts] = moe_router[...]
    small_own[...] = small_hold[...].astype(bf16)
    lane = lax.broadcasted_iota(jnp.int32, (experts, seq_len), 1)
    live = lane < lengths[...]
    told_own[0:experts] = jnp.where(live, moe_choice[0], -1).astype(f32)
    told_own[experts : 2 * experts] = jnp.where(live, moe_choice[1], -1).astype(f32)
    barrier([peers[mask] for mask in range(1, 8)] + [(group, other) for other in others])

    def remote(source, target, send, recv, device):
        return pltpu.make_async_remote_copy(
            src_ref=source,
            dst_ref=target,
            send_sem=send,
            recv_sem=recv,
            device_id=device,
            device_id_type=MESH,
        )

    small_at = pl.ds(pl.multiple_of(group * extent, extent), extent)
    told_at = pl.ds(pl.multiple_of(group * 2 * experts, 2 * experts), 2 * experts)
    smalls = []
    for mask in range(1, 8):
        smalls.append(
            remote(
                small_own,
                small_full.at[:, small_at],
                small_send.at[mask],
                small_recv.at[mask],
                peers[mask],
            )
        )
        smalls.append(
            remote(
                told_own,
                told_full.at[told_at],
                told_send.at[mask],
                told_recv.at[mask],
                peers[mask],
            )
        )
    homes = [
        remote(home, inputs.at[mine], home_send.at[hop], home_recv.at[hop], (group, other))
        for hop, other in enumerate(others)
    ]
    for copy in smalls + homes:
        copy.start()
    small_full[:, small_at] = small_own[...]
    told_full[told_at] = told_own[...]

    def piece(which, mask, half):
        start = flips(group, mask, bits) * extent + half * half_extent
        return buffers[which].at[pl.ds(pl.multiple_of(start, half_extent), half_extent)]

    def block(which, mask):
        start = flips(group, mask, bits) * extent
        return buffers[which].at[pl.ds(pl.multiple_of(start, extent), extent)]

    far = {}
    near = {}
    for which in range(4):
        for slot, (mask, half, towards) in enumerate(
            ((0, 0, 2), (0, 1, 2), (0, 1, 4), (0, 0, 4), (2, 0, 4), (4, 1, 2))
        ):
            far[which, slot] = remote(
                piece(which, mask, half),
                piece(which, mask, half),
                far_send.at[which, slot],
                far_recv.at[which, slot],
                peers[towards],
            )
        for chip in range(4):
            near[which, chip] = remote(
                block(which, 2 * chip),
                block(which, 2 * chip),
                near_send.at[which, chip],
                near_recv.at[which, chip],
                peers[1],
            )

    def convert(which):
        loads[which].wait()
        count = 32

        def one(step, carry):
            at = pl.ds(pl.multiple_of(step * count, count), count)
            to = pl.ds(pl.multiple_of(group * extent + step * count, count), count)
            buffers[which][to] = stages[which][at].astype(bf16)
            return carry

        lax.fori_loop(0, extent // count, one, 0)

    def leave(which):
        for slot in (0, 2, 1, 3):
            far[which, slot].start()
        near[which, 0].start()

    def pass_on(which):
        far[which, 0].wait_recv()
        far[which, 4].start()
        far[which, 2].wait_recv()
        far[which, 5].start()

    def spread(which):
        far[which, 1].wait_recv()
        near[which, 1].start()
        far[which, 3].wait_recv()
        near[which, 2].start()
        far[which, 4].wait_recv()
        far[which, 5].wait_recv()
        near[which, 3].start()

    def complete(which):
        for chip in range(4):
            near[which, chip].wait_recv()

    convert(0)
    leave(0)
    convert(1)
    leave(1)

    chosen = ((attn_choice[0] == mine) | (attn_choice[1] == mine)) & live
    picked = chosen.astype(f32)
    early = lax.broadcasted_iota(jnp.int32, (seq_len, seq_len), 0)
    late = lax.broadcasted_iota(jnp.int32, (seq_len, seq_len), 1)
    until = (early <= late).astype(f32)
    seats = lax.broadcasted_iota(jnp.int32, (capacity, seq_len), 0).astype(f32) + 1.0
    spot = lax.broadcasted_iota(jnp.int32, (capacity, seq_len), 1).astype(f32)

    def seated(taken):
        slot_of = jnp.dot(taken, until, preferred_element_type=f32)
        return [
            ((slot_of[row : row + 1] == seats) & (taken[row : row + 1] > 0.0)).astype(f32)
            for row in range(experts)
        ]

    tables = seated(picked)
    row_of = lax.broadcasted_iota(jnp.int32, (experts, seq_len), 0)

    def own_row(value):
        return jnp.sum(jnp.where(row_of == mine, value, 0), axis=0, keepdims=True)

    own_live = lane < own_row(jnp.broadcast_to(lengths[...], (experts, seq_len)))
    for choice, table_ref in ((attn_choice, attn_table), (moe_choice, moe_table)):
        goes = ((own_row(choice[0]) == row_of) | (own_row(choice[1]) == row_of)) & own_live
        table_ref[...] = jnp.concatenate(seated(goes.astype(f32)), axis=0).astype(bf16)
    for other in range(experts):
        given_hold[other] = jnp.dot(
            moe_table[other * capacity : (other + 1) * capacity],
            given[...],
            preferred_element_type=f32,
        ).astype(bf16)
    empty = jnp.zeros((capacity, seq_len), f32)
    table_out[...] = jnp.concatenate(
        [
            jnp.concatenate(
                [tables[seq] if seq == other else empty for other in range(experts)], axis=1
            )
            for seq in range(experts)
        ],
        axis=0,
    ).astype(bf16)
    place_out[...] = jnp.concatenate(
        [jnp.sum(table * spot, axis=1, keepdims=True) for table in tables], axis=0
    ).astype(jnp.int32)
    stacked = jnp.concatenate(tables, axis=0)
    vacant = 1.0 - jnp.sum(stacked, axis=1, keepdims=True)
    cos_far[...] = vacant + jnp.dot(
        stacked, cos_home[...], precision=highest, preferred_element_type=f32
    )
    sin_far[...] = jnp.dot(stacked, sin_home[...], precision=highest, preferred_element_type=f32)

    pass_on(0)
    convert(2)
    pass_on(1)
    leave(2)
    convert(3)
    spread(0)
    complete(0)
    spread(1)

    seat.wait()
    for copy in smalls:
        copy.wait_recv()
    gain = small_full[0:1].astype(f32)
    for hop in range(experts):
        source = (mine + experts - hop) % experts
        if hop > 0:
            homes[hop - 1].wait_recv()
        count = 32

        def one(step, carry):
            at = pl.ds(pl.multiple_of(step * count, count), count)
            to = pl.ds(pl.multiple_of(source * seq_len + step * count, count), count)
            value = inputs[source, at].astype(f32)
            normed[to] = (value * norm_scale(value) * gain).astype(bf16)
            return carry

        lax.fori_loop(0, seq_len // count, one, 0)
    own_at = pl.ds(pl.multiple_of(mine * own_width, own_width), own_width)
    values[:, own_at] = jnp.dot(
        normed[...], value_buf[...], preferred_element_type=f32
    ).astype(bf16)
    heads = [
        remote(
            values.at[:, own_at],
            values.at[:, own_at],
            heads_send.at[hop],
            heads_recv.at[hop],
            (group, other),
        )
        for hop, other in enumerate(others)
    ]
    for copy in heads:
        copy.start()
    rows_hold[...] = jnp.dot(table_out[...], normed[...], preferred_element_type=f32).astype(bf16)
    saves = [
        pltpu.make_async_copy(normed, normed_out, save_sem.at[0]),
        pltpu.make_async_copy(rows_hold, rows_out, save_sem.at[1]),
        pltpu.make_async_copy(value_buf, value_own, save_sem.at[2]),
    ]
    for copy in saves:
        copy.start()

    def save(source, target, number):
        copy = pltpu.make_async_copy(source, target, save_sem.at[number])
        copy.start()
        saves.append(copy)

    complete(1)
    save(key_buf.at[:, own_at], key_own, 3)

    def make_keys(step, carry):
        cut = pl.ds(pl.multiple_of(step * tile, tile), tile)
        made = jnp.dot(normed[...], key_buf[:, cut], preferred_element_type=f32)
        for head in range(tile // HEAD):
            lanes = pl.ds(pl.multiple_of(step * tile + head * HEAD, HEAD), HEAD)
            part = made[:, head * HEAD : (head + 1) * HEAD]
            for seq in range(experts):
                rows = slice(seq * seq_len, (seq + 1) * seq_len)
                keys[rows, lanes] = turn(part[rows], cos_home[...], sin_home[...]).astype(bf16)
        return carry

    lax.fori_loop(0, heads_width // tile, make_keys, 0)
    save(keys, key_out, 4)
    pass_on(2)
    leave(3)
    spread(2)
    complete(2)
    save(query_buf, query_full, 5)

    blocks = blocks_of(experts, expert_rows, tokens, tile)
    contract = (((1,), (1,)), ((), ()))
    spots = lax.broadcasted_iota(jnp.int32, (expert_rows, seq_len), 1)
    span_rows = len(blocks) * capacity

    def make_chances(step, carry):
        cut = pl.ds(pl.multiple_of(step * tile, tile), tile)
        made = jnp.dot(rows_hold[...], query_buf[:, cut], preferred_element_type=f32)
        for head in range(tile // HEAD):
            part = slice(head * HEAD, (head + 1) * HEAD)
            query_hold[:, part] = turn(made[:, part], cos_far[...], sin_far[...])
        query_low[:, cut] = query_hold[...].astype(bf16)
        tile_keys = keys[:, cut]
        scores = jnp.concatenate(
            [
                lax.dot_general(
                    query_hold[rows, lanes].astype(bf16),
                    tile_keys[spans, lanes],
                    contract,
                    preferred_element_type=f32,
                )
                for rows, spans, lanes in blocks
            ],
            axis=0,
        )
        seen = spots <= place_out[...]
        probs = softmax_all(scores, jnp.concatenate([seen] * (tile // HEAD), axis=0))
        chances[pl.ds(pl.multiple_of(step * span_rows, 64), span_rows)] = probs.astype(bf16)
        return carry

    lax.fori_loop(0, heads_width // tile, make_chances, 0)
    save(query_low, query_out, 6)
    pass_on(3)
    for copy in heads:
        copy.wait_recv()
    givens = [
        remote(
            given_hold.at[other],
            given_out.at[mine],
            given_send.at[hop],
            given_recv.at[hop],
            (group, other),
        )
        for hop, other in enumerate(others)
    ]
    for copy in givens:
        copy.start()
    save(given_hold.at[mine], given_out.at[mine], 11)
    save(values, value_out, 7)

    def mix(step, carry):
        cut = pl.ds(pl.multiple_of(step * tile, tile), tile)
        tile_values = values[:, cut]
        probs = chances[pl.ds(pl.multiple_of(step * span_rows, 64), span_rows)].astype(f32)
        for count, (rows, spans, lanes) in enumerate(blocks):
            query_hold[rows, lanes] = jnp.dot(
                probs[count * capacity : (count + 1) * capacity].astype(bf16),
                tile_values[spans, lanes],
                preferred_element_type=f32,
            )
        mixture[:, cut] = query_hold[...].astype(bf16)
        return carry

    lax.fori_loop(0, heads_width // tile, mix, 0)
    save(mixture, mixture_out, 8)
    spread(3)
    complete(3)
    save(output_buf, output_full, 9)

    def project(step, carry):
        cut = pl.ds(pl.multiple_of(step * tile, tile), tile)
        branch[:, cut] = jnp.dot(
            mixture[...], output_buf[:, cut], preferred_element_type=f32
        ).astype(bf16)
        return carry

    lax.fori_loop(0, depth // tile, project, 0)
    save(branch, branch_out, 10)
    for copy in givens:
        copy.wait_recv()
    for copy in smalls + homes + heads + givens + list(far.values()) + list(near.values()):
        copy.wait_send()
    for copy in saves:
        copy.wait()


def start_call(
    home,
    attn_gain,
    moe_gain,
    attn_router,
    moe_router,
    attn_choice,
    moe_choice,
    lengths,
    near,
    given,
    value_weight,
    key_weight,
    query_weight,
    output_weight,
):
    experts = 4
    groups = 8
    seq_len, depth = home.shape
    extent, heads_width = key_weight.shape
    capacity = 2 * seq_len // experts + 8
    rows = experts * capacity
    tokens = experts * seq_len
    own_width = heads_width // experts
    small_room = -(-(2 + 2 * experts) // 16) * 16
    vmem = pl.BlockSpec(memory_space=pltpu.VMEM)

    def shaped(*shape, kind=bf16):
        return jax.ShapeDtypeStruct(shape, kind)

    def dma(*shape):
        return pltpu.SemaphoreType.DMA(shape)

    return pl.pallas_call(
        start_kernel,
        out_shape=[
            shaped(small_room, depth),
            shaped(groups * 2 * experts, seq_len, kind=f32),
            shaped(rows, tokens),
            shaped(rows, 1, kind=jnp.int32),
            shaped(rows, HEAD, kind=f32),
            shaped(rows, HEAD, kind=f32),
            shaped(rows, seq_len),
            shaped(rows, seq_len),
            shaped(tokens, depth),
            shaped(rows, depth),
            shaped(rows, heads_width),
            shaped(tokens, heads_width),
            shaped(tokens, heads_width),
            shaped(rows, heads_width),
            shaped(rows, depth),
            shaped(depth, own_width),
            shaped(depth, own_width),
            shaped(depth, heads_width),
            shaped(heads_width, depth),
            shaped(experts, capacity, depth),
        ],
        in_specs=[ANY] + [vmem] * 10 + [ANY] * 4,
        out_specs=[vmem] * 8 + [ANY] * 12,
        scratch_shapes=[
            pltpu.VMEM((experts, seq_len, depth), bf16),
            pltpu.VMEM((small_room, extent), bf16),
            pltpu.VMEM((2 * experts, seq_len), f32),
            pltpu.VMEM((small_room, extent), f32),
            pltpu.VMEM((tokens, depth), bf16),
            pltpu.VMEM((rows, depth), bf16),
            pltpu.VMEM((rows, 256), f32),
            pltpu.VMEM((rows, heads_width), bf16),
            pltpu.VMEM((tokens, heads_width), bf16),
            pltpu.VMEM((tokens, heads_width), bf16),
            pltpu.VMEM((rows * heads_width // HEAD, seq_len), bf16),
            pltpu.VMEM((rows, heads_width), bf16),
            pltpu.VMEM((rows, depth), bf16),
            pltpu.VMEM((experts, capacity, depth), bf16),
            pltpu.VMEM((extent, own_width), f32),
            pltpu.VMEM((extent, heads_width), f32),
            pltpu.VMEM((extent, heads_width), f32),
            pltpu.VMEM((extent, depth), f32),
            pltpu.VMEM((depth, own_width), bf16),
            pltpu.VMEM((depth, heads_width), bf16),
            pltpu.VMEM((depth, heads_width), bf16),
            pltpu.VMEM((heads_width, depth), bf16),
            dma(5),
            dma(4, 6),
            dma(4, 6),
            dma(4, 4),
            dma(4, 4),
            dma(3),
            dma(3),
            dma(8),
            dma(8),
            dma(8),
            dma(8),
            dma(3),
            dma(3),
            dma(3),
            dma(3),
            dma(12),
        ],
        compiler_params=pltpu.CompilerParams(
            collective_id=4, has_side_effects=True, vmem_limit_bytes=61 * 1024 * 1024
        ),
        cost_estimate=pl.CostEstimate(
            flops=100_000_000_000, bytes_accessed=300_000_000, transcendentals=0
        ),
        name="attend_start",
    )(
        home,
        attn_gain,
        moe_gain,
        attn_router,
        moe_router,
        attn_choice,
        moe_choice,
        lengths,
        *near,
        given,
        value_weight,
        key_weight,
        query_weight,
        output_weight,
    )


def start_plain(
    home,
    attn_gain,
    moe_gain,
    attn_router,
    moe_router,
    attn_choice,
    moe_choice,
    lengths,
    near,
    given,
    value_weight,
    key_weight,
    query_weight,
    output_weight,
):
    experts = lax.axis_size("expert")
    mine = lax.axis_index("expert")
    seq_len, depth = home.shape
    heads_width = key_weight.shape[1]
    own_width = heads_width // experts
    capacity = 2 * seq_len // experts + 8
    rows = experts * capacity
    kinds = 2 + 2 * experts
    small_own = jnp.concatenate(
        [
            attn_gain,
            moe_gain,
            attn_router,
            moe_router,
            jnp.zeros((-kinds % 16, attn_gain.shape[1]), f32),
        ]
    ).astype(bf16)
    places = jnp.arange(seq_len, dtype=jnp.int32)
    live = places[None] < lengths
    told = jnp.where(live, moe_choice, -1).astype(f32).reshape(2 * experts, seq_len)
    key_full, value_full, query_full, output_full, small_full, told_full, inputs = gather_all(
        [
            key_weight.astype(bf16),
            value_weight.astype(bf16),
            query_weight.astype(bf16),
            output_weight.astype(bf16),
            small_own,
            told,
        ],
        (2, 2, 2, 2, 1, 1),
        (0, 0, 0, 0, 1, 0),
        home,
    )

    def tables_of(choice):
        return jax.vmap(partial(route_table, experts=experts, capacity=capacity))(
            choice.transpose(1, 2, 0), lengths[:, 0]
        )

    attn_all, moe_all = tables_of(attn_choice), tables_of(moe_choice)
    group_table = lax.dynamic_index_in_dim(attn_all, mine, 1, keepdims=False)
    own_attn = lax.dynamic_index_in_dim(attn_all, mine, 0, keepdims=False).astype(bf16)
    own_moe = lax.dynamic_index_in_dim(moe_all, mine, 0, keepdims=False).astype(bf16)
    row_places = jnp.sum(jnp.where(group_table, places, 0), axis=-1).reshape(rows, 1)
    same = jnp.eye(experts, dtype=bool)[:, None, :, None]
    table = (group_table[:, :, None, :] & same).astype(bf16).reshape(rows, experts * seq_len)
    far = signed_tables(row_places[:, 0])
    all_near = tuple(jnp.tile(part, (experts, 1)) for part in near)
    normed, rows_flat, queries, keys, values, mixture = attend(
        experts,
        inputs.reshape(experts * seq_len, depth),
        small_full,
        table,
        row_places,
        far,
        all_near,
        query_full,
        key_full,
        value_full,
    )
    branch = jnp.dot(mixture, output_full, preferred_element_type=f32).astype(bf16)
    given_rows = jnp.einsum("ect,td->ecd", own_moe, given, preferred_element_type=f32)

    def own_heads(weight):
        return lax.dynamic_slice_in_dim(weight, mine * own_width, own_width, 1)

    return (
        small_full,
        told_full,
        table,
        row_places,
        *far,
        own_attn.reshape(rows, seq_len),
        own_moe.reshape(rows, seq_len),
        normed,
        rows_flat,
        queries,
        keys,
        values,
        mixture,
        branch,
        own_heads(value_full),
        own_heads(key_full),
        query_full,
        output_full,
        exchange(given_rows.astype(bf16)),
    )


def ffn_plain(own, slopes, picks, router, gate, up, down):
    groups, rows, width = slopes.shape
    depth = own.shape[1]
    held = lax.all_gather(own, "dp", axis=0, tiled=True)
    logits = jnp.einsum("rd,ed->re", held, router, preferred_element_type=f32)
    weight = 1.0 / (1.0 + jnp.exp(jnp.sum(logits * picks, axis=-1, keepdims=True)))
    plain = slopes.reshape(groups * rows, width)
    gate_pre = jnp.einsum("rd,fd->rf", held, gate, preferred_element_type=f32)
    up_pre = jnp.einsum("rd,fd->rf", held, up, preferred_element_type=f32)
    sigmoid = 1.0 / (1.0 + jnp.exp(-gate_pre))
    active = gate_pre * sigmoid
    hidden = (active * up_pre).astype(bf16)
    wide = hidden.astype(f32)
    inner = weight * plain
    grad_gate = (inner * up_pre * (sigmoid * (1.0 + gate_pre * (1.0 - sigmoid)))).astype(bf16)
    grad_up = (inner * active).astype(bf16)
    made = jnp.dot(hidden, down, preferred_element_type=f32).astype(bf16)
    grads = (
        jnp.dot(grad_gate, gate, preferred_element_type=f32)
        + jnp.dot(grad_up, up, preferred_element_type=f32)
    ).astype(bf16)
    grads = lax.psum_scatter(
        grads.reshape(groups, rows, depth), "dp", scatter_dimension=0, tiled=True
    )[0]
    dense = lax.psum_scatter(
        jnp.sum(wide * plain, axis=-1).reshape(groups, rows),
        "dp",
        scatter_dimension=0,
        tiled=True,
    )

    def split(value):
        return value.reshape(groups, rows, value.shape[-1])

    upper = dense[0][:, None].astype(bf16)
    lower = (dense[0][:, None] - upper.astype(f32)).astype(bf16)
    grads = jnp.concatenate([grads, upper, lower, jnp.zeros((rows, 126), bf16)], axis=1)
    scaled = (weight * wide).astype(bf16)
    return (
        split(held),
        split(scaled),
        split(grad_gate),
        split(grad_up),
        split(made),
        grads,
    )


def back_plain(grad_rows, rows_flat, places, far, near, output_w, query, key, value, mixture):
    experts = lax.axis_size("expert")
    grad_query, keys_part, values_part, output_part = attend_back(
        experts, grad_rows, places, far, output_w, query, key, value, mixture
    )
    output_sum = lax.psum_scatter(output_part, "dp", scatter_dimension=0, tiled=True)
    grad_values = jnp.sum(exchange(values_part).astype(f32), axis=0).astype(bf16)
    grad_keys = jnp.sum(exchange(keys_part).astype(f32), axis=0)
    grad_keys = jnp.concatenate(
        [
            turned_back(grad_keys[:, start : start + HEAD], near)
            for start in range(0, grad_keys.shape[1], HEAD)
        ],
        axis=1,
    ).astype(bf16)
    query_part = jnp.einsum("rd,re->de", rows_flat, grad_query, preferred_element_type=f32)
    query_sum = lax.psum_scatter(
        query_part.astype(bf16), "dp", scatter_dimension=0, tiled=True
    )
    return grad_query, grad_keys, grad_values, output_sum, query_sum


def exchange(value):
    return lax.all_to_all(value, "expert", split_axis=0, concat_axis=0, tiled=True)


def on_device(
    hidden_in,
    out_grad,
    seq_lengths,
    attn_choice,
    moe_choice,
    attn_gain,
    moe_gain,
    attn_router,
    moe_router,
    key_weight,
    value_weight,
    query_weight,
    output_weight,
    gate_weight,
    up_weight,
    down_weight,
):
    experts = lax.axis_size("expert")
    groups = lax.axis_size("dp")
    mine_index = lax.axis_index("expert")
    seq_len = hidden_in.shape[1]
    model_width = hidden_in.shape[2]
    head_width = query_weight.shape[2]
    own_width = head_width // experts
    capacity = 2 * seq_len // experts + 8
    expert_rows = experts * capacity
    total_rows = groups * expert_rows
    score_scale = HEAD ** (-0.5)
    places = jnp.arange(seq_len, dtype=jnp.int32)
    own_length = lax.dynamic_index_in_dim(seq_lengths, mine_index, 0, keepdims=False)
    live_rows = (places < own_length).astype(f32)
    own_attn = lax.dynamic_index_in_dim(attn_choice, mine_index, 0, keepdims=False)
    own_moe = lax.dynamic_index_in_dim(moe_choice, mine_index, 0, keepdims=False)
    kinds = 2 + 2 * experts
    ready = groups == 8 and experts == 4
    near_home = signed_tables(places)
    (
        small_full,
        told_full,
        spread_table,
        row_places,
        cos_far,
        sin_far,
        table_attn,
        table_moe,
        normed_group,
        rows_flat,
        queries,
        keys_all,
        values_all,
        mixture,
        attn_rows,
        value_own,
        key_own,
        query_full,
        output_full,
        given_rows,
    ) = (start_call if ready else start_plain)(
        hidden_in[0],
        attn_gain[None],
        moe_gain[None],
        attn_router.T,
        moe_router.T,
        attn_choice.transpose(2, 0, 1),
        moe_choice.transpose(2, 0, 1),
        seq_lengths[:, None],
        near_home,
        out_grad[0],
        value_weight,
        key_weight,
        query_weight[0],
        output_weight[0],
    )
    far = (cos_far, sin_far)
    near = tuple(jnp.tile(part, (experts, 1)) for part in near_home)
    table_attn = table_attn.reshape(experts, capacity, seq_len)
    table_moe = table_moe.reshape(experts, capacity, seq_len)
    given_all = lax.all_gather(
        given_rows.reshape(expert_rows, model_width), "dp", axis=0, tiled=True
    )
    attn_rows = attn_rows.reshape(experts, capacity, model_width)

    gain_attn = small_full[0].astype(f32)
    gain_moe = small_full[1].astype(f32)
    router_attn = small_full[2 : 2 + experts]
    router_moe = small_full[2 + experts : kinds]
    inputs_f = hidden_in[0].astype(f32)
    scale_one = norm_scale(inputs_f)
    normed_one = (inputs_f * scale_one * gain_attn).astype(bf16)
    attn_logits = jnp.einsum("td,ed->te", normed_one, router_attn, preferred_element_type=f32)
    onehot_attn, shares_attn, dense_attn = router_gates(attn_logits, own_attn, live_rows, experts)

    told = told_full.reshape(groups, 2, experts, seq_len).transpose(1, 0, 2, 3)
    told = told.reshape(2, groups * experts, seq_len).astype(jnp.int32)
    comes = (told[0] == mine_index) | (told[1] == mine_index)
    order = jnp.cumsum(comes.astype(jnp.int32), axis=1) - 1
    slots = jnp.arange(capacity, dtype=jnp.int32)[None, :, None]
    rivals = jnp.sum(
        jnp.where(
            (order[:, None, :] == slots) & comes[:, None, :],
            (told[0] + told[1] - mine_index)[:, None, :],
            0,
        ),
        axis=-1,
    ).reshape(total_rows, 1)
    back_attn = exchange(attn_rows)
    spread_attn = jnp.einsum("ect,ecd->etd", table_attn, back_attn, preferred_element_type=f32)
    attn_sum = jnp.sum(dense_attn.T[:, :, None] * spread_attn, axis=0)
    middle = inputs_f + attn_sum
    scale_two = norm_scale(middle)
    normed_two = (middle * scale_two * gain_moe).astype(bf16)
    moe_logits = jnp.einsum("td,ed->te", normed_two, router_moe, preferred_element_type=f32)
    onehot_moe, shares_moe, dense_moe = router_gates(moe_logits, own_moe, live_rows, experts)
    send_moe = jnp.einsum(
        "ect,td->ecd", table_moe, normed_two, preferred_element_type=f32
    ).astype(bf16)
    rows_moe = exchange(send_moe).reshape(expert_rows, model_width)

    units = gate_weight.shape[2]
    room = -(-units // 256) * 256
    gate_slice = jnp.pad(gate_weight[0].T.astype(bf16), ((0, room - units), (0, 0)))
    up_slice = jnp.pad(up_weight[0].T.astype(bf16), ((0, room - units), (0, 0)))
    down_slice = jnp.pad(down_weight[0].astype(bf16), ((0, room - units), (0, 0)))
    slopes = jnp.einsum("rd,fd->rf", given_all, down_slice, preferred_element_type=f32)
    expert_ids = jnp.arange(16, dtype=jnp.int32)[None, :]
    picks = (expert_ids == rivals).astype(f32) - (
        expert_ids == mine_index
    ).astype(f32)
    router_rows = jnp.pad(router_moe, ((0, 16 - experts), (0, 0)))
    feed = ffn_call if groups == 8 and expert_rows % 96 == 0 else ffn_plain
    ffn_rows, scaled, grad_gate, grad_up, partial_out, grad_ffn = feed(
        rows_moe,
        slopes.reshape(groups, expert_rows, room),
        picks,
        router_rows,
        gate_slice,
        up_slice,
        down_slice,
    )
    back_moe_grad = exchange(grad_ffn.reshape(experts, capacity, model_width + 128))
    summed_out = lax.psum_scatter(partial_out, "dp", scatter_dimension=0, tiled=True)
    ffn_rows = ffn_rows.reshape(total_rows, model_width)
    down_grad = jnp.einsum(
        "rf,rd->fd",
        scaled.reshape(total_rows, room)[:, :units],
        given_all,
        preferred_element_type=f32,
    )[None]
    gate_grad = jnp.einsum(
        "rd,rf->df",
        ffn_rows,
        grad_gate.reshape(total_rows, room)[:, :units],
        preferred_element_type=f32,
    )[None]
    up_grad = jnp.einsum(
        "rd,rf->df",
        ffn_rows,
        grad_up.reshape(total_rows, room)[:, :units],
        preferred_element_type=f32,
    )[None]
    back_moe_grad, down_grad, gate_grad = lax.optimization_barrier(
        (back_moe_grad, down_grad, gate_grad)
    )
    back_dense = jnp.sum(back_moe_grad[:, :, model_width:].astype(f32), axis=-1)
    back_moe_grad = back_moe_grad[:, :, :model_width]

    grad_out = out_grad[0].astype(f32) * live_rows[:, None]
    grad_dense_moe = jnp.sum(table_moe.astype(f32) * back_dense[:, :, None], axis=1).T
    grad_normed_two = jnp.einsum(
        "ect,ecd->td", table_moe, back_moe_grad, preferred_element_type=f32
    )
    grad_logits_moe = gates_backward(grad_dense_moe, onehot_moe, shares_moe, live_rows)
    grad_normed_two = grad_normed_two + jnp.dot(
        grad_logits_moe, router_moe.astype(f32), precision=highest
    )
    moe_router_part = jnp.dot(grad_logits_moe.T, normed_two.astype(f32), precision=highest)
    grad_middle_norm, moe_gain_part = norm_backward(grad_normed_two, middle, scale_two, gain_moe)
    grad_middle = grad_out + grad_middle_norm
    grad_dense_attn = jnp.sum(grad_middle[None] * spread_attn, axis=-1).T
    rows_attn_grad = (dense_attn.T[:, :, None] * grad_middle[None]).astype(bf16)
    send_attn_grad = jnp.einsum(
        "ect,etd->ecd", table_attn, rows_attn_grad, preferred_element_type=f32
    ).astype(bf16)
    recv_attn_grad = exchange(send_attn_grad)
    recv_attn_grad, up_grad, summed_out = lax.optimization_barrier(
        (recv_attn_grad, up_grad, summed_out)
    )

    back_moe = exchange(summed_out[0].reshape(experts, capacity, model_width))
    backward = back_call if ready else back_plain
    grad_query_pre, grad_key_pre, grad_values, output_out, query_out = backward(
        recv_attn_grad.reshape(expert_rows, model_width),
        rows_flat,
        row_places,
        far,
        near,
        output_full,
        queries,
        keys_all,
        values_all,
        mixture,
    )
    grad_query_pre, back_moe = lax.optimization_barrier((grad_query_pre, back_moe))
    grad_rows_attn = jnp.einsum(
        "re,de->rd", grad_query_pre, query_full, preferred_element_type=f32
    ).astype(bf16)
    grad_normed_part = (
        jnp.einsum("rt,rd->td", spread_table, grad_rows_attn, preferred_element_type=f32)
        + jnp.einsum("te,de->td", grad_key_pre, key_own, preferred_element_type=f32)
        + jnp.einsum("te,de->td", grad_values, value_own, preferred_element_type=f32)
    ).astype(bf16)
    grad_normed_part, grad_key_pre, grad_values = lax.optimization_barrier(
        (grad_normed_part, grad_key_pre, grad_values)
    )
    normed_got = exchange(grad_normed_part.reshape(experts, seq_len, model_width))
    both_part = jnp.einsum(
        "td,te->de",
        normed_group,
        jnp.concatenate([grad_key_pre, grad_values], axis=1),
        preferred_element_type=f32,
    ).astype(bf16)
    both_own = lax.psum_scatter(both_part, "dp", scatter_dimension=0, tiled=True)
    normed_got, both_part = lax.optimization_barrier((normed_got, both_part))
    grad_normed_one = jnp.sum(normed_got.astype(f32), axis=0)
    both_own = exchange(both_own.reshape(experts, -1, 2 * own_width))
    both_own = both_own.reshape(experts, -1, 2, own_width).transpose(2, 1, 0, 3).astype(f32)
    key_grad = both_own[0].reshape(-1, head_width)
    value_grad = both_own[1].reshape(-1, head_width)

    spread_moe = jnp.einsum("ect,ecd->etd", table_moe, back_moe, preferred_element_type=f32)
    moe_sum = jnp.sum(dense_moe.T[:, :, None] * spread_moe, axis=0)
    block_out = (live_rows[:, None] * (middle + moe_sum)).astype(bf16)[None]
    grad_logits_attn = gates_backward(grad_dense_attn, onehot_attn, shares_attn, live_rows)
    attn_router_part = jnp.dot(grad_logits_attn.T, normed_one.astype(f32), precision=highest)
    grad_normed_one = grad_normed_one + jnp.dot(
        grad_logits_attn, router_attn.astype(f32), precision=highest
    )
    grad_inputs_norm, attn_gain_part = norm_backward(
        grad_normed_one, inputs_f, scale_one, gain_attn
    )
    input_grad = (grad_middle + grad_inputs_norm).astype(bf16)[None]
    smalls = total_small(
        jnp.concatenate(
            [attn_gain_part[None], moe_gain_part[None], attn_router_part, moe_router_part]
        )
    )
    return (
        block_out,
        input_grad,
        smalls[0],
        smalls[1],
        smalls[2 : 2 + experts].T,
        smalls[2 + experts : kinds].T,
        key_grad,
        value_grad,
        query_out.astype(f32)[None],
        output_out.astype(f32)[None],
        gate_grad,
        up_grad,
        down_grad,
    )


def solution(mesh):
    placed = (
        P(("dp", "expert"), None, None),
        P(("dp", "expert"), None, None),
        P("dp"),
        P("dp", None, None),
        P("dp", None, None),
        P("dp"),
        P("dp"),
        P("dp", None),
        P("dp", None),
        P("dp", None),
        P("dp", None),
        P("expert", "dp", None),
        P("expert", "dp", None),
        P("expert", None, "dp"),
        P("expert", None, "dp"),
        P("expert", "dp", None),
    )
    return jax.shard_map(
        on_device,
        mesh=mesh,
        in_specs=placed,
        out_specs=(
            P(("dp", "expert"), None, None),
            P(("dp", "expert"), None, None),
            P(("dp", "expert")),
            P(("dp", "expert")),
            P(("dp", "expert"), None),
            P(("dp", "expert"), None),
            P(("dp", "expert"), None),
            P(("dp", "expert"), None),
            P("expert", "dp", None),
            P("expert", "dp", None),
            P("expert", None, "dp"),
            P("expert", None, "dp"),
            P("expert", "dp", None),
        ),
        check_vma=False,
    )
```

```python
from functools import partial

import jax
import jax.numpy as jnp
from jax import lax
from jax.experimental import pallas as pl
from jax.experimental.pallas import tpu as pltpu
from jax.sharding import PartitionSpec as P

HEADS = 16
HEAD = 128
MESH = pl.DeviceIdType.MESH
ANY = pl.BlockSpec(memory_space=pl.ANY)

eps = 1e-06
theta = 10000.0
highest = lax.Precision.HIGHEST
f32 = jnp.float32
bf16 = jnp.bfloat16


def rope_tables(positions, head_size):
    half_size = head_size // 2
    frequency = theta ** (-(jnp.arange(half_size, dtype=f32) * 2.0 / head_size))
    angles = positions.astype(f32)[:, None] * frequency[None, :]
    return (jnp.cos(angles), jnp.sin(angles))


def signed_tables(positions):
    cosine, sine = rope_tables(positions, HEAD)
    return (jnp.concatenate([cosine, cosine], 1), jnp.concatenate([-sine, sine], 1))


def turned_back(value, tables):
    half_size = HEAD // 2
    swapped = jnp.concatenate([value[:, half_size:], value[:, :half_size]], axis=1)
    return value * tables[0] - swapped * tables[1]


def norm_scale(value):
    return lax.rsqrt(jnp.mean(value * value, axis=-1, keepdims=True) + eps)


def norm_backward(grad_normed, value, scale_value, gain_value):
    scaled_grad = grad_normed * gain_value
    gain_part = jnp.sum(grad_normed * value * scale_value, axis=0)
    grad_value = scale_value * scaled_grad - value * scale_value**3 * jnp.mean(
        scaled_grad * value, axis=-1, keepdims=True
    )
    return (grad_value, gain_part)


def softmax_rows(values):
    peak = jnp.max(values, axis=-1, keepdims=True)
    powers = jnp.exp(values - peak)
    return powers / jnp.sum(powers, axis=-1, keepdims=True)


def router_gates(logits, choices, live_rows, experts):
    onehot = (choices[:, :, None] == jnp.arange(experts, dtype=jnp.int32)[None, None, :]).astype(
        f32
    )
    chosen = jnp.sum(logits[:, None, :] * onehot, axis=-1)
    shares = softmax_rows(chosen)
    dense = jnp.sum((shares * live_rows[:, None])[:, :, None] * onehot, axis=1)
    return (onehot, shares, dense)


def gates_backward(grad_dense, onehot, shares, live_rows):
    grad_shares = jnp.sum(grad_dense[:, None, :] * onehot, axis=-1) * live_rows[:, None]
    grad_chosen = shares * (grad_shares - jnp.sum(shares * grad_shares, axis=-1, keepdims=True))
    return jnp.sum(grad_chosen[:, :, None] * onehot, axis=1)


def route_table(choices, length_value, experts, capacity):
    places = jnp.arange(choices.shape[0], dtype=jnp.int32)
    living = (places < length_value).astype(jnp.int32)
    picked = (
        jnp.sum(
            (choices[:, :, None] == jnp.arange(experts, dtype=jnp.int32)[None, None, :]).astype(
                jnp.int32
            ),
            axis=1,
        )
        * living[:, None]
    )
    slot_of = jnp.cumsum(picked, axis=0) - 1
    slot_ids = jnp.arange(capacity, dtype=jnp.int32)
    return (slot_of.T[:, None, :] == slot_ids[None, :, None]) & (picked.T[:, None, :] == 1)


def flip(index, bit):
    return index + bit * (1 - 2 * ((index // bit) % 2))


def flips(index, mask, bits):
    for bit in bits:
        if mask & bit:
            index = flip(index, bit)
    return index


def span(bits):
    masks = [0]
    for bit in bits:
        masks = masks + [mask | bit for mask in masks]
    return masks


def bit_orders(size):
    bits = [1 << k for k in range(size.bit_length() - 1)]
    high = bits[1:]
    return (high + bits[:1], high[::-1] + bits[:1])


def barrier(targets):
    semaphore = pltpu.get_barrier_semaphore()
    for target in targets:
        pl.semaphore_signal(semaphore, inc=1, device_id=target, device_id_type=MESH)
    pl.semaphore_wait(semaphore, len(targets))


def gather_kernel(groups, experts, splits, axes, *refs):
    count = len(splits)
    shards, home = refs[:count], refs[count]
    fulls, home_all = refs[count + 1 : 2 * count + 1], refs[2 * count + 1]
    local_sem, send_sem, recv_sem, home_send, home_recv = refs[2 * count + 2 :]
    group = lax.axis_index("dp")
    mine = lax.axis_index("expert")
    orders = bit_orders(groups)
    bits = sorted(orders[0])
    others = [(mine + step) % experts for step in range(1, experts)]
    barrier([(flip(group, bit), mine) for bit in bits] + [(group, other) for other in others])

    home_copies = []
    for step, other in enumerate(others):
        copy = pltpu.make_async_remote_copy(
            src_ref=home,
            dst_ref=home_all.at[mine],
            send_sem=home_send.at[step],
            recv_sem=home_recv.at[step],
            device_id=(group, other),
            device_id_type=MESH,
        )
        copy.start()
        home_copies.append(copy)

    def part(ref, which, block, half):
        pieces, axis = splits[which], axes[which]
        extent = shards[which].shape[axis]
        size = extent // pieces
        start = half * size if block is None else block * extent + half * size
        if block is not None:
            start = pl.multiple_of(start, size)
        where = pl.ds(start, size)
        return ref.at[where] if axis == 0 else ref.at[:, where]

    stages = {}
    slot = 0
    for which in range(count):
        for half in range(splits[which]):
            order = orders[half]
            for stage, bit in enumerate(order):
                copies = []
                for mask in span(order[:stage]):
                    block = flips(group, mask, bits)
                    target = part(fulls[which], which, block, half)
                    source = part(shards[which], which, None, half) if mask == 0 else target
                    copies.append(
                        pltpu.make_async_remote_copy(
                            src_ref=source,
                            dst_ref=target,
                            send_sem=send_sem.at[slot],
                            recv_sem=recv_sem.at[slot],
                            device_id=(flip(group, bit), mine),
                            device_id_type=MESH,
                        )
                    )
                    slot += 1
                stages[which, half, stage] = copies
    keys = [(which, half) for which in range(count) for half in range(splits[which])]
    for which, half in keys:
        for copy in stages[which, half, 0]:
            copy.start()
    local = [pltpu.make_async_copy(home, home_all.at[mine], local_sem.at[count])]
    for which in range(count):
        extent = shards[which].shape[axes[which]]
        where = pl.ds(pl.multiple_of(group * extent, extent), extent)
        target = fulls[which].at[where] if axes[which] == 0 else fulls[which].at[:, where]
        local.append(pltpu.make_async_copy(shards[which], target, local_sem.at[which]))
    for copy in local:
        copy.start()
    for stage in range(len(bits)):
        for which, half in keys:
            for copy in stages[which, half, stage]:
                copy.wait_recv()
            if stage + 1 < len(bits):
                for copy in stages[which, half, stage + 1]:
                    copy.start()
    for copies in stages.values():
        for copy in copies:
            copy.wait_send()
    for copy in home_copies:
        copy.wait()
    for copy in local:
        copy.wait()


def gather_all(arrays, splits, axes, home):
    groups = lax.axis_size("dp")
    experts = lax.axis_size("expert")
    shapes = []
    for array, axis in zip(arrays, axes):
        shape = list(array.shape)
        shape[axis] *= groups
        shapes.append(jax.ShapeDtypeStruct(tuple(shape), array.dtype))
    shapes.append(jax.ShapeDtypeStruct((experts,) + home.shape, home.dtype))
    slots = sum(splits) * (groups - 1)
    return pl.pallas_call(
        partial(gather_kernel, groups, experts, splits, axes),
        out_shape=shapes,
        in_specs=[ANY] * (len(arrays) + 1),
        out_specs=[ANY] * (len(arrays) + 1),
        scratch_shapes=[
            pltpu.SemaphoreType.DMA((len(arrays) + 1,)),
            pltpu.SemaphoreType.DMA((slots,)),
            pltpu.SemaphoreType.DMA((slots,)),
            pltpu.SemaphoreType.DMA((experts - 1,)),
            pltpu.SemaphoreType.DMA((experts - 1,)),
        ],
        compiler_params=pltpu.CompilerParams(collective_id=0, has_side_effects=True),
        name="gather_all",
    )(*arrays, home)


def total_kernel(groups, experts, parts, total, held, send_sem, recv_sem):
    devices = groups * experts
    me = lax.axis_index("dp") * experts + lax.axis_index("expert")
    semaphore = pltpu.get_barrier_semaphore()

    def greet(step, carry):
        other = (me + step) % devices
        pl.semaphore_signal(
            semaphore,
            inc=1,
            device_id=(other // experts, other % experts),
            device_id_type=MESH,
        )
        return carry

    lax.fori_loop(1, devices, greet, 0)
    pl.semaphore_wait(semaphore, devices - 1)

    def copy_of(step):
        other = (me + step) % devices
        return pltpu.make_async_remote_copy(
            src_ref=parts.at[other],
            dst_ref=held.at[step],
            send_sem=send_sem.at[step],
            recv_sem=recv_sem.at[step],
            device_id=(other // experts, other % experts),
            device_id_type=MESH,
        )

    def send(step, carry):
        copy_of(step).start()
        return carry

    lax.fori_loop(1, devices, send, 0)
    held[0] = parts[me]

    def finish(step, carry):
        copy_of(step).wait()
        return carry

    lax.fori_loop(1, devices, finish, 0)
    total[...] = jnp.sum(held[...], axis=0)


def total_small(rows):
    groups = lax.axis_size("dp")
    experts = lax.axis_size("expert")
    devices = groups * experts
    kinds, width = rows.shape
    share = width // devices
    packed = rows.reshape(kinds, devices, share).transpose(1, 0, 2).reshape(devices, kinds * share)
    room = -(-kinds * share // 1024) * 1024
    packed = jnp.pad(packed, ((0, 0), (0, room - kinds * share))).reshape(
        devices, room // 128, 128
    )
    summed = pl.pallas_call(
        partial(total_kernel, groups, experts),
        out_shape=jax.ShapeDtypeStruct((room // 128, 128), f32),
        in_specs=[pl.BlockSpec(memory_space=pltpu.VMEM)],
        out_specs=pl.BlockSpec(memory_space=pltpu.VMEM),
        scratch_shapes=[
            pltpu.VMEM((devices, room // 128, 128), f32),
            pltpu.SemaphoreType.DMA((devices,)),
            pltpu.SemaphoreType.DMA((devices,)),
        ],
        compiler_params=pltpu.CompilerParams(collective_id=1, has_side_effects=True),
        name="total_small",
    )(packed)
    return summed.reshape(-1)[: kinds * share].reshape(kinds, share)


def turn(value, cosine, sine):
    return value * cosine + pltpu.roll(value, HEAD // 2, 1) * sine


def softmax_all(scores, seen):
    masked = jnp.where(seen, scores * (HEAD ** (-0.5)), -1e30)
    powers = jnp.exp(masked - jnp.max(masked, axis=-1, keepdims=True))
    return powers / jnp.sum(powers, axis=-1, keepdims=True)


def blocks_of(experts, rows, tokens, width):
    capacity, seq_len = rows // experts, tokens // experts
    return [
        (
            slice(seq * capacity, (seq + 1) * capacity),
            slice(seq * seq_len, (seq + 1) * seq_len),
            slice(head * HEAD, (head + 1) * HEAD),
        )
        for head in range(width // HEAD)
        for seq in range(experts)
    ]


def attend_kernel(
    experts,
    inputs_ref,
    small_ref,
    table_ref,
    place_ref,
    cos_far,
    sin_far,
    cos_near,
    sin_near,
    query_weight,
    key_weight,
    value_weight,
    normed_out,
    rows_out,
    query_out,
    key_out,
    value_out,
    mixture_out,
    query_hold,
):
    @pl.when(pl.program_id(0) == 0)
    def _():
        gain = small_ref[0:1].astype(f32)

        def norm_part(step, carry):
            at = pl.ds(pl.multiple_of(step * 32, 32), 32)
            value = inputs_ref[at].astype(f32)
            normed_out[at] = (value * norm_scale(value) * gain).astype(bf16)
            return carry

        lax.fori_loop(0, inputs_ref.shape[0] // 32, norm_part, 0)
        rows_out[...] = jnp.dot(
            table_ref[...], normed_out[...], preferred_element_type=f32
        ).astype(bf16)

    capacity = rows_out.shape[0] // experts
    seq_len = normed_out.shape[0] // experts
    width = key_out.shape[1]
    key = jnp.dot(normed_out[...], key_weight[...], preferred_element_type=f32)
    value_out[...] = jnp.dot(
        normed_out[...], value_weight[...], preferred_element_type=f32
    ).astype(bf16)
    query = jnp.dot(rows_out[...], query_weight[...], preferred_element_type=f32)
    for head in range(width // HEAD):
        cut = slice(head * HEAD, (head + 1) * HEAD)
        key_out[:, cut] = turn(key[:, cut], cos_near[...], sin_near[...]).astype(bf16)
        query_hold[:, cut] = turn(query[:, cut], cos_far[...], sin_far[...])
    query_out[...] = query_hold[...].astype(bf16)
    blocks = blocks_of(experts, rows_out.shape[0], normed_out.shape[0], width)
    contract = (((1,), (1,)), ((), ()))
    scores = jnp.concatenate(
        [
            lax.dot_general(
                query_hold[rows, cut].astype(bf16),
                key_out[keys, cut],
                contract,
                preferred_element_type=f32,
            )
            for rows, keys, cut in blocks
        ],
        axis=0,
    )
    spots = lax.broadcasted_iota(jnp.int32, (rows_out.shape[0], seq_len), 1)
    seen = spots <= place_ref[...]
    probs = softmax_all(scores, jnp.concatenate([seen] * (width // HEAD), axis=0))
    for number, (rows, keys, cut) in enumerate(blocks):
        query_hold[rows, cut] = jnp.dot(
            probs[number * capacity : (number + 1) * capacity].astype(bf16),
            value_out[keys, cut],
            preferred_element_type=f32,
        )
    mixture_out[...] = query_hold[...].astype(bf16)


def attend(experts, inputs, small, table, places, far, near, query_w, key_w, value_w):
    tokens, depth = inputs.shape
    rows = table.shape[0]
    heads_width = query_w.shape[1]
    tile = 256

    def full(shape):
        return pl.BlockSpec(shape, lambda step: (0, 0))

    def cut(height):
        return pl.BlockSpec((height, tile), lambda step: (0, step))

    def shaped(height, width):
        return jax.ShapeDtypeStruct((height, width), bf16)

    return pl.pallas_call(
        partial(attend_kernel, experts),
        grid=(heads_width // tile,),
        out_shape=[
            shaped(tokens, depth),
            shaped(rows, depth),
            shaped(rows, heads_width),
            shaped(tokens, heads_width),
            shaped(tokens, heads_width),
            shaped(rows, heads_width),
        ],
        in_specs=[
            full((tokens, depth)),
            full(small.shape),
            full(table.shape),
            full(places.shape),
            full((rows, HEAD)),
            full((rows, HEAD)),
            full((tokens, HEAD)),
            full((tokens, HEAD)),
            cut(depth),
            cut(depth),
            cut(depth),
        ],
        out_specs=[
            full((tokens, depth)),
            full((rows, depth)),
            cut(rows),
            cut(tokens),
            cut(tokens),
            cut(rows),
        ],
        scratch_shapes=[pltpu.VMEM((rows, tile), f32)],
        compiler_params=pltpu.CompilerParams(vmem_limit_bytes=48 * 1024 * 1024),
        cost_estimate=pl.CostEstimate(
            flops=2 * depth * heads_width * (2 * tokens + rows),
            bytes_accessed=6 * depth * heads_width + 8 * tokens * depth,
            transcendentals=rows * heads_width,
        ),
        name="attend",
    )(inputs, small, table, places, *far, *near, query_w, key_w, value_w)


def attend_back_kernel(
    experts,
    grad_ref,
    place_ref,
    cos_far,
    sin_far,
    weight_ref,
    query_ref,
    key_ref,
    value_ref,
    mixture_ref,
    query_out,
    key_out,
    value_out,
    output_out,
    grad_hold,
    query_hold,
    back_hold,
):
    contract = (((1,), (1,)), ((), ()))
    stack = (((0,), (0,)), ((), ()))
    rows_all = grad_ref.shape[0]
    capacity = rows_all // experts
    width = query_ref.shape[1]
    seq_len = key_ref.shape[0] // experts
    scale = HEAD ** (-0.5)
    grad_hold[...] = (
        lax.dot_general(grad_ref[...], weight_ref[...], contract, preferred_element_type=f32)
        .astype(bf16)
        .astype(f32)
    )
    output_out[...] = lax.dot_general(
        mixture_ref[...], grad_ref[...], stack, preferred_element_type=f32
    ).astype(bf16)
    query_hold[...] = query_ref[...].astype(f32)
    blocks = blocks_of(experts, rows_all, key_ref.shape[0], width)
    queries = [query_hold[rows, cut].astype(bf16) for rows, keys, cut in blocks]
    grads = [grad_hold[rows, cut].astype(bf16) for rows, keys, cut in blocks]
    scores = jnp.concatenate(
        [
            lax.dot_general(query, key_ref[keys, cut], contract, preferred_element_type=f32)
            for query, (rows, keys, cut) in zip(queries, blocks)
        ],
        axis=0,
    )
    grad_probs = jnp.concatenate(
        [
            lax.dot_general(grad, value_ref[keys, cut], contract, preferred_element_type=f32)
            for grad, (rows, keys, cut) in zip(grads, blocks)
        ],
        axis=0,
    )
    spots = lax.broadcasted_iota(jnp.int32, (rows_all, seq_len), 1)
    seen = spots <= place_ref[...]
    probs = softmax_all(scores, jnp.concatenate([seen] * (width // HEAD), axis=0))
    inner = jnp.sum(probs * grad_probs, axis=-1, keepdims=True)
    slopes = probs * (grad_probs - inner)
    for number, (rows, keys, cut) in enumerate(blocks):
        own = slice(number * capacity, (number + 1) * capacity)
        slope = slopes[own].astype(bf16)
        value_out[0, keys, cut] = lax.dot_general(
            probs[own].astype(bf16), grads[number], stack, preferred_element_type=f32
        ).astype(bf16)
        key_out[0, keys, cut] = (
            lax.dot_general(slope, queries[number], stack, preferred_element_type=f32) * scale
        ).astype(bf16)
        back_hold[rows, cut] = (
            jnp.dot(slope, key_ref[keys, cut], preferred_element_type=f32) * scale
        )
    for head in range(width // HEAD):
        cut = slice(head * HEAD, (head + 1) * HEAD)
        query_out[:, cut] = turn(back_hold[:, cut], cos_far[...], -sin_far[...]).astype(bf16)


def attend_back(experts, grad_rows, places, far, output_w, query, key, value, mixture):
    rows, depth = grad_rows.shape
    tokens, heads_width = key.shape
    tile = 256
    own_width = heads_width // experts
    steps = own_width // tile

    def full(shape):
        return pl.BlockSpec(shape, lambda step: (0, 0))

    def cut(height):
        return pl.BlockSpec((height, tile), lambda step: (0, step))

    by_heads = pl.BlockSpec((1, tokens, tile), lambda step: (step // steps, 0, step % steps))
    return pl.pallas_call(
        partial(attend_back_kernel, experts),
        grid=(heads_width // tile,),
        out_shape=[
            jax.ShapeDtypeStruct((rows, heads_width), bf16),
            jax.ShapeDtypeStruct((experts, tokens, own_width), bf16),
            jax.ShapeDtypeStruct((experts, tokens, own_width), bf16),
            jax.ShapeDtypeStruct((heads_width, depth), bf16),
        ],
        in_specs=[
            full((rows, depth)),
            full(places.shape),
            full((rows, HEAD)),
            full((rows, HEAD)),
            pl.BlockSpec((tile, depth), lambda step: (step, 0)),
            cut(rows),
            cut(tokens),
            cut(tokens),
            cut(rows),
        ],
        out_specs=[
            cut(rows),
            by_heads,
            by_heads,
            pl.BlockSpec((tile, depth), lambda step: (step, 0)),
        ],
        scratch_shapes=[pltpu.VMEM((rows, tile), f32)] * 3,
        compiler_params=pltpu.CompilerParams(vmem_limit_bytes=48 * 1024 * 1024),
        cost_estimate=pl.CostEstimate(
            flops=4 * rows * depth * heads_width,
            bytes_accessed=4 * depth * heads_width + 8 * tokens * heads_width,
            transcendentals=rows * heads_width,
        ),
        name="attend_back",
    )(grad_rows, places, *far, output_w, query, key, value, mixture)


def halves(ref, block, rows, half):
    size = rows // 2
    return ref.at[pl.ds(pl.multiple_of(block * rows + half * size, size), size)]


def whole(ref, block, rows):
    return ref.at[pl.ds(pl.multiple_of(block * rows, rows), rows)]


def ffn_kernel(
    rows,
    own_ref,
    slope_ref,
    pick_ref,
    router_ref,
    gate_ref,
    up_ref,
    down_ref,
    rows_out,
    hidden_out,
    grad_gate_out,
    grad_up_out,
    out_out,
    grad_out,
    held,
    pulled,
    hidden,
    scaled,
    grad_gate,
    grad_up,
    made,
    grads,
    near,
    far,
    dense,
    dense_far,
    dense_hold,
    far_send,
    far_recv,
    near_send,
    near_recv,
    sum_send,
    sum_recv,
    dense_send,
    dense_recv,
    load_sem,
    save_sem,
):
    group = lax.axis_index("dp")
    mine = lax.axis_index("expert")
    depth = held.shape[1]
    width = hidden.shape[1]
    pair = 2 * rows
    bits = (1, 2, 4)
    peers = {mask: (flips(group, mask, bits), mine) for mask in range(1, 8)}
    barrier([peers[mask] for mask in range(1, 8)])

    def remote(source, target, send, recv, mask):
        return pltpu.make_async_remote_copy(
            src_ref=source,
            dst_ref=target,
            send_sem=send,
            recv_sem=recv,
            device_id=peers[mask],
            device_id_type=MESH,
        )

    def own_half(half):
        size = rows // 2
        return own_ref.at[pl.ds(half * size, size)]

    sends = {}
    for slot, (mask, half) in enumerate(((2, 0), (4, 1), (2, 1), (4, 0))):
        sends[mask, half] = remote(
            own_half(half),
            halves(held, mask, rows, half),
            far_send.at[slot],
            far_recv.at[slot],
            mask,
        )
    sends[6, 0] = remote(
        halves(held, 2, rows, 0), halves(held, 6, rows, 0), far_send.at[4], far_recv.at[4], 4
    )
    sends[6, 1] = remote(
        halves(held, 4, rows, 1), halves(held, 6, rows, 1), far_send.at[5], far_recv.at[5], 2
    )
    across = {}
    for chip in range(4):
        across[chip] = remote(
            own_ref if chip == 0 else whole(held, 2 * chip, rows),
            whole(held, 2 * chip + 1, rows),
            near_send.at[chip],
            near_recv.at[chip],
            1,
        )
    sends[2, 0].start()
    sends[4, 1].start()
    across[0].start()
    sends[2, 1].start()
    sends[4, 0].start()
    seat = pltpu.make_async_copy(own_ref, whole(held, 0, rows), load_sem.at[2])
    seat.start()

    def pull(chip, slot, which):
        block = group_of(2 * chip + which)
        return pltpu.make_async_copy(
            slope_ref.at[block], whole(pulled, 2 * slot + which, rows), load_sem.at[which]
        )

    def group_of(index):
        result = group
        for bit in bits:
            on = (index // bit) % 2
            turned = bit * (1 - 2 * ((group // bit) % 2))
            result = result + on * turned
        return result

    def saves(chip):
        copies = []
        for which in range(2):
            block = group_of(2 * chip + which)
            for number, (source, target) in enumerate(
                (
                    (whole(held, 2 * chip + which, rows), rows_out.at[block]),
                    (whole(scaled, which, rows), hidden_out.at[block]),
                    (whole(grad_gate, which, rows), grad_gate_out.at[block]),
                    (whole(grad_up, which, rows), grad_up_out.at[block]),
                    (whole(made, which, rows), out_out.at[block]),
                )
            ):
                copies.append(
                    pltpu.make_async_copy(source, target, save_sem.at[5 * which + number])
                )
        return copies

    def across_sum(chip):
        return remote(
            whole(grads, 2 * chip + 1, rows),
            whole(near, chip, rows),
            near_send.at[4 + chip],
            near_recv.at[4 + chip],
            1,
        )

    hops = {}
    for slot, (key, block, half, mask) in enumerate(
        (
            ("x2", 2, 0, 2),
            ("x6", 6, 0, 2),
            ("y4", 4, 1, 4),
            ("y6", 6, 1, 4),
            ("then_y", 4, 0, 4),
            ("then_x", 2, 1, 2),
        )
    ):
        size = rows // 2
        hops[key] = remote(
            halves(grads, block, rows, half),
            far.at[pl.ds(slot * size, size)],
            sum_send.at[slot],
            sum_recv.at[slot],
            mask,
        )
    far_slots = {"x2": 0, "x6": 1, "y4": 2, "y6": 3, "then_y": 4, "then_x": 5}

    def dense_hop(mask):
        return remote(
            dense.at[mask],
            dense_far.at[mask],
            dense_send.at[mask],
            dense_recv.at[mask],
            mask,
        )

    def join(chip):
        across_sum(chip).wait_recv()
        block = 2 * chip

        def add(step, carry):
            at = pl.ds(pl.multiple_of(block * rows + step * 48, 16), 48)
            other = pl.ds(pl.multiple_of(chip * rows + step * 48, 16), 48)
            grads[at] = (grads[at].astype(f32) + near[other].astype(f32)).astype(bf16)
            return carry

        lax.fori_loop(0, rows // 48, add, 0)

    def add_far(block, half, key):
        size = rows // 2
        hops[key].wait_recv()

        def add(step, carry):
            at = pl.ds(pl.multiple_of(block * rows + half * size + step * 48, 16), 48)
            other = pl.ds(far_slots[key] * size + pl.multiple_of(step * 48, 16), 48)
            grads[at] = (grads[at].astype(f32) + far[other].astype(f32)).astype(bf16)
            return carry

        lax.fori_loop(0, size // 48, add, 0)

    for which in range(2):
        pull(0, 0, which).start()
    seat.wait()

    def step(chip, carry):
        @pl.when(chip == 0)
        def _():
            across[0].wait_recv()

        @pl.when(chip == 1)
        def _():
            sends[2, 0].wait_recv()
            sends[6, 0].start()
            sends[4, 1].wait_recv()
            sends[6, 1].start()
            sends[2, 1].wait_recv()
            across[1].start()
            sends[4, 0].wait_recv()
            across[2].start()
            across[1].wait_recv()

        @pl.when(chip == 2)
        def _():
            sends[6, 0].wait_recv()
            sends[6, 1].wait_recv()
            across[3].start()
            across[2].wait_recv()

        @pl.when(chip == 3)
        def _():
            across[3].wait_recv()

        slot = chip % 2
        for which in range(2):
            pull(chip, slot, which).wait()

        @pl.when(chip < 3)
        def _():
            for which in range(2):
                pull(chip + 1, 1 - slot, which).start()

        @pl.when(chip > 0)
        def _():
            for copy in saves(chip - 1):
                copy.wait()

        base = pl.multiple_of(chip * pair, pair)
        at = pl.ds(base, pair)
        logits = lax.dot_general(
            held[at], router_ref[...], (((1,), (1,)), ((), ())), preferred_element_type=f32
        )
        apart = []
        for which in range(2):
            block = group_of(2 * chip + which)
            picks = pick_ref[pl.ds(pl.multiple_of(block * rows, rows), rows)]
            apart.append(
                jnp.sum(
                    logits[which * rows : (which + 1) * rows] * picks, axis=-1, keepdims=True
                )
            )
        weight = 1.0 / (1.0 + jnp.exp(jnp.concatenate(apart, axis=0)))
        loads = pl.ds(pl.multiple_of(slot * pair, pair), pair)
        tile = width
        wide = 1024
        partial_dense = jnp.zeros((pair, 128), f32)

        def units(number, total):
            cut = pl.ds(pl.multiple_of(number * tile, tile), tile)
            contract = (((1,), (1,)), ((), ()))
            gate = lax.dot_general(
                held[at], gate_ref[cut], contract, preferred_element_type=f32
            )
            up = lax.dot_general(held[at], up_ref[cut], contract, preferred_element_type=f32)
            sigmoid = 1.0 / (1.0 + jnp.exp(-gate))
            active = gate * sigmoid
            value = (active * up).astype(bf16)
            exact = value.astype(f32)
            plain = pulled[loads, cut]
            hidden[:, cut] = value
            scaled[:, cut] = (weight * exact).astype(bf16)
            inner = weight * plain
            grad_gate[:, cut] = (inner * up * (sigmoid * (1.0 + gate * (1.0 - sigmoid)))).astype(
                bf16
            )
            grad_up[:, cut] = (inner * active).astype(bf16)
            both = exact * plain
            for start in range(0, tile, 128):
                total = total + both[:, start : start + 128]
            return total

        partial_dense = lax.fori_loop(0, width // tile, units, partial_dense)
        ones = jnp.ones((8, 128), f32)
        for which in range(2):
            dense[2 * chip + which] = lax.dot_general(
                ones,
                partial_dense[which * rows : (which + 1) * rows],
                (((1,), (1,)), ((), ())),
                precision=highest,
                preferred_element_type=f32,
            )

        @pl.when(chip == 1)
        def _():
            join(0)

        @pl.when(chip == 2)
        def _():
            join(1)
            hops["x2"].start()

        @pl.when(chip == 3)
        def _():
            join(2)
            hops["y4"].start()

        def columns(number, carry):
            cut = pl.ds(pl.multiple_of(number * wide, wide), wide)
            made[:, cut] = jnp.dot(
                hidden[...], down_ref[:, cut], preferred_element_type=f32
            ).astype(bf16)
            grads[at, cut] = (
                jnp.dot(grad_gate[...], gate_ref[:, cut], preferred_element_type=f32)
                + jnp.dot(grad_up[...], up_ref[:, cut], preferred_element_type=f32)
            ).astype(bf16)
            return carry

        lax.fori_loop(0, depth // wide, columns, 0)
        across_sum(chip).start()
        for copy in saves(chip):
            copy.start()
        return carry

    lax.fori_loop(0, 4, step, 0)
    join(3)
    hops["x6"].start()
    hops["y6"].start()
    for mask in range(1, 8):
        dense_hop(mask).start()
    add_far(0, 0, "x2")
    add_far(0, 1, "y4")
    add_far(4, 0, "x6")
    hops["then_y"].start()
    add_far(2, 1, "y6")
    hops["then_x"].start()
    total = dense[0]
    for mask in range(1, 8):
        dense_hop(mask).wait_recv()
        total = total + dense_far[mask]
    for copy in saves(3):
        copy.wait()
    pick = (lax.broadcasted_iota(jnp.int32, (8, 128), 0) == 0).astype(f32)
    column = lax.dot_general(
        total, pick, (((0,), (0,)), ((), ())), precision=highest, preferred_element_type=f32
    )
    upper = column.astype(bf16)
    lower = (column - upper.astype(f32)).astype(bf16)
    lane = lax.broadcasted_iota(jnp.int32, column.shape, 1)
    dense_hold[...] = jnp.where(lane == 0, upper, jnp.where(lane == 1, lower, 0.0)).astype(bf16)
    add_far(0, 0, "then_y")
    add_far(0, 1, "then_x")
    tail = pltpu.make_async_copy(dense_hold, grad_out.at[:, pl.ds(depth, 128)], load_sem.at[0])
    tail.start()
    last = pltpu.make_async_copy(
        whole(grads, 0, rows), grad_out.at[:, pl.ds(0, depth)], load_sem.at[2]
    )
    last.start()
    for copy in list(sends.values()) + list(across.values()) + list(hops.values()):
        copy.wait_send()
    for chip in range(4):
        across_sum(chip).wait_send()
    for mask in range(1, 8):
        dense_hop(mask).wait_send()
    last.wait()
    tail.wait()


def ffn_call(own, slopes, picks, router, gate, up, down):
    rows, depth = own.shape
    width = gate.shape[0]
    vmem = pl.BlockSpec(memory_space=pltpu.VMEM)
    return pl.pallas_call(
        partial(ffn_kernel, rows),
        out_shape=[
            jax.ShapeDtypeStruct((8, rows, depth), bf16),
            jax.ShapeDtypeStruct((8, rows, width), bf16),
            jax.ShapeDtypeStruct((8, rows, width), bf16),
            jax.ShapeDtypeStruct((8, rows, width), bf16),
            jax.ShapeDtypeStruct((8, rows, depth), bf16),
            jax.ShapeDtypeStruct((rows, depth + 128), bf16),
        ],
        in_specs=[ANY, ANY, vmem, vmem, vmem, vmem, vmem],
        out_specs=[ANY] * 6,
        scratch_shapes=[
            pltpu.VMEM((8 * rows, depth), bf16),
            pltpu.VMEM((4 * rows, width), f32),
            pltpu.VMEM((2 * rows, width), bf16),
            pltpu.VMEM((2 * rows, width), bf16),
            pltpu.VMEM((2 * rows, width), bf16),
            pltpu.VMEM((2 * rows, width), bf16),
            pltpu.VMEM((2 * rows, depth), bf16),
            pltpu.VMEM((8 * rows, depth), bf16),
            pltpu.VMEM((4 * rows, depth), bf16),
            pltpu.VMEM((3 * rows, depth), bf16),
            pltpu.VMEM((8, 8, rows), f32),
            pltpu.VMEM((8, 8, rows), f32),
            pltpu.VMEM((rows, 128), bf16),
            pltpu.SemaphoreType.DMA((6,)),
            pltpu.SemaphoreType.DMA((6,)),
            pltpu.SemaphoreType.DMA((8,)),
            pltpu.SemaphoreType.DMA((8,)),
            pltpu.SemaphoreType.DMA((6,)),
            pltpu.SemaphoreType.DMA((6,)),
            pltpu.SemaphoreType.DMA((8,)),
            pltpu.SemaphoreType.DMA((8,)),
            pltpu.SemaphoreType.DMA((3,)),
            pltpu.SemaphoreType.DMA((10,)),
        ],
        compiler_params=pltpu.CompilerParams(
            collective_id=2, has_side_effects=True, vmem_limit_bytes=61 * 1024 * 1024
        ),
        name="ffn",
    )(own, slopes, picks, router, gate, up, down)


class ChipSums:
    def __init__(self, remote, blocks, near, far, sems, rows):
        self.blocks, self.near, self.far, self.rows = blocks, near, far, rows
        self.remote = remote
        self.near_send, self.near_recv, self.sum_send, self.sum_recv = sems
        self.hops = {}
        size = rows // 2
        for slot, (key, block, half, mask) in enumerate(
            (
                ("x2", 2, 0, 2),
                ("x6", 6, 0, 2),
                ("y4", 4, 1, 4),
                ("y6", 6, 1, 4),
                ("then_y", 4, 0, 4),
                ("then_x", 2, 1, 2),
            )
        ):
            self.hops[key] = (
                remote(
                    halves(blocks, block, rows, half),
                    far.at[pl.ds(slot * size, size)],
                    self.sum_send.at[slot],
                    self.sum_recv.at[slot],
                    mask,
                ),
                slot * size,
            )

    def across(self, chip):
        return self.remote(
            whole(self.blocks, 2 * chip + 1, self.rows),
            whole(self.near, chip, self.rows),
            self.near_send.at[chip],
            self.near_recv.at[chip],
            1,
        )

    def add(self, start, other, other_start, count):
        piece = 48 if count % 48 == 0 else 32

        def one(step, carry):
            at = pl.ds(pl.multiple_of(start + step * piece, 16), piece)
            have = pl.ds(pl.multiple_of(other_start + step * piece, 16), piece)
            self.blocks[at] = (self.blocks[at].astype(f32) + other[have].astype(f32)).astype(bf16)
            return carry

        lax.fori_loop(0, count // piece, one, 0)

    def join(self, chip):
        self.across(chip).wait_recv()
        self.add(2 * chip * self.rows, self.near, chip * self.rows, self.rows)

    def begin(self, key):
        self.hops[key][0].start()

    def settle(self, chip):
        self.join(chip)

        @pl.when(chip == 1)
        def _():
            self.begin("x2")

        @pl.when(chip == 2)
        def _():
            self.begin("y4")

        @pl.when(chip == 3)
        def _():
            self.begin("x6")
            self.begin("y6")

    def add_far(self, block, half, key):
        size = self.rows // 2
        copy, place = self.hops[key]
        copy.wait_recv()
        self.add(block * self.rows + half * size, self.far, place, size)

    def cross(self):
        self.add_far(4, 0, "x6")
        self.begin("then_y")
        self.add_far(2, 1, "y6")
        self.begin("then_x")
        self.add_far(0, 0, "x2")
        self.add_far(0, 1, "y4")

    def close(self):
        self.add_far(0, 0, "then_y")
        self.add_far(0, 1, "then_x")

    def drain(self):
        for copy, place in self.hops.values():
            copy.wait_send()
        for chip in range(4):
            self.across(chip).wait_send()


def turned_pair(index, other, bits):
    result = index
    for bit in bits:
        on = (other // bit) % 2
        result = result + on * bit * (1 - 2 * ((index // bit) % 2))
    return result


def back_kernel(
    grad_ref,
    rows_ref,
    place_ref,
    cos_far,
    sin_far,
    cos_near,
    sin_near,
    weight_ref,
    query_ref,
    key_ref,
    value_ref,
    mixture_ref,
    query_weight,
    back_out,
    key_out,
    value_out,
    output_sum,
    query_sum,
    query_out,
    grad_hold,
    query_hold,
    back_hold,
    weights,
    key_part,
    value_part,
    key_got,
    value_got,
    key_pass,
    value_pass,
    total_hold,
    output_blocks,
    output_near,
    output_far,
    query_blocks,
    query_near,
    query_far,
    output_near_send,
    output_near_recv,
    output_sum_send,
    output_sum_recv,
    query_near_send,
    query_near_recv,
    query_sum_send,
    query_sum_recv,
    got_send,
    got_recv,
    pass_send,
    pass_recv,
    load_sem,
):
    group = lax.axis_index("dp")
    mine = lax.axis_index("expert")
    experts = 4
    side = mine // 2
    edge = ((mine + 1) % experts) // 2 == 0
    bits = (1, 2, 4)
    peers = {mask: (flips(group, mask, bits), mine) for mask in (1, 2, 4)}
    barrier(
        [peers[mask] for mask in (1, 2, 4)]
        + [(group, (mine + step) % experts) for step in range(1, experts)]
    )

    def remote(source, target, send, recv, mask):
        return pltpu.make_async_remote_copy(
            src_ref=source,
            dst_ref=target,
            send_sem=send,
            recv_sem=recv,
            device_id=peers[mask],
            device_id_type=MESH,
        )

    rows_all, depth = grad_ref.shape
    tokens = key_ref.shape[0]
    capacity = rows_all // experts
    seq_len = tokens // experts
    tile = 256
    contract = (((1,), (1,)), ((), ()))
    stack = (((0,), (0,)), ((), ()))
    scale = HEAD ** (-0.5)
    outputs = ChipSums(
        remote,
        output_blocks,
        output_near,
        output_far,
        (output_near_send, output_near_recv, output_sum_send, output_sum_recv),
        tile,
    )
    queries_sum = ChipSums(
        remote,
        query_blocks,
        query_near,
        query_far,
        (query_near_send, query_near_recv, query_sum_send, query_sum_recv),
        tile,
    )

    def owner_of(number):
        return jnp.where(
            number == 0,
            2 - side,
            jnp.where(number == 1, 3 - 3 * side, jnp.where(number == 2, 1 + 4 * side - mine, mine)),
        )

    def chip_of(owner):
        return turned_pair(owner, group // 2, (1, 2))

    def load(step):
        at = pl.multiple_of((2 * owner_of(step // 2) + step % 2) * tile, tile)
        return pltpu.make_async_copy(
            weight_ref.at[pl.ds(at, tile)], weights.at[step % 2], load_sem.at[step % 2]
        )

    def part_at(owner):
        return pl.ds(pl.multiple_of(owner * tokens, tokens), tokens)

    def give(owner):
        return [
            pltpu.make_async_remote_copy(
                src_ref=part.at[part_at(owner)],
                dst_ref=got.at[part_at(mine)],
                send_sem=got_send.at[owner, number],
                recv_sem=got_recv.at[mine, number],
                device_id=(group, owner),
                device_id_type=MESH,
            )
            for number, (part, got) in enumerate(
                ((key_part, key_got), (value_part, value_got))
            )
        ]

    def got_from(source):
        return [
            pltpu.make_async_remote_copy(
                src_ref=part.at[part_at(source)],
                dst_ref=got.at[part_at(source)],
                send_sem=got_send.at[source, number],
                recv_sem=got_recv.at[source, number],
                device_id=(group, source),
                device_id_type=MESH,
            )
            for number, (part, got) in enumerate(
                ((key_part, key_got), (value_part, value_got))
            )
        ]

    def hand_on(target):
        return [
            pltpu.make_async_remote_copy(
                src_ref=part.at[part_at(2 - side)],
                dst_ref=pile,
                send_sem=pass_send.at[number],
                recv_sem=pass_recv.at[number],
                device_id=(group, target),
                device_id_type=MESH,
            )
            for number, (part, pile) in enumerate(
                ((key_part, key_pass), (value_part, value_pass))
            )
        ]

    load(0).start()
    block_slices = blocks_of(experts, rows_all, tokens, tile)
    spots = lax.broadcasted_iota(jnp.int32, (rows_all, seq_len), 1)

    def one(step, carry):
        owner = owner_of(step // 2)
        parity = step % 2
        number = 2 * owner + parity
        chip = chip_of(owner)
        load(step).wait()

        @pl.when(step < 7)
        def _():
            load(step + 1).start()

        columns = pl.ds(pl.multiple_of(number * tile, tile), tile)
        block = turned_pair(number, group, bits)
        block_at = pl.ds(pl.multiple_of(block * tile, tile), tile)
        grad_hold[...] = (
            lax.dot_general(
                grad_ref[...], weights[parity], contract, preferred_element_type=f32
            )
            .astype(bf16)
            .astype(f32)
        )
        output_blocks[block_at] = lax.dot_general(
            mixture_ref[:, columns], grad_ref[...], stack, preferred_element_type=f32
        ).astype(bf16)

        @pl.when((parity == 1) & (step > 1))
        def _():
            outputs.settle(chip_of(owner_of(step // 2 - 1)))

        query_hold[...] = query_ref[:, columns].astype(f32)
        keys_tile = key_ref[:, columns]
        values_tile = value_ref[:, columns]
        queries = [query_hold[rows, cut].astype(bf16) for rows, keys, cut in block_slices]
        grads = [grad_hold[rows, cut].astype(bf16) for rows, keys, cut in block_slices]
        scores = jnp.concatenate(
            [
                lax.dot_general(query, keys_tile[keys, cut], contract, preferred_element_type=f32)
                for query, (rows, keys, cut) in zip(queries, block_slices)
            ],
            axis=0,
        )
        grad_probs = jnp.concatenate(
            [
                lax.dot_general(grad, values_tile[keys, cut], contract, preferred_element_type=f32)
                for grad, (rows, keys, cut) in zip(grads, block_slices)
            ],
            axis=0,
        )
        seen = spots <= place_ref[...]
        probs = softmax_all(scores, jnp.concatenate([seen] * (tile // HEAD), axis=0))
        inner = jnp.sum(probs * grad_probs, axis=-1, keepdims=True)
        slopes = probs * (grad_probs - inner)
        for count, (rows, keys, cut) in enumerate(block_slices):
            own = slice(count * capacity, (count + 1) * capacity)
            slope = slopes[own].astype(bf16)
            token_at = pl.ds(
                pl.multiple_of(owner * tokens + keys.start, seq_len), seq_len
            )
            lanes = pl.ds(pl.multiple_of(parity * tile + cut.start, HEAD), HEAD)
            value_part[token_at, lanes] = lax.dot_general(
                probs[own].astype(bf16), grads[count], stack, preferred_element_type=f32
            ).astype(bf16)
            key_part[token_at, lanes] = (
                lax.dot_general(slope, queries[count], stack, preferred_element_type=f32) * scale
            ).astype(bf16)
            back_hold[rows, cut] = (
                jnp.dot(slope, keys_tile[keys, cut], preferred_element_type=f32) * scale
            )
        for head in range(tile // HEAD):
            cut = slice(head * HEAD, (head + 1) * HEAD)
            lanes = pl.ds(pl.multiple_of(number * tile + head * HEAD, HEAD), HEAD)
            query_out[:, lanes] = turn(back_hold[:, cut], cos_far[...], -sin_far[...]).astype(bf16)

        @pl.when(parity == 1)
        def _():
            outputs.across(chip).start()

            @pl.when(step == 1)
            def _():
                @pl.when(edge)
                def _():
                    for copy in hand_on(1 + side):
                        copy.start()

            @pl.when((step == 3) | (step == 5))
            def _():
                for copy in give(owner):
                    copy.start()

        return carry

    lax.fori_loop(0, 8, one, 0)

    def project(block, carry):
        number = turned_pair(block, group, bits)
        columns = pl.ds(pl.multiple_of(number * tile, tile), tile)
        block_at = pl.ds(pl.multiple_of(block * tile, tile), tile)
        query_blocks[block_at] = lax.dot_general(
            rows_ref[:, columns], query_out[...], stack, preferred_element_type=f32
        ).astype(bf16)

        @pl.when(block % 2 == 1)
        def _():
            queries_sum.across(block // 2).start()

        return carry

    lax.fori_loop(0, 8, project, 0)
    outputs.settle(chip_of(mine))

    def stream(step):
        at = pl.multiple_of(step * tile, tile)
        return pltpu.make_async_copy(
            query_weight.at[pl.ds(at, tile)], weights.at[step % 2], load_sem.at[step % 2]
        )

    stream(0).start()

    def rows_back(step, carry):
        stream(step).wait()

        @pl.when(step < depth // tile - 1)
        def _():
            stream(step + 1).start()

        cut = pl.ds(pl.multiple_of(step * tile, tile), tile)
        back_out[:, cut] = lax.dot_general(
            query_out[...], weights[step % 2], contract, preferred_element_type=f32
        ).astype(bf16)
        return carry

    lax.fori_loop(0, depth // tile, rows_back, 0)
    piece = 32

    @pl.when(jnp.logical_not(edge))
    def _():
        for (part, pile), copy in zip(
            ((key_part, key_pass), (value_part, value_pass)), hand_on(1 + side)
        ):
            copy.wait_recv()

            def add(step, carry):
                at = pl.ds(pl.multiple_of((2 - side) * tokens + step * piece, piece), piece)
                other = pl.ds(pl.multiple_of(step * piece, piece), piece)
                part[at] = (part[at].astype(f32) + pile[other].astype(f32)).astype(bf16)
                return carry

            lax.fori_loop(0, tokens // piece, add, 0)
        for copy in give(2 - side):
            copy.start()

    for chip in range(4):
        queries_sum.settle(chip)
    outputs.cross()
    outputs.close()
    result = pltpu.make_async_copy(whole(output_blocks, 0, tile), output_sum, load_sem.at[0])
    result.start()
    queries_sum.cross()
    queries_sum.close()
    second = pltpu.make_async_copy(whole(query_blocks, 0, tile), query_sum, load_sem.at[1])
    second.start()

    def expected(source):
        far_end = (mine + 2) % experts
        middle = ((mine + 1) % experts) // 2 == 1
        return jnp.logical_not(middle & (source == far_end))

    def gather(number, part, got):
        def first(step, carry):
            at = pl.ds(pl.multiple_of(mine * tokens + step * piece, piece), piece)
            where = pl.ds(pl.multiple_of(step * piece, piece), piece)
            total_hold[where] = part[at].astype(f32)
            return carry

        lax.fori_loop(0, tokens // piece, first, 0)
        for hop in range(1, experts):
            source = (mine + hop) % experts

            @pl.when(expected(source))
            def _():
                got_from(source)[number].wait_recv()

                def add(step, carry):
                    at = pl.ds(pl.multiple_of(source * tokens + step * piece, piece), piece)
                    where = pl.ds(pl.multiple_of(step * piece, piece), piece)
                    total_hold[where] = total_hold[where] + got[at].astype(f32)
                    return carry

                lax.fori_loop(0, tokens // piece, add, 0)

    gather(1, value_part, value_got)
    value_out[...] = total_hold[...].astype(bf16)
    gather(0, key_part, key_got)
    for head in range(key_out.shape[1] // HEAD):
        cut = slice(head * HEAD, (head + 1) * HEAD)
        key_out[:, cut] = turn(total_hold[:, cut], cos_near[...], -sin_near[...]).astype(bf16)

    @pl.when(edge)
    def _():
        for copy in hand_on(1 + side):
            copy.wait_send()

    @pl.when(jnp.logical_not(edge))
    def _():
        for copy in give(2 - side):
            copy.wait_send()

    for number in (1, 2):
        for copy in give(owner_of(number)):
            copy.wait_send()
    outputs.drain()
    queries_sum.drain()
    result.wait()
    second.wait()


def back_call(
    grad_rows, rows_flat, places, far, near, output_w, query, key, value, mixture, query_w
):
    rows, depth = grad_rows.shape
    tokens, heads_width = key.shape
    own = heads_width // 4
    tile = 256
    vmem = pl.BlockSpec(memory_space=pltpu.VMEM)

    def dma(*shape):
        return pltpu.SemaphoreType.DMA(shape)

    def blocks(count):
        return pltpu.VMEM((count * tile, depth), bf16)

    return pl.pallas_call(
        back_kernel,
        out_shape=[
            jax.ShapeDtypeStruct((rows, depth), bf16),
            jax.ShapeDtypeStruct((tokens, own), bf16),
            jax.ShapeDtypeStruct((tokens, own), bf16),
            jax.ShapeDtypeStruct((tile, depth), bf16),
            jax.ShapeDtypeStruct((tile, depth), bf16),
        ],
        in_specs=[vmem] * 7 + [ANY] + [vmem] * 4 + [ANY],
        out_specs=[vmem] * 3 + [ANY] * 2,
        scratch_shapes=[
            pltpu.VMEM((rows, heads_width), bf16),
            pltpu.VMEM((rows, tile), f32),
            pltpu.VMEM((rows, tile), f32),
            pltpu.VMEM((rows, tile), f32),
            pltpu.VMEM((2, tile, depth), bf16),
            pltpu.VMEM((4 * tokens, own), bf16),
            pltpu.VMEM((4 * tokens, own), bf16),
            pltpu.VMEM((4 * tokens, own), bf16),
            pltpu.VMEM((4 * tokens, own), bf16),
            pltpu.VMEM((tokens, own), bf16),
            pltpu.VMEM((tokens, own), bf16),
            pltpu.VMEM((tokens, own), f32),
            blocks(8),
            blocks(4),
            blocks(3),
            blocks(8),
            blocks(4),
            blocks(3),
            dma(4),
            dma(4),
            dma(6),
            dma(6),
            dma(4),
            dma(4),
            dma(6),
            dma(6),
            dma(4, 2),
            dma(4, 2),
            dma(2),
            dma(2),
            dma(2),
        ],
        compiler_params=pltpu.CompilerParams(
            collective_id=3, has_side_effects=True, vmem_limit_bytes=61 * 1024 * 1024
        ),
        cost_estimate=pl.CostEstimate(
            flops=60_000_000_000, bytes_accessed=200_000_000, transcendentals=0
        ),
        name="attend_back_sums",
    )(
        grad_rows,
        rows_flat,
        places,
        *far,
        *near,
        output_w,
        query,
        key,
        value,
        mixture,
        query_w,
    )


def start_kernel(
    home,
    attn_gain,
    moe_gain,
    attn_router,
    moe_router,
    attn_choice,
    moe_choice,
    lengths,
    cos_home,
    sin_home,
    given,
    value_shard,
    key_shard,
    query_shard,
    output_shard,
    small_full,
    told_full,
    table_out,
    place_out,
    cos_far,
    sin_far,
    attn_table,
    moe_table,
    normed_out,
    rows_out,
    query_out,
    key_out,
    value_out,
    mixture_out,
    branch_out,
    value_own,
    key_own,
    query_full,
    output_full,
    given_out,
    inputs,
    small_own,
    told_own,
    small_hold,
    normed,
    rows_hold,
    query_hold,
    query_low,
    keys,
    values,
    chances,
    mixture,
    branch,
    given_hold,
    value_stage,
    key_stage,
    query_stage,
    output_stage,
    value_buf,
    key_buf,
    query_buf,
    output_buf,
    load_sem,
    far_send,
    far_recv,
    near_send,
    near_recv,
    home_send,
    home_recv,
    small_send,
    small_recv,
    told_send,
    told_recv,
    heads_send,
    heads_recv,
    given_send,
    given_recv,
    save_sem,
):
    group = lax.axis_index("dp")
    mine = lax.axis_index("expert")
    experts = 4
    bits = (1, 2, 4)
    peers = {mask: (flips(group, mask, bits), mine) for mask in range(1, 8)}
    others = [(mine + hop) % experts for hop in range(1, experts)]
    seq_len, depth = home.shape
    expert_rows = rows_out.shape[0]
    capacity = expert_rows // experts
    tokens = experts * seq_len
    extent = key_shard.shape[0]
    half_extent = extent // 2
    own_width = value_buf.shape[1]
    heads_width = key_buf.shape[1]
    tile = 256
    shards = (value_shard, key_shard, query_shard, output_shard)
    stages = (value_stage, key_stage, query_stage, output_stage)
    buffers = (value_buf, key_buf, query_buf, output_buf)
    loads = []
    for which in range(4):
        source = shards[which]
        if which == 0:
            source = source.at[:, pl.ds(pl.multiple_of(mine * own_width, own_width), own_width)]
        loads.append(pltpu.make_async_copy(source, stages[which], load_sem.at[which]))
    seat = pltpu.make_async_copy(home, inputs.at[mine], load_sem.at[4])
    for copy in loads:
        copy.start()
    seat.start()

    small_hold[...] = jnp.zeros_like(small_hold)
    small_hold[0:1] = attn_gain[...]
    small_hold[1:2] = moe_gain[...]
    small_hold[2 : 2 + experts] = attn_router[...]
    small_hold[2 + experts : 2 + 2 * experts] = moe_router[...]
    small_own[...] = small_hold[...].astype(bf16)
    lane = lax.broadcasted_iota(jnp.int32, (experts, seq_len), 1)
    live = lane < lengths[...]
    told_own[0:experts] = jnp.where(live, moe_choice[0], -1).astype(f32)
    told_own[experts : 2 * experts] = jnp.where(live, moe_choice[1], -1).astype(f32)
    barrier([peers[mask] for mask in range(1, 8)] + [(group, other) for other in others])

    def remote(source, target, send, recv, device):
        return pltpu.make_async_remote_copy(
            src_ref=source,
            dst_ref=target,
            send_sem=send,
            recv_sem=recv,
            device_id=device,
            device_id_type=MESH,
        )

    small_at = pl.ds(pl.multiple_of(group * extent, extent), extent)
    told_at = pl.ds(pl.multiple_of(group * 2 * experts, 2 * experts), 2 * experts)
    smalls = []
    for mask in range(1, 8):
        smalls.append(
            remote(
                small_own,
                small_full.at[:, small_at],
                small_send.at[mask],
                small_recv.at[mask],
                peers[mask],
            )
        )
        smalls.append(
            remote(
                told_own,
                told_full.at[told_at],
                told_send.at[mask],
                told_recv.at[mask],
                peers[mask],
            )
        )
    homes = [
        remote(home, inputs.at[mine], home_send.at[hop], home_recv.at[hop], (group, other))
        for hop, other in enumerate(others)
    ]
    for copy in smalls + homes:
        copy.start()
    small_full[:, small_at] = small_own[...]
    told_full[told_at] = told_own[...]

    def piece(which, mask, half):
        start = flips(group, mask, bits) * extent + half * half_extent
        return buffers[which].at[pl.ds(pl.multiple_of(start, half_extent), half_extent)]

    def block(which, mask):
        start = flips(group, mask, bits) * extent
        return buffers[which].at[pl.ds(pl.multiple_of(start, extent), extent)]

    far = {}
    near = {}
    for which in range(4):
        for slot, (mask, half, towards) in enumerate(
            ((0, 0, 2), (0, 1, 2), (0, 1, 4), (0, 0, 4), (2, 0, 4), (4, 1, 2))
        ):
            far[which, slot] = remote(
                piece(which, mask, half),
                piece(which, mask, half),
                far_send.at[which, slot],
                far_recv.at[which, slot],
                peers[towards],
            )
        for chip in range(4):
            near[which, chip] = remote(
                block(which, 2 * chip),
                block(which, 2 * chip),
                near_send.at[which, chip],
                near_recv.at[which, chip],
                peers[1],
            )

    def convert(which):
        loads[which].wait()
        count = 32

        def one(step, carry):
            at = pl.ds(pl.multiple_of(step * count, count), count)
            to = pl.ds(pl.multiple_of(group * extent + step * count, count), count)
            buffers[which][to] = stages[which][at].astype(bf16)
            return carry

        lax.fori_loop(0, extent // count, one, 0)

    def leave(which):
        for slot in (0, 2, 1, 3):
            far[which, slot].start()
        near[which, 0].start()

    def pass_on(which):
        far[which, 0].wait_recv()
        far[which, 4].start()
        far[which, 2].wait_recv()
        far[which, 5].start()

    def spread(which):
        far[which, 1].wait_recv()
        near[which, 1].start()
        far[which, 3].wait_recv()
        near[which, 2].start()
        far[which, 4].wait_recv()
        far[which, 5].wait_recv()
        near[which, 3].start()

    def complete(which):
        for chip in range(4):
            near[which, chip].wait_recv()

    convert(0)
    leave(0)
    convert(1)
    leave(1)

    chosen = ((attn_choice[0] == mine) | (attn_choice[1] == mine)) & live
    picked = chosen.astype(f32)
    early = lax.broadcasted_iota(jnp.int32, (seq_len, seq_len), 0)
    late = lax.broadcasted_iota(jnp.int32, (seq_len, seq_len), 1)
    until = (early <= late).astype(f32)
    seats = lax.broadcasted_iota(jnp.int32, (capacity, seq_len), 0).astype(f32) + 1.0
    spot = lax.broadcasted_iota(jnp.int32, (capacity, seq_len), 1).astype(f32)

    def seated(taken):
        slot_of = jnp.dot(taken, until, preferred_element_type=f32)
        return [
            ((slot_of[row : row + 1] == seats) & (taken[row : row + 1] > 0.0)).astype(f32)
            for row in range(experts)
        ]

    tables = seated(picked)
    row_of = lax.broadcasted_iota(jnp.int32, (experts, seq_len), 0)

    def own_row(value):
        return jnp.sum(jnp.where(row_of == mine, value, 0), axis=0, keepdims=True)

    own_live = lane < own_row(jnp.broadcast_to(lengths[...], (experts, seq_len)))
    for choice, table_ref in ((attn_choice, attn_table), (moe_choice, moe_table)):
        goes = ((own_row(choice[0]) == row_of) | (own_row(choice[1]) == row_of)) & own_live
        table_ref[...] = jnp.concatenate(seated(goes.astype(f32)), axis=0).astype(bf16)
    for other in range(experts):
        given_hold[other] = jnp.dot(
            moe_table[other * capacity : (other + 1) * capacity],
            given[...],
            preferred_element_type=f32,
        ).astype(bf16)
    empty = jnp.zeros((capacity, seq_len), f32)
    table_out[...] = jnp.concatenate(
        [
            jnp.concatenate(
                [tables[seq] if seq == other else empty for other in range(experts)], axis=1
            )
            for seq in range(experts)
        ],
        axis=0,
    ).astype(bf16)
    place_out[...] = jnp.concatenate(
        [jnp.sum(table * spot, axis=1, keepdims=True) for table in tables], axis=0
    ).astype(jnp.int32)
    stacked = jnp.concatenate(tables, axis=0)
    vacant = 1.0 - jnp.sum(stacked, axis=1, keepdims=True)
    cos_far[...] = vacant + jnp.dot(
        stacked, cos_home[...], precision=highest, preferred_element_type=f32
    )
    sin_far[...] = jnp.dot(stacked, sin_home[...], precision=highest, preferred_element_type=f32)

    pass_on(0)
    convert(2)
    pass_on(1)
    leave(2)
    convert(3)
    spread(0)
    complete(0)
    spread(1)

    seat.wait()
    for copy in smalls:
        copy.wait_recv()
    gain = small_full[0:1].astype(f32)
    for hop in range(experts):
        source = (mine + experts - hop) % experts
        if hop > 0:
            homes[hop - 1].wait_recv()
        count = 32

        def one(step, carry):
            at = pl.ds(pl.multiple_of(step * count, count), count)
            to = pl.ds(pl.multiple_of(source * seq_len + step * count, count), count)
            value = inputs[source, at].astype(f32)
            normed[to] = (value * norm_scale(value) * gain).astype(bf16)
            return carry

        lax.fori_loop(0, seq_len // count, one, 0)
    own_at = pl.ds(pl.multiple_of(mine * own_width, own_width), own_width)
    values[:, own_at] = jnp.dot(
        normed[...], value_buf[...], preferred_element_type=f32
    ).astype(bf16)
    heads = [
        remote(
            values.at[:, own_at],
            values.at[:, own_at],
            heads_send.at[hop],
            heads_recv.at[hop],
            (group, other),
        )
        for hop, other in enumerate(others)
    ]
    for copy in heads:
        copy.start()
    rows_hold[...] = jnp.dot(table_out[...], normed[...], preferred_element_type=f32).astype(bf16)
    saves = [
        pltpu.make_async_copy(normed, normed_out, save_sem.at[0]),
        pltpu.make_async_copy(rows_hold, rows_out, save_sem.at[1]),
        pltpu.make_async_copy(value_buf, value_own, save_sem.at[2]),
    ]
    for copy in saves:
        copy.start()

    def save(source, target, number):
        copy = pltpu.make_async_copy(source, target, save_sem.at[number])
        copy.start()
        saves.append(copy)

    complete(1)
    save(key_buf.at[:, own_at], key_own, 3)

    def make_keys(step, carry):
        cut = pl.ds(pl.multiple_of(step * tile, tile), tile)
        made = jnp.dot(normed[...], key_buf[:, cut], preferred_element_type=f32)
        for head in range(tile // HEAD):
            lanes = pl.ds(pl.multiple_of(step * tile + head * HEAD, HEAD), HEAD)
            part = made[:, head * HEAD : (head + 1) * HEAD]
            for seq in range(experts):
                rows = slice(seq * seq_len, (seq + 1) * seq_len)
                keys[rows, lanes] = turn(part[rows], cos_home[...], sin_home[...]).astype(bf16)
        return carry

    lax.fori_loop(0, heads_width // tile, make_keys, 0)
    save(keys, key_out, 4)
    pass_on(2)
    leave(3)
    spread(2)
    complete(2)
    save(query_buf, query_full, 5)

    blocks = blocks_of(experts, expert_rows, tokens, tile)
    contract = (((1,), (1,)), ((), ()))
    spots = lax.broadcasted_iota(jnp.int32, (expert_rows, seq_len), 1)
    span_rows = len(blocks) * capacity

    def make_chances(step, carry):
        cut = pl.ds(pl.multiple_of(step * tile, tile), tile)
        made = jnp.dot(rows_hold[...], query_buf[:, cut], preferred_element_type=f32)
        for head in range(tile // HEAD):
            part = slice(head * HEAD, (head + 1) * HEAD)
            query_hold[:, part] = turn(made[:, part], cos_far[...], sin_far[...])
        query_low[:, cut] = query_hold[...].astype(bf16)
        tile_keys = keys[:, cut]
        scores = jnp.concatenate(
            [
                lax.dot_general(
                    query_hold[rows, lanes].astype(bf16),
                    tile_keys[spans, lanes],
                    contract,
                    preferred_element_type=f32,
                )
                for rows, spans, lanes in blocks
            ],
            axis=0,
        )
        seen = spots <= place_out[...]
        probs = softmax_all(scores, jnp.concatenate([seen] * (tile // HEAD), axis=0))
        chances[pl.ds(pl.multiple_of(step * span_rows, 64), span_rows)] = probs.astype(bf16)
        return carry

    lax.fori_loop(0, heads_width // tile, make_chances, 0)
    save(query_low, query_out, 6)
    pass_on(3)
    for copy in heads:
        copy.wait_recv()
    givens = [
        remote(
            given_hold.at[other],
            given_out.at[mine],
            given_send.at[hop],
            given_recv.at[hop],
            (group, other),
        )
        for hop, other in enumerate(others)
    ]
    for copy in givens:
        copy.start()
    save(given_hold.at[mine], given_out.at[mine], 11)
    save(values, value_out, 7)

    def mix(step, carry):
        cut = pl.ds(pl.multiple_of(step * tile, tile), tile)
        tile_values = values[:, cut]
        probs = chances[pl.ds(pl.multiple_of(step * span_rows, 64), span_rows)].astype(f32)
        for count, (rows, spans, lanes) in enumerate(blocks):
            query_hold[rows, lanes] = jnp.dot(
                probs[count * capacity : (count + 1) * capacity].astype(bf16),
                tile_values[spans, lanes],
                preferred_element_type=f32,
            )
        mixture[:, cut] = query_hold[...].astype(bf16)
        return carry

    lax.fori_loop(0, heads_width // tile, mix, 0)
    save(mixture, mixture_out, 8)
    spread(3)
    complete(3)
    save(output_buf, output_full, 9)

    def project(step, carry):
        cut = pl.ds(pl.multiple_of(step * tile, tile), tile)
        branch[:, cut] = jnp.dot(
            mixture[...], output_buf[:, cut], preferred_element_type=f32
        ).astype(bf16)
        return carry

    lax.fori_loop(0, depth // tile, project, 0)
    save(branch, branch_out, 10)
    for copy in givens:
        copy.wait_recv()
    for copy in smalls + homes + heads + givens + list(far.values()) + list(near.values()):
        copy.wait_send()
    for copy in saves:
        copy.wait()


def start_call(
    home,
    attn_gain,
    moe_gain,
    attn_router,
    moe_router,
    attn_choice,
    moe_choice,
    lengths,
    near,
    given,
    value_weight,
    key_weight,
    query_weight,
    output_weight,
):
    experts = 4
    groups = 8
    seq_len, depth = home.shape
    extent, heads_width = key_weight.shape
    capacity = 2 * seq_len // experts + 8
    rows = experts * capacity
    tokens = experts * seq_len
    own_width = heads_width // experts
    small_room = -(-(2 + 2 * experts) // 16) * 16
    vmem = pl.BlockSpec(memory_space=pltpu.VMEM)

    def shaped(*shape, kind=bf16):
        return jax.ShapeDtypeStruct(shape, kind)

    def dma(*shape):
        return pltpu.SemaphoreType.DMA(shape)

    return pl.pallas_call(
        start_kernel,
        out_shape=[
            shaped(small_room, depth),
            shaped(groups * 2 * experts, seq_len, kind=f32),
            shaped(rows, tokens),
            shaped(rows, 1, kind=jnp.int32),
            shaped(rows, HEAD, kind=f32),
            shaped(rows, HEAD, kind=f32),
            shaped(rows, seq_len),
            shaped(rows, seq_len),
            shaped(tokens, depth),
            shaped(rows, depth),
            shaped(rows, heads_width),
            shaped(tokens, heads_width),
            shaped(tokens, heads_width),
            shaped(rows, heads_width),
            shaped(rows, depth),
            shaped(depth, own_width),
            shaped(depth, own_width),
            shaped(depth, heads_width),
            shaped(heads_width, depth),
            shaped(experts, capacity, depth),
        ],
        in_specs=[ANY] + [vmem] * 10 + [ANY] * 4,
        out_specs=[vmem] * 8 + [ANY] * 12,
        scratch_shapes=[
            pltpu.VMEM((experts, seq_len, depth), bf16),
            pltpu.VMEM((small_room, extent), bf16),
            pltpu.VMEM((2 * experts, seq_len), f32),
            pltpu.VMEM((small_room, extent), f32),
            pltpu.VMEM((tokens, depth), bf16),
            pltpu.VMEM((rows, depth), bf16),
            pltpu.VMEM((rows, 256), f32),
            pltpu.VMEM((rows, heads_width), bf16),
            pltpu.VMEM((tokens, heads_width), bf16),
            pltpu.VMEM((tokens, heads_width), bf16),
            pltpu.VMEM((rows * heads_width // HEAD, seq_len), bf16),
            pltpu.VMEM((rows, heads_width), bf16),
            pltpu.VMEM((rows, depth), bf16),
            pltpu.VMEM((experts, capacity, depth), bf16),
            pltpu.VMEM((extent, own_width), f32),
            pltpu.VMEM((extent, heads_width), f32),
            pltpu.VMEM((extent, heads_width), f32),
            pltpu.VMEM((extent, depth), f32),
            pltpu.VMEM((depth, own_width), bf16),
            pltpu.VMEM((depth, heads_width), bf16),
            pltpu.VMEM((depth, heads_width), bf16),
            pltpu.VMEM((heads_width, depth), bf16),
            dma(5),
            dma(4, 6),
            dma(4, 6),
            dma(4, 4),
            dma(4, 4),
            dma(3),
            dma(3),
            dma(8),
            dma(8),
            dma(8),
            dma(8),
            dma(3),
            dma(3),
            dma(3),
            dma(3),
            dma(12),
        ],
        compiler_params=pltpu.CompilerParams(
            collective_id=4, has_side_effects=True, vmem_limit_bytes=61 * 1024 * 1024
        ),
        cost_estimate=pl.CostEstimate(
            flops=100_000_000_000, bytes_accessed=300_000_000, transcendentals=0
        ),
        name="attend_start",
    )(
        home,
        attn_gain,
        moe_gain,
        attn_router,
        moe_router,
        attn_choice,
        moe_choice,
        lengths,
        *near,
        given,
        value_weight,
        key_weight,
        query_weight,
        output_weight,
    )


def start_plain(
    home,
    attn_gain,
    moe_gain,
    attn_router,
    moe_router,
    attn_choice,
    moe_choice,
    lengths,
    near,
    given,
    value_weight,
    key_weight,
    query_weight,
    output_weight,
):
    experts = lax.axis_size("expert")
    mine = lax.axis_index("expert")
    seq_len, depth = home.shape
    heads_width = key_weight.shape[1]
    own_width = heads_width // experts
    capacity = 2 * seq_len // experts + 8
    rows = experts * capacity
    kinds = 2 + 2 * experts
    small_own = jnp.concatenate(
        [
            attn_gain,
            moe_gain,
            attn_router,
            moe_router,
            jnp.zeros((-kinds % 16, attn_gain.shape[1]), f32),
        ]
    ).astype(bf16)
    places = jnp.arange(seq_len, dtype=jnp.int32)
    live = places[None] < lengths
    told = jnp.where(live, moe_choice, -1).astype(f32).reshape(2 * experts, seq_len)
    key_full, value_full, query_full, output_full, small_full, told_full, inputs = gather_all(
        [
            key_weight.astype(bf16),
            value_weight.astype(bf16),
            query_weight.astype(bf16),
            output_weight.astype(bf16),
            small_own,
            told,
        ],
        (2, 2, 2, 2, 1, 1),
        (0, 0, 0, 0, 1, 0),
        home,
    )

    def tables_of(choice):
        return jax.vmap(partial(route_table, experts=experts, capacity=capacity))(
            choice.transpose(1, 2, 0), lengths[:, 0]
        )

    attn_all, moe_all = tables_of(attn_choice), tables_of(moe_choice)
    group_table = lax.dynamic_index_in_dim(attn_all, mine, 1, keepdims=False)
    own_attn = lax.dynamic_index_in_dim(attn_all, mine, 0, keepdims=False).astype(bf16)
    own_moe = lax.dynamic_index_in_dim(moe_all, mine, 0, keepdims=False).astype(bf16)
    row_places = jnp.sum(jnp.where(group_table, places, 0), axis=-1).reshape(rows, 1)
    same = jnp.eye(experts, dtype=bool)[:, None, :, None]
    table = (group_table[:, :, None, :] & same).astype(bf16).reshape(rows, experts * seq_len)
    far = signed_tables(row_places[:, 0])
    all_near = tuple(jnp.tile(part, (experts, 1)) for part in near)
    normed, rows_flat, queries, keys, values, mixture = attend(
        experts,
        inputs.reshape(experts * seq_len, depth),
        small_full,
        table,
        row_places,
        far,
        all_near,
        query_full,
        key_full,
        value_full,
    )
    branch = jnp.dot(mixture, output_full, preferred_element_type=f32).astype(bf16)
    given_rows = jnp.einsum("ect,td->ecd", own_moe, given, preferred_element_type=f32)

    def own_heads(weight):
        return lax.dynamic_slice_in_dim(weight, mine * own_width, own_width, 1)

    return (
        small_full,
        told_full,
        table,
        row_places,
        *far,
        own_attn.reshape(rows, seq_len),
        own_moe.reshape(rows, seq_len),
        normed,
        rows_flat,
        queries,
        keys,
        values,
        mixture,
        branch,
        own_heads(value_full),
        own_heads(key_full),
        query_full,
        output_full,
        exchange(given_rows.astype(bf16)),
    )


def last_kernel(
    rows_back,
    table_ref,
    key_own,
    value_own,
    grad_keys,
    grad_values,
    normed_ref,
    home_out,
    key_out,
    value_out,
    part,
    got,
    pile,
    blocks,
    near,
    far,
    swapped,
    near_send,
    near_recv,
    sum_send,
    sum_recv,
    got_send,
    got_recv,
    pass_send,
    pass_recv,
    swap_send,
    swap_recv,
):
    group = lax.axis_index("dp")
    mine = lax.axis_index("expert")
    experts = 4
    side = mine // 2
    edge = ((mine + 1) % experts) // 2 == 0
    bits = (1, 2, 4)
    peers = {mask: (flips(group, mask, bits), mine) for mask in (1, 2, 4)}
    others = [(mine + hop) % experts for hop in range(1, experts)]
    barrier([peers[mask] for mask in (1, 2, 4)] + [(group, other) for other in others])

    def send_to(device, source, target, send, recv):
        return pltpu.make_async_remote_copy(
            src_ref=source,
            dst_ref=target,
            send_sem=send,
            recv_sem=recv,
            device_id=device,
            device_id_type=MESH,
        )

    def remote(source, target, send, recv, mask):
        return send_to(peers[mask], source, target, send, recv)

    seq_len, depth = home_out.shape
    own_width = grad_keys.shape[1]
    tile = depth // 8
    contract = (((1,), (1,)), ((), ()))
    stack = (((0,), (0,)), ((), ()))
    sums = ChipSums(
        remote, blocks, near, far, (near_send, near_recv, sum_send, sum_recv), tile
    )

    def owner_of(number):
        return jnp.where(
            number == 0,
            2 - side,
            jnp.where(number == 1, 3 - 3 * side, jnp.where(number == 2, 1 + 4 * side - mine, mine)),
        )

    def give(owner):
        return send_to(
            (group, owner), part.at[owner], got.at[mine], got_send.at[owner], got_recv.at[mine]
        )

    def got_from(source):
        return send_to(
            (group, source),
            part.at[source],
            got.at[source],
            got_send.at[source],
            got_recv.at[source],
        )

    hand_on = send_to(
        (group, 1 + side), part.at[2 - side], pile, pass_send.at[0], pass_recv.at[0]
    )

    def one(step, carry):
        owner = owner_of(step)
        at = pl.ds(pl.multiple_of(owner * seq_len, seq_len), seq_len)
        part[owner] = (
            lax.dot_general(
                table_ref[:, at], rows_back[...], stack, preferred_element_type=f32
            )
            + lax.dot_general(
                grad_keys[at], key_own[...], contract, preferred_element_type=f32
            )
            + lax.dot_general(
                grad_values[at], value_own[...], contract, preferred_element_type=f32
            )
        ).astype(bf16)

        @pl.when((step == 0) & edge)
        def _():
            hand_on.start()

        @pl.when((step == 1) | (step == 2))
        def _():
            give(owner).start()

        return carry

    lax.fori_loop(0, experts, one, 0)

    def project(block, carry):
        number = turned_pair(block, group, bits)
        columns = pl.ds(pl.multiple_of(number * tile, tile), tile)
        block_at = pl.ds(pl.multiple_of(block * tile, tile), tile)
        for half, value in enumerate((grad_keys, grad_values)):
            blocks[block_at, half * own_width : (half + 1) * own_width] = lax.dot_general(
                normed_ref[:, columns], value[...], stack, preferred_element_type=f32
            ).astype(bf16)

        @pl.when(block % 2 == 1)
        def _():
            sums.across(block // 2).start()

        return carry

    lax.fori_loop(0, 8, project, 0)
    piece = 32

    def add_rows(target, start, source, other_start, count):
        def add(step, carry):
            at = pl.ds(pl.multiple_of(start + step * piece, piece), piece)
            have = pl.ds(pl.multiple_of(other_start + step * piece, piece), piece)
            target[at] = (target[at].astype(f32) + source[have].astype(f32)).astype(target.dtype)
            return carry

        lax.fori_loop(0, count // piece, add, 0)

    for chip in range(4):
        sums.settle(chip)

    @pl.when(jnp.logical_not(edge))
    def _():
        hand_on.wait_recv()
        add_rows(part.at[2 - side], 0, pile, 0, seq_len)
        give(2 - side).start()

    sums.cross()
    sums.close()
    share = tile // experts
    swaps = [
        send_to(
            (group, other),
            blocks.at[pl.ds(pl.multiple_of(other * share, share), share)],
            swapped.at[mine],
            swap_send.at[hop],
            swap_recv.at[hop],
        )
        for hop, other in enumerate(others)
    ]
    for copy in swaps:
        copy.start()

    def hand_out(source, value):
        at = pl.ds(pl.multiple_of(source * own_width, own_width), own_width)
        key_out[:, at] = value[:, :own_width].astype(f32)
        value_out[:, at] = value[:, own_width:].astype(f32)

    hand_out(mine, blocks[pl.ds(pl.multiple_of(mine * share, share), share)])
    for hop in range(1, experts):
        source = (mine + experts - hop) % experts
        swaps[hop - 1].wait_recv()
        hand_out(source, swapped[source])

    home_out[...] = part[mine].astype(f32)
    for hop in range(1, experts):
        source = (mine + hop) % experts
        middle = ((mine + 1) % experts) // 2 == 1

        @pl.when(jnp.logical_not(middle & (source == (mine + 2) % experts)))
        def _():
            got_from(source).wait_recv()

            def add(step, carry):
                at = pl.ds(pl.multiple_of(step * piece, piece), piece)
                home_out[at] = home_out[at] + got[source, at].astype(f32)
                return carry

            lax.fori_loop(0, seq_len // piece, add, 0)

    @pl.when(edge)
    def _():
        hand_on.wait_send()

    @pl.when(jnp.logical_not(edge))
    def _():
        give(2 - side).wait_send()

    for number in (1, 2):
        give(owner_of(number)).wait_send()
    for copy in swaps:
        copy.wait_send()
    sums.drain()


def last_call(rows_back, table, key_own, value_own, grad_keys, grad_values, normed):
    tokens, own = grad_keys.shape
    depth = normed.shape[1]
    experts = 4
    heads_width = own * experts
    seq_len = tokens // experts
    tile = depth // 8
    share = tile // experts
    vmem = pl.BlockSpec(memory_space=pltpu.VMEM)

    def dma(*shape):
        return pltpu.SemaphoreType.DMA(shape)

    def blocks(count):
        return pltpu.VMEM((count * tile, 2 * own), bf16)

    return pl.pallas_call(
        last_kernel,
        out_shape=[
            jax.ShapeDtypeStruct((seq_len, depth), f32),
            jax.ShapeDtypeStruct((share, heads_width), f32),
            jax.ShapeDtypeStruct((share, heads_width), f32),
        ],
        in_specs=[vmem] * 7,
        out_specs=[vmem] * 3,
        scratch_shapes=[
            pltpu.VMEM((experts, seq_len, depth), bf16),
            pltpu.VMEM((experts, seq_len, depth), bf16),
            pltpu.VMEM((seq_len, depth), bf16),
            blocks(8),
            blocks(4),
            blocks(3),
            pltpu.VMEM((experts, share, 2 * own), bf16),
            dma(4),
            dma(4),
            dma(6),
            dma(6),
            dma(4),
            dma(4),
            dma(1),
            dma(1),
            dma(3),
            dma(3),
        ],
        compiler_params=pltpu.CompilerParams(
            collective_id=5, has_side_effects=True, vmem_limit_bytes=56 * 1024 * 1024
        ),
        name="attend_last",
    )(rows_back, table, key_own, value_own, grad_keys, grad_values, normed)


def last_plain(rows_back, table, key_own, value_own, grad_keys, grad_values, normed):
    experts = lax.axis_size("expert")
    own_width = grad_keys.shape[1]
    depth = normed.shape[1]
    part = (
        jnp.einsum("rt,rd->td", table, rows_back, preferred_element_type=f32)
        + jnp.einsum("te,de->td", grad_keys, key_own, preferred_element_type=f32)
        + jnp.einsum("te,de->td", grad_values, value_own, preferred_element_type=f32)
    ).astype(bf16)
    home = jnp.sum(exchange(part.reshape(experts, -1, depth)).astype(f32), axis=0)
    both = jnp.einsum(
        "td,te->de",
        normed,
        jnp.concatenate([grad_keys, grad_values], axis=1),
        preferred_element_type=f32,
    ).astype(bf16)
    both = lax.psum_scatter(both, "dp", scatter_dimension=0, tiled=True)
    both = exchange(both.reshape(experts, -1, 2 * own_width))
    both = both.reshape(experts, -1, 2, own_width).transpose(2, 1, 0, 3).astype(f32)
    return home, both[0].reshape(-1, experts * own_width), both[1].reshape(
        -1, experts * own_width
    )


def ffn_plain(own, slopes, picks, router, gate, up, down):
    groups, rows, width = slopes.shape
    depth = own.shape[1]
    held = lax.all_gather(own, "dp", axis=0, tiled=True)
    logits = jnp.einsum("rd,ed->re", held, router, preferred_element_type=f32)
    weight = 1.0 / (1.0 + jnp.exp(jnp.sum(logits * picks, axis=-1, keepdims=True)))
    plain = slopes.reshape(groups * rows, width)
    gate_pre = jnp.einsum("rd,fd->rf", held, gate, preferred_element_type=f32)
    up_pre = jnp.einsum("rd,fd->rf", held, up, preferred_element_type=f32)
    sigmoid = 1.0 / (1.0 + jnp.exp(-gate_pre))
    active = gate_pre * sigmoid
    hidden = (active * up_pre).astype(bf16)
    wide = hidden.astype(f32)
    inner = weight * plain
    grad_gate = (inner * up_pre * (sigmoid * (1.0 + gate_pre * (1.0 - sigmoid)))).astype(bf16)
    grad_up = (inner * active).astype(bf16)
    made = jnp.dot(hidden, down, preferred_element_type=f32).astype(bf16)
    grads = (
        jnp.dot(grad_gate, gate, preferred_element_type=f32)
        + jnp.dot(grad_up, up, preferred_element_type=f32)
    ).astype(bf16)
    grads = lax.psum_scatter(
        grads.reshape(groups, rows, depth), "dp", scatter_dimension=0, tiled=True
    )[0]
    dense = lax.psum_scatter(
        jnp.sum(wide * plain, axis=-1).reshape(groups, rows),
        "dp",
        scatter_dimension=0,
        tiled=True,
    )

    def split(value):
        return value.reshape(groups, rows, value.shape[-1])

    upper = dense[0][:, None].astype(bf16)
    lower = (dense[0][:, None] - upper.astype(f32)).astype(bf16)
    grads = jnp.concatenate([grads, upper, lower, jnp.zeros((rows, 126), bf16)], axis=1)
    scaled = (weight * wide).astype(bf16)
    return (
        split(held),
        split(scaled),
        split(grad_gate),
        split(grad_up),
        split(made),
        grads,
    )


def back_plain(
    grad_rows, rows_flat, places, far, near, output_w, query, key, value, mixture, query_w
):
    experts = lax.axis_size("expert")
    grad_query, keys_part, values_part, output_part = attend_back(
        experts, grad_rows, places, far, output_w, query, key, value, mixture
    )
    output_sum = lax.psum_scatter(output_part, "dp", scatter_dimension=0, tiled=True)
    grad_values = jnp.sum(exchange(values_part).astype(f32), axis=0).astype(bf16)
    grad_keys = jnp.sum(exchange(keys_part).astype(f32), axis=0)
    grad_keys = jnp.concatenate(
        [
            turned_back(grad_keys[:, start : start + HEAD], near)
            for start in range(0, grad_keys.shape[1], HEAD)
        ],
        axis=1,
    ).astype(bf16)
    query_part = jnp.einsum("rd,re->de", rows_flat, grad_query, preferred_element_type=f32)
    query_sum = lax.psum_scatter(
        query_part.astype(bf16), "dp", scatter_dimension=0, tiled=True
    )
    rows_back = jnp.einsum("re,de->rd", grad_query, query_w, preferred_element_type=f32)
    return rows_back.astype(bf16), grad_keys, grad_values, output_sum, query_sum


def exchange(value):
    return lax.all_to_all(value, "expert", split_axis=0, concat_axis=0, tiled=True)


def on_device(
    hidden_in,
    out_grad,
    seq_lengths,
    attn_choice,
    moe_choice,
    attn_gain,
    moe_gain,
    attn_router,
    moe_router,
    key_weight,
    value_weight,
    query_weight,
    output_weight,
    gate_weight,
    up_weight,
    down_weight,
):
    experts = lax.axis_size("expert")
    groups = lax.axis_size("dp")
    mine_index = lax.axis_index("expert")
    seq_len = hidden_in.shape[1]
    model_width = hidden_in.shape[2]
    head_width = query_weight.shape[2]
    own_width = head_width // experts
    capacity = 2 * seq_len // experts + 8
    expert_rows = experts * capacity
    total_rows = groups * expert_rows
    score_scale = HEAD ** (-0.5)
    places = jnp.arange(seq_len, dtype=jnp.int32)
    own_length = lax.dynamic_index_in_dim(seq_lengths, mine_index, 0, keepdims=False)
    live_rows = (places < own_length).astype(f32)
    own_attn = lax.dynamic_index_in_dim(attn_choice, mine_index, 0, keepdims=False)
    own_moe = lax.dynamic_index_in_dim(moe_choice, mine_index, 0, keepdims=False)
    kinds = 2 + 2 * experts
    ready = groups == 8 and experts == 4
    near_home = signed_tables(places)
    (
        small_full,
        told_full,
        spread_table,
        row_places,
        cos_far,
        sin_far,
        table_attn,
        table_moe,
        normed_group,
        rows_flat,
        queries,
        keys_all,
        values_all,
        mixture,
        attn_rows,
        value_own,
        key_own,
        query_full,
        output_full,
        given_rows,
    ) = (start_call if ready else start_plain)(
        hidden_in[0],
        attn_gain[None],
        moe_gain[None],
        attn_router.T,
        moe_router.T,
        attn_choice.transpose(2, 0, 1),
        moe_choice.transpose(2, 0, 1),
        seq_lengths[:, None],
        near_home,
        out_grad[0],
        value_weight,
        key_weight,
        query_weight[0],
        output_weight[0],
    )
    far = (cos_far, sin_far)
    near = tuple(jnp.tile(part, (experts, 1)) for part in near_home)
    table_attn = table_attn.reshape(experts, capacity, seq_len)
    table_moe = table_moe.reshape(experts, capacity, seq_len)
    given_all = lax.all_gather(
        given_rows.reshape(expert_rows, model_width), "dp", axis=0, tiled=True
    )
    attn_rows = attn_rows.reshape(experts, capacity, model_width)

    gain_attn = small_full[0].astype(f32)
    gain_moe = small_full[1].astype(f32)
    router_attn = small_full[2 : 2 + experts]
    router_moe = small_full[2 + experts : kinds]
    inputs_f = hidden_in[0].astype(f32)
    scale_one = norm_scale(inputs_f)
    normed_one = (inputs_f * scale_one * gain_attn).astype(bf16)
    attn_logits = jnp.einsum("td,ed->te", normed_one, router_attn, preferred_element_type=f32)
    onehot_attn, shares_attn, dense_attn = router_gates(attn_logits, own_attn, live_rows, experts)

    told = told_full.reshape(groups, 2, experts, seq_len).transpose(1, 0, 2, 3)
    told = told.reshape(2, groups * experts, seq_len).astype(jnp.int32)
    comes = (told[0] == mine_index) | (told[1] == mine_index)
    order = jnp.cumsum(comes.astype(jnp.int32), axis=1) - 1
    slots = jnp.arange(capacity, dtype=jnp.int32)[None, :, None]
    rivals = jnp.sum(
        jnp.where(
            (order[:, None, :] == slots) & comes[:, None, :],
            (told[0] + told[1] - mine_index)[:, None, :],
            0,
        ),
        axis=-1,
    ).reshape(total_rows, 1)
    back_attn = exchange(attn_rows)
    spread_attn = jnp.einsum("ect,ecd->etd", table_attn, back_attn, preferred_element_type=f32)
    attn_sum = jnp.sum(dense_attn.T[:, :, None] * spread_attn, axis=0)
    middle = inputs_f + attn_sum
    scale_two = norm_scale(middle)
    normed_two = (middle * scale_two * gain_moe).astype(bf16)
    moe_logits = jnp.einsum("td,ed->te", normed_two, router_moe, preferred_element_type=f32)
    onehot_moe, shares_moe, dense_moe = router_gates(moe_logits, own_moe, live_rows, experts)
    send_moe = jnp.einsum(
        "ect,td->ecd", table_moe, normed_two, preferred_element_type=f32
    ).astype(bf16)
    rows_moe = exchange(send_moe).reshape(expert_rows, model_width)

    units = gate_weight.shape[2]
    room = -(-units // 256) * 256
    gate_slice = jnp.pad(gate_weight[0].T.astype(bf16), ((0, room - units), (0, 0)))
    up_slice = jnp.pad(up_weight[0].T.astype(bf16), ((0, room - units), (0, 0)))
    down_slice = jnp.pad(down_weight[0].astype(bf16), ((0, room - units), (0, 0)))
    slopes = jnp.einsum("rd,fd->rf", given_all, down_slice, preferred_element_type=f32)
    expert_ids = jnp.arange(16, dtype=jnp.int32)[None, :]
    picks = (expert_ids == rivals).astype(f32) - (
        expert_ids == mine_index
    ).astype(f32)
    router_rows = jnp.pad(router_moe, ((0, 16 - experts), (0, 0)))
    feed = ffn_call if groups == 8 and expert_rows % 96 == 0 else ffn_plain
    ffn_rows, scaled, grad_gate, grad_up, partial_out, grad_ffn = feed(
        rows_moe,
        slopes.reshape(groups, expert_rows, room),
        picks,
        router_rows,
        gate_slice,
        up_slice,
        down_slice,
    )
    back_moe_grad = exchange(grad_ffn.reshape(experts, capacity, model_width + 128))
    summed_out = lax.psum_scatter(partial_out, "dp", scatter_dimension=0, tiled=True)
    ffn_rows = ffn_rows.reshape(total_rows, model_width)
    down_grad = jnp.einsum(
        "rf,rd->fd",
        scaled.reshape(total_rows, room)[:, :units],
        given_all,
        preferred_element_type=f32,
    )[None]
    gate_grad = jnp.einsum(
        "rd,rf->df",
        ffn_rows,
        grad_gate.reshape(total_rows, room)[:, :units],
        preferred_element_type=f32,
    )[None]
    up_grad = jnp.einsum(
        "rd,rf->df",
        ffn_rows,
        grad_up.reshape(total_rows, room)[:, :units],
        preferred_element_type=f32,
    )[None]
    back_moe_grad, down_grad, gate_grad = lax.optimization_barrier(
        (back_moe_grad, down_grad, gate_grad)
    )
    back_dense = jnp.sum(back_moe_grad[:, :, model_width:].astype(f32), axis=-1)
    back_moe_grad = back_moe_grad[:, :, :model_width]

    grad_out = out_grad[0].astype(f32) * live_rows[:, None]
    grad_dense_moe = jnp.sum(table_moe.astype(f32) * back_dense[:, :, None], axis=1).T
    grad_normed_two = jnp.einsum(
        "ect,ecd->td", table_moe, back_moe_grad, preferred_element_type=f32
    )
    grad_logits_moe = gates_backward(grad_dense_moe, onehot_moe, shares_moe, live_rows)
    grad_normed_two = grad_normed_two + jnp.dot(
        grad_logits_moe, router_moe.astype(f32), precision=highest
    )
    moe_router_part = jnp.dot(grad_logits_moe.T, normed_two.astype(f32), precision=highest)
    grad_middle_norm, moe_gain_part = norm_backward(grad_normed_two, middle, scale_two, gain_moe)
    grad_middle = grad_out + grad_middle_norm
    grad_dense_attn = jnp.sum(grad_middle[None] * spread_attn, axis=-1).T
    rows_attn_grad = (dense_attn.T[:, :, None] * grad_middle[None]).astype(bf16)
    send_attn_grad = jnp.einsum(
        "ect,etd->ecd", table_attn, rows_attn_grad, preferred_element_type=f32
    ).astype(bf16)
    recv_attn_grad = exchange(send_attn_grad)
    recv_attn_grad, up_grad, summed_out = lax.optimization_barrier(
        (recv_attn_grad, up_grad, summed_out)
    )

    back_moe = exchange(summed_out[0].reshape(experts, capacity, model_width))
    backward = back_call if ready else back_plain
    rows_back, grad_keys, grad_values, output_out, query_out = backward(
        recv_attn_grad.reshape(expert_rows, model_width),
        rows_flat,
        row_places,
        far,
        near,
        output_full,
        queries,
        keys_all,
        values_all,
        mixture,
        query_full,
    )
    rows_back, back_moe = lax.optimization_barrier((rows_back, back_moe))
    grad_normed_one, key_grad, value_grad = (last_call if ready else last_plain)(
        rows_back, spread_table, key_own, value_own, grad_keys, grad_values, normed_group
    )
    spread_moe = jnp.einsum("ect,ecd->etd", table_moe, back_moe, preferred_element_type=f32)
    moe_sum = jnp.sum(dense_moe.T[:, :, None] * spread_moe, axis=0)
    block_out = (live_rows[:, None] * (middle + moe_sum)).astype(bf16)[None]
    grad_logits_attn = gates_backward(grad_dense_attn, onehot_attn, shares_attn, live_rows)
    attn_router_part = jnp.dot(grad_logits_attn.T, normed_one.astype(f32), precision=highest)
    grad_normed_one = grad_normed_one + jnp.dot(
        grad_logits_attn, router_attn.astype(f32), precision=highest
    )
    grad_inputs_norm, attn_gain_part = norm_backward(
        grad_normed_one, inputs_f, scale_one, gain_attn
    )
    input_grad = (grad_middle + grad_inputs_norm).astype(bf16)[None]
    smalls = total_small(
        jnp.concatenate(
            [attn_gain_part[None], moe_gain_part[None], attn_router_part, moe_router_part]
        )
    )
    return (
        block_out,
        input_grad,
        smalls[0],
        smalls[1],
        smalls[2 : 2 + experts].T,
        smalls[2 + experts : kinds].T,
        key_grad,
        value_grad,
        query_out.astype(f32)[None],
        output_out.astype(f32)[None],
        gate_grad,
        up_grad,
        down_grad,
    )


def solution(mesh):
    placed = (
        P(("dp", "expert"), None, None),
        P(("dp", "expert"), None, None),
        P("dp"),
        P("dp", None, None),
        P("dp", None, None),
        P("dp"),
        P("dp"),
        P("dp", None),
        P("dp", None),
        P("dp", None),
        P("dp", None),
        P("expert", "dp", None),
        P("expert", "dp", None),
        P("expert", None, "dp"),
        P("expert", None, "dp"),
        P("expert", "dp", None),
    )
    return jax.shard_map(
        on_device,
        mesh=mesh,
        in_specs=placed,
        out_specs=(
            P(("dp", "expert"), None, None),
            P(("dp", "expert"), None, None),
            P(("dp", "expert")),
            P(("dp", "expert")),
            P(("dp", "expert"), None),
            P(("dp", "expert"), None),
            P(("dp", "expert"), None),
            P(("dp", "expert"), None),
            P("expert", "dp", None),
            P("expert", "dp", None),
            P("expert", None, "dp"),
            P("expert", None, "dp"),
            P("expert", "dp", None),
        ),
        check_vma=False,
    )
```

```python
from functools import partial

import jax
import jax.numpy as jnp
from jax import lax
from jax.experimental import pallas as pl
from jax.experimental.pallas import tpu as pltpu
from jax.sharding import PartitionSpec as P

HEADS = 16
HEAD = 128
MESH = pl.DeviceIdType.MESH
ANY = pl.BlockSpec(memory_space=pl.ANY)

eps = 1e-06
theta = 10000.0
highest = lax.Precision.HIGHEST
f32 = jnp.float32
bf16 = jnp.bfloat16


def rope_tables(positions, head_size):
    half_size = head_size // 2
    frequency = theta ** (-(jnp.arange(half_size, dtype=f32) * 2.0 / head_size))
    angles = positions.astype(f32)[:, None] * frequency[None, :]
    return (jnp.cos(angles), jnp.sin(angles))


def signed_tables(positions):
    cosine, sine = rope_tables(positions, HEAD)
    return (jnp.concatenate([cosine, cosine], 1), jnp.concatenate([-sine, sine], 1))


def turned_back(value, tables):
    half_size = HEAD // 2
    swapped = jnp.concatenate([value[:, half_size:], value[:, :half_size]], axis=1)
    return value * tables[0] - swapped * tables[1]


def norm_scale(value):
    return lax.rsqrt(jnp.mean(value * value, axis=-1, keepdims=True) + eps)


def norm_backward(grad_normed, value, scale_value, gain_value):
    scaled_grad = grad_normed * gain_value
    gain_part = jnp.sum(grad_normed * value * scale_value, axis=0)
    grad_value = scale_value * scaled_grad - value * scale_value**3 * jnp.mean(
        scaled_grad * value, axis=-1, keepdims=True
    )
    return (grad_value, gain_part)


def softmax_rows(values):
    peak = jnp.max(values, axis=-1, keepdims=True)
    powers = jnp.exp(values - peak)
    return powers / jnp.sum(powers, axis=-1, keepdims=True)


def router_gates(logits, choices, live_rows, experts):
    onehot = (choices[:, :, None] == jnp.arange(experts, dtype=jnp.int32)[None, None, :]).astype(
        f32
    )
    chosen = jnp.sum(logits[:, None, :] * onehot, axis=-1)
    shares = softmax_rows(chosen)
    dense = jnp.sum((shares * live_rows[:, None])[:, :, None] * onehot, axis=1)
    return (onehot, shares, dense)


def gates_backward(grad_dense, onehot, shares, live_rows):
    grad_shares = jnp.sum(grad_dense[:, None, :] * onehot, axis=-1) * live_rows[:, None]
    grad_chosen = shares * (grad_shares - jnp.sum(shares * grad_shares, axis=-1, keepdims=True))
    return jnp.sum(grad_chosen[:, :, None] * onehot, axis=1)


def route_table(choices, length_value, experts, capacity):
    places = jnp.arange(choices.shape[0], dtype=jnp.int32)
    living = (places < length_value).astype(jnp.int32)
    picked = (
        jnp.sum(
            (choices[:, :, None] == jnp.arange(experts, dtype=jnp.int32)[None, None, :]).astype(
                jnp.int32
            ),
            axis=1,
        )
        * living[:, None]
    )
    slot_of = jnp.cumsum(picked, axis=0) - 1
    slot_ids = jnp.arange(capacity, dtype=jnp.int32)
    return (slot_of.T[:, None, :] == slot_ids[None, :, None]) & (picked.T[:, None, :] == 1)


def flip(index, bit):
    return index + bit * (1 - 2 * ((index // bit) % 2))


def flips(index, mask, bits):
    for bit in bits:
        if mask & bit:
            index = flip(index, bit)
    return index


def span(bits):
    masks = [0]
    for bit in bits:
        masks = masks + [mask | bit for mask in masks]
    return masks


def bit_orders(size):
    bits = [1 << k for k in range(size.bit_length() - 1)]
    high = bits[1:]
    return (high + bits[:1], high[::-1] + bits[:1])


def barrier(targets):
    semaphore = pltpu.get_barrier_semaphore()
    for target in targets:
        pl.semaphore_signal(semaphore, inc=1, device_id=target, device_id_type=MESH)
    pl.semaphore_wait(semaphore, len(targets))


def gather_kernel(groups, experts, splits, axes, *refs):
    count = len(splits)
    shards, home = refs[:count], refs[count]
    fulls, home_all = refs[count + 1 : 2 * count + 1], refs[2 * count + 1]
    local_sem, send_sem, recv_sem, home_send, home_recv = refs[2 * count + 2 :]
    group = lax.axis_index("dp")
    mine = lax.axis_index("expert")
    orders = bit_orders(groups)
    bits = sorted(orders[0])
    others = [(mine + step) % experts for step in range(1, experts)]
    barrier([(flip(group, bit), mine) for bit in bits] + [(group, other) for other in others])

    home_copies = []
    for step, other in enumerate(others):
        copy = pltpu.make_async_remote_copy(
            src_ref=home,
            dst_ref=home_all.at[mine],
            send_sem=home_send.at[step],
            recv_sem=home_recv.at[step],
            device_id=(group, other),
            device_id_type=MESH,
        )
        copy.start()
        home_copies.append(copy)

    def part(ref, which, block, half):
        pieces, axis = splits[which], axes[which]
        extent = shards[which].shape[axis]
        size = extent // pieces
        start = half * size if block is None else block * extent + half * size
        if block is not None:
            start = pl.multiple_of(start, size)
        where = pl.ds(start, size)
        return ref.at[where] if axis == 0 else ref.at[:, where]

    stages = {}
    slot = 0
    for which in range(count):
        for half in range(splits[which]):
            order = orders[half]
            for stage, bit in enumerate(order):
                copies = []
                for mask in span(order[:stage]):
                    block = flips(group, mask, bits)
                    target = part(fulls[which], which, block, half)
                    source = part(shards[which], which, None, half) if mask == 0 else target
                    copies.append(
                        pltpu.make_async_remote_copy(
                            src_ref=source,
                            dst_ref=target,
                            send_sem=send_sem.at[slot],
                            recv_sem=recv_sem.at[slot],
                            device_id=(flip(group, bit), mine),
                            device_id_type=MESH,
                        )
                    )
                    slot += 1
                stages[which, half, stage] = copies
    keys = [(which, half) for which in range(count) for half in range(splits[which])]
    for which, half in keys:
        for copy in stages[which, half, 0]:
            copy.start()
    local = [pltpu.make_async_copy(home, home_all.at[mine], local_sem.at[count])]
    for which in range(count):
        extent = shards[which].shape[axes[which]]
        where = pl.ds(pl.multiple_of(group * extent, extent), extent)
        target = fulls[which].at[where] if axes[which] == 0 else fulls[which].at[:, where]
        local.append(pltpu.make_async_copy(shards[which], target, local_sem.at[which]))
    for copy in local:
        copy.start()
    for stage in range(len(bits)):
        for which, half in keys:
            for copy in stages[which, half, stage]:
                copy.wait_recv()
            if stage + 1 < len(bits):
                for copy in stages[which, half, stage + 1]:
                    copy.start()
    for copies in stages.values():
        for copy in copies:
            copy.wait_send()
    for copy in home_copies:
        copy.wait()
    for copy in local:
        copy.wait()


def gather_all(arrays, splits, axes, home):
    groups = lax.axis_size("dp")
    experts = lax.axis_size("expert")
    shapes = []
    for array, axis in zip(arrays, axes):
        shape = list(array.shape)
        shape[axis] *= groups
        shapes.append(jax.ShapeDtypeStruct(tuple(shape), array.dtype))
    shapes.append(jax.ShapeDtypeStruct((experts,) + home.shape, home.dtype))
    slots = sum(splits) * (groups - 1)
    return pl.pallas_call(
        partial(gather_kernel, groups, experts, splits, axes),
        out_shape=shapes,
        in_specs=[ANY] * (len(arrays) + 1),
        out_specs=[ANY] * (len(arrays) + 1),
        scratch_shapes=[
            pltpu.SemaphoreType.DMA((len(arrays) + 1,)),
            pltpu.SemaphoreType.DMA((slots,)),
            pltpu.SemaphoreType.DMA((slots,)),
            pltpu.SemaphoreType.DMA((experts - 1,)),
            pltpu.SemaphoreType.DMA((experts - 1,)),
        ],
        compiler_params=pltpu.CompilerParams(collective_id=0, has_side_effects=True),
        name="gather_all",
    )(*arrays, home)


def total_kernel(groups, experts, parts, total, held, send_sem, recv_sem):
    devices = groups * experts
    me = lax.axis_index("dp") * experts + lax.axis_index("expert")
    semaphore = pltpu.get_barrier_semaphore()

    def greet(step, carry):
        other = (me + step) % devices
        pl.semaphore_signal(
            semaphore,
            inc=1,
            device_id=(other // experts, other % experts),
            device_id_type=MESH,
        )
        return carry

    lax.fori_loop(1, devices, greet, 0)
    pl.semaphore_wait(semaphore, devices - 1)

    share = parts.shape[1] // devices

    def columns(owner):
        return pl.ds(pl.multiple_of((owner * share // 128) * 128, 128), 128)

    def copy_of(step):
        other = (me + step) % devices
        return pltpu.make_async_remote_copy(
            src_ref=parts.at[:, columns(other)],
            dst_ref=held.at[step],
            send_sem=send_sem.at[step],
            recv_sem=recv_sem.at[step],
            device_id=(other // experts, other % experts),
            device_id_type=MESH,
        )

    def send(step, carry):
        copy_of(step).start()
        return carry

    lax.fori_loop(1, devices, send, 0)
    held[0] = parts[:, columns(me)]

    def finish(step, carry):
        copy_of(step).wait()
        return carry

    lax.fori_loop(1, devices, finish, 0)
    total[...] = jnp.sum(held[...], axis=0)


def total_small(rows):
    groups = lax.axis_size("dp")
    experts = lax.axis_size("expert")
    devices = groups * experts
    kinds, width = rows.shape
    share = width // devices
    room = -(-kinds // 8) * 8
    total = pl.pallas_call(
        partial(total_kernel, groups, experts),
        out_shape=jax.ShapeDtypeStruct((room, 128), f32),
        in_specs=[pl.BlockSpec(memory_space=pltpu.VMEM)],
        out_specs=pl.BlockSpec(memory_space=pltpu.VMEM),
        scratch_shapes=[
            pltpu.VMEM((devices, room, 128), f32),
            pltpu.SemaphoreType.DMA((devices,)),
            pltpu.SemaphoreType.DMA((devices,)),
        ],
        compiler_params=pltpu.CompilerParams(collective_id=1, has_side_effects=True),
        name="total_small",
    )(jnp.pad(rows, ((0, room - kinds), (0, 0))))
    place = (lax.axis_index("dp") * experts + lax.axis_index("expert")) % (128 // share)
    return lax.dynamic_slice_in_dim(total, place * share, share, 1)[:kinds]


def turn(value, cosine, sine):
    return value * cosine + pltpu.roll(value, HEAD // 2, 1) * sine


def softmax_all(scores, seen):
    masked = jnp.where(seen, scores * (HEAD ** (-0.5)), -1e30)
    powers = jnp.exp(masked - jnp.max(masked, axis=-1, keepdims=True))
    return powers / jnp.sum(powers, axis=-1, keepdims=True)


def blocks_of(experts, rows, tokens, width):
    capacity, seq_len = rows // experts, tokens // experts
    return [
        (
            slice(seq * capacity, (seq + 1) * capacity),
            slice(seq * seq_len, (seq + 1) * seq_len),
            slice(head * HEAD, (head + 1) * HEAD),
        )
        for head in range(width // HEAD)
        for seq in range(experts)
    ]


def attend_kernel(
    experts,
    inputs_ref,
    small_ref,
    table_ref,
    place_ref,
    cos_far,
    sin_far,
    cos_near,
    sin_near,
    query_weight,
    key_weight,
    value_weight,
    normed_out,
    rows_out,
    query_out,
    key_out,
    value_out,
    mixture_out,
    query_hold,
):
    @pl.when(pl.program_id(0) == 0)
    def _():
        gain = small_ref[0:1].astype(f32)

        def norm_part(step, carry):
            at = pl.ds(pl.multiple_of(step * 32, 32), 32)
            value = inputs_ref[at].astype(f32)
            normed_out[at] = (value * norm_scale(value) * gain).astype(bf16)
            return carry

        lax.fori_loop(0, inputs_ref.shape[0] // 32, norm_part, 0)
        rows_out[...] = jnp.dot(
            table_ref[...], normed_out[...], preferred_element_type=f32
        ).astype(bf16)

    capacity = rows_out.shape[0] // experts
    seq_len = normed_out.shape[0] // experts
    width = key_out.shape[1]
    key = jnp.dot(normed_out[...], key_weight[...], preferred_element_type=f32)
    value_out[...] = jnp.dot(
        normed_out[...], value_weight[...], preferred_element_type=f32
    ).astype(bf16)
    query = jnp.dot(rows_out[...], query_weight[...], preferred_element_type=f32)
    for head in range(width // HEAD):
        cut = slice(head * HEAD, (head + 1) * HEAD)
        key_out[:, cut] = turn(key[:, cut], cos_near[...], sin_near[...]).astype(bf16)
        query_hold[:, cut] = turn(query[:, cut], cos_far[...], sin_far[...])
    query_out[...] = query_hold[...].astype(bf16)
    blocks = blocks_of(experts, rows_out.shape[0], normed_out.shape[0], width)
    contract = (((1,), (1,)), ((), ()))
    scores = jnp.concatenate(
        [
            lax.dot_general(
                query_hold[rows, cut].astype(bf16),
                key_out[keys, cut],
                contract,
                preferred_element_type=f32,
            )
            for rows, keys, cut in blocks
        ],
        axis=0,
    )
    spots = lax.broadcasted_iota(jnp.int32, (rows_out.shape[0], seq_len), 1)
    seen = spots <= place_ref[...]
    probs = softmax_all(scores, jnp.concatenate([seen] * (width // HEAD), axis=0))
    for number, (rows, keys, cut) in enumerate(blocks):
        query_hold[rows, cut] = jnp.dot(
            probs[number * capacity : (number + 1) * capacity].astype(bf16),
            value_out[keys, cut],
            preferred_element_type=f32,
        )
    mixture_out[...] = query_hold[...].astype(bf16)


def attend(experts, inputs, small, table, places, far, near, query_w, key_w, value_w):
    tokens, depth = inputs.shape
    rows = table.shape[0]
    heads_width = query_w.shape[1]
    tile = 256

    def full(shape):
        return pl.BlockSpec(shape, lambda step: (0, 0))

    def cut(height):
        return pl.BlockSpec((height, tile), lambda step: (0, step))

    def shaped(height, width):
        return jax.ShapeDtypeStruct((height, width), bf16)

    return pl.pallas_call(
        partial(attend_kernel, experts),
        grid=(heads_width // tile,),
        out_shape=[
            shaped(tokens, depth),
            shaped(rows, depth),
            shaped(rows, heads_width),
            shaped(tokens, heads_width),
            shaped(tokens, heads_width),
            shaped(rows, heads_width),
        ],
        in_specs=[
            full((tokens, depth)),
            full(small.shape),
            full(table.shape),
            full(places.shape),
            full((rows, HEAD)),
            full((rows, HEAD)),
            full((tokens, HEAD)),
            full((tokens, HEAD)),
            cut(depth),
            cut(depth),
            cut(depth),
        ],
        out_specs=[
            full((tokens, depth)),
            full((rows, depth)),
            cut(rows),
            cut(tokens),
            cut(tokens),
            cut(rows),
        ],
        scratch_shapes=[pltpu.VMEM((rows, tile), f32)],
        compiler_params=pltpu.CompilerParams(vmem_limit_bytes=48 * 1024 * 1024),
        cost_estimate=pl.CostEstimate(
            flops=2 * depth * heads_width * (2 * tokens + rows),
            bytes_accessed=6 * depth * heads_width + 8 * tokens * depth,
            transcendentals=rows * heads_width,
        ),
        name="attend",
    )(inputs, small, table, places, *far, *near, query_w, key_w, value_w)


def attend_back_kernel(
    experts,
    grad_ref,
    place_ref,
    cos_far,
    sin_far,
    weight_ref,
    query_ref,
    key_ref,
    value_ref,
    mixture_ref,
    query_out,
    key_out,
    value_out,
    output_out,
    grad_hold,
    query_hold,
    back_hold,
):
    contract = (((1,), (1,)), ((), ()))
    stack = (((0,), (0,)), ((), ()))
    rows_all = grad_ref.shape[0]
    capacity = rows_all // experts
    width = query_ref.shape[1]
    seq_len = key_ref.shape[0] // experts
    scale = HEAD ** (-0.5)
    grad_hold[...] = (
        lax.dot_general(grad_ref[...], weight_ref[...], contract, preferred_element_type=f32)
        .astype(bf16)
        .astype(f32)
    )
    output_out[...] = lax.dot_general(
        mixture_ref[...], grad_ref[...], stack, preferred_element_type=f32
    ).astype(bf16)
    query_hold[...] = query_ref[...].astype(f32)
    blocks = blocks_of(experts, rows_all, key_ref.shape[0], width)
    queries = [query_hold[rows, cut].astype(bf16) for rows, keys, cut in blocks]
    grads = [grad_hold[rows, cut].astype(bf16) for rows, keys, cut in blocks]
    scores = jnp.concatenate(
        [
            lax.dot_general(query, key_ref[keys, cut], contract, preferred_element_type=f32)
            for query, (rows, keys, cut) in zip(queries, blocks)
        ],
        axis=0,
    )
    grad_probs = jnp.concatenate(
        [
            lax.dot_general(grad, value_ref[keys, cut], contract, preferred_element_type=f32)
            for grad, (rows, keys, cut) in zip(grads, blocks)
        ],
        axis=0,
    )
    spots = lax.broadcasted_iota(jnp.int32, (rows_all, seq_len), 1)
    seen = spots <= place_ref[...]
    probs = softmax_all(scores, jnp.concatenate([seen] * (width // HEAD), axis=0))
    inner = jnp.sum(probs * grad_probs, axis=-1, keepdims=True)
    slopes = probs * (grad_probs - inner)
    for number, (rows, keys, cut) in enumerate(blocks):
        own = slice(number * capacity, (number + 1) * capacity)
        slope = slopes[own].astype(bf16)
        value_out[0, keys, cut] = lax.dot_general(
            probs[own].astype(bf16), grads[number], stack, preferred_element_type=f32
        ).astype(bf16)
        key_out[0, keys, cut] = (
            lax.dot_general(slope, queries[number], stack, preferred_element_type=f32) * scale
        ).astype(bf16)
        back_hold[rows, cut] = (
            jnp.dot(slope, key_ref[keys, cut], preferred_element_type=f32) * scale
        )
    for head in range(width // HEAD):
        cut = slice(head * HEAD, (head + 1) * HEAD)
        query_out[:, cut] = turn(back_hold[:, cut], cos_far[...], -sin_far[...]).astype(bf16)


def attend_back(experts, grad_rows, places, far, output_w, query, key, value, mixture):
    rows, depth = grad_rows.shape
    tokens, heads_width = key.shape
    tile = 256
    own_width = heads_width // experts
    steps = own_width // tile

    def full(shape):
        return pl.BlockSpec(shape, lambda step: (0, 0))

    def cut(height):
        return pl.BlockSpec((height, tile), lambda step: (0, step))

    by_heads = pl.BlockSpec((1, tokens, tile), lambda step: (step // steps, 0, step % steps))
    return pl.pallas_call(
        partial(attend_back_kernel, experts),
        grid=(heads_width // tile,),
        out_shape=[
            jax.ShapeDtypeStruct((rows, heads_width), bf16),
            jax.ShapeDtypeStruct((experts, tokens, own_width), bf16),
            jax.ShapeDtypeStruct((experts, tokens, own_width), bf16),
            jax.ShapeDtypeStruct((heads_width, depth), bf16),
        ],
        in_specs=[
            full((rows, depth)),
            full(places.shape),
            full((rows, HEAD)),
            full((rows, HEAD)),
            pl.BlockSpec((tile, depth), lambda step: (step, 0)),
            cut(rows),
            cut(tokens),
            cut(tokens),
            cut(rows),
        ],
        out_specs=[
            cut(rows),
            by_heads,
            by_heads,
            pl.BlockSpec((tile, depth), lambda step: (step, 0)),
        ],
        scratch_shapes=[pltpu.VMEM((rows, tile), f32)] * 3,
        compiler_params=pltpu.CompilerParams(vmem_limit_bytes=48 * 1024 * 1024),
        cost_estimate=pl.CostEstimate(
            flops=4 * rows * depth * heads_width,
            bytes_accessed=4 * depth * heads_width + 8 * tokens * heads_width,
            transcendentals=rows * heads_width,
        ),
        name="attend_back",
    )(grad_rows, places, *far, output_w, query, key, value, mixture)


def halves(ref, block, rows, half):
    size = rows // 2
    return ref.at[pl.ds(pl.multiple_of(block * rows + half * size, size), size)]


def whole(ref, block, rows):
    return ref.at[pl.ds(pl.multiple_of(block * rows, rows), rows)]


def ffn_kernel(
    rows,
    own_ref,
    slope_ref,
    pick_ref,
    router_ref,
    gate_in,
    up_in,
    down_in,
    rows_out,
    hidden_out,
    grad_gate_out,
    grad_up_out,
    out_out,
    grad_out,
    gate_ref,
    up_ref,
    down_ref,
    held,
    pulled,
    hidden,
    scaled,
    grad_gate,
    grad_up,
    made,
    grads,
    near,
    far,
    dense,
    dense_far,
    dense_hold,
    far_send,
    far_recv,
    near_send,
    near_recv,
    sum_send,
    sum_recv,
    dense_send,
    dense_recv,
    load_sem,
    save_sem,
    intake_sem,
):
    group = lax.axis_index("dp")
    mine = lax.axis_index("expert")
    depth = held.shape[1]
    width = hidden.shape[1]
    pair = 2 * rows
    bits = (1, 2, 4)
    peers = {mask: (flips(group, mask, bits), mine) for mask in range(1, 8)}
    intake = [
        pltpu.make_async_copy(source, target, intake_sem.at[number])
        for number, (source, target) in enumerate(
            ((gate_in, gate_ref), (up_in, up_ref), (down_in, down_ref))
        )
    ]
    for copy in intake:
        copy.start()
    barrier([peers[mask] for mask in range(1, 8)])

    def remote(source, target, send, recv, mask):
        return pltpu.make_async_remote_copy(
            src_ref=source,
            dst_ref=target,
            send_sem=send,
            recv_sem=recv,
            device_id=peers[mask],
            device_id_type=MESH,
        )

    def own_half(half):
        size = rows // 2
        return own_ref.at[pl.ds(half * size, size)]

    sends = {}
    for slot, (mask, half) in enumerate(((2, 0), (4, 1), (2, 1), (4, 0))):
        sends[mask, half] = remote(
            own_half(half),
            halves(held, mask, rows, half),
            far_send.at[slot],
            far_recv.at[slot],
            mask,
        )
    sends[6, 0] = remote(
        halves(held, 2, rows, 0), halves(held, 6, rows, 0), far_send.at[4], far_recv.at[4], 4
    )
    sends[6, 1] = remote(
        halves(held, 4, rows, 1), halves(held, 6, rows, 1), far_send.at[5], far_recv.at[5], 2
    )
    across = {}
    for chip in range(4):
        across[chip] = remote(
            own_ref if chip == 0 else whole(held, 2 * chip, rows),
            whole(held, 2 * chip + 1, rows),
            near_send.at[chip],
            near_recv.at[chip],
            1,
        )
    sends[2, 0].start()
    sends[4, 1].start()
    across[0].start()
    sends[2, 1].start()
    sends[4, 0].start()
    seat = pltpu.make_async_copy(own_ref, whole(held, 0, rows), load_sem.at[2])
    seat.start()

    def pull(chip, slot, which):
        block = group_of(2 * chip + which)
        return pltpu.make_async_copy(
            slope_ref.at[block], whole(pulled, 2 * slot + which, rows), load_sem.at[which]
        )

    def group_of(index):
        result = group
        for bit in bits:
            on = (index // bit) % 2
            turned = bit * (1 - 2 * ((group // bit) % 2))
            result = result + on * turned
        return result

    def saves(chip):
        copies = []
        for which in range(2):
            block = group_of(2 * chip + which)
            for number, (source, target) in enumerate(
                (
                    (whole(held, 2 * chip + which, rows), rows_out.at[block]),
                    (whole(scaled, which, rows), hidden_out.at[block]),
                    (whole(grad_gate, which, rows), grad_gate_out.at[block]),
                    (whole(grad_up, which, rows), grad_up_out.at[block]),
                    (whole(made, which, rows), out_out.at[block]),
                )
            ):
                copies.append(
                    pltpu.make_async_copy(source, target, save_sem.at[5 * which + number])
                )
        return copies

    def across_sum(chip):
        return remote(
            whole(grads, 2 * chip + 1, rows),
            whole(near, chip, rows),
            near_send.at[4 + chip],
            near_recv.at[4 + chip],
            1,
        )

    hops = {}
    for slot, (key, block, half, mask) in enumerate(
        (
            ("x2", 2, 0, 2),
            ("x6", 6, 0, 2),
            ("y4", 4, 1, 4),
            ("y6", 6, 1, 4),
            ("then_y", 4, 0, 4),
            ("then_x", 2, 1, 2),
        )
    ):
        size = rows // 2
        hops[key] = remote(
            halves(grads, block, rows, half),
            far.at[pl.ds(slot * size, size)],
            sum_send.at[slot],
            sum_recv.at[slot],
            mask,
        )
    far_slots = {"x2": 0, "x6": 1, "y4": 2, "y6": 3, "then_y": 4, "then_x": 5}

    def dense_hop(mask):
        return remote(
            dense.at[mask],
            dense_far.at[mask],
            dense_send.at[mask],
            dense_recv.at[mask],
            mask,
        )

    def join(chip):
        across_sum(chip).wait_recv()
        block = 2 * chip

        def add(step, carry):
            at = pl.ds(pl.multiple_of(block * rows + step * 48, 16), 48)
            other = pl.ds(pl.multiple_of(chip * rows + step * 48, 16), 48)
            grads[at] = (grads[at].astype(f32) + near[other].astype(f32)).astype(bf16)
            return carry

        lax.fori_loop(0, rows // 48, add, 0)

    def add_far(block, half, key):
        size = rows // 2
        hops[key].wait_recv()

        def add(step, carry):
            at = pl.ds(pl.multiple_of(block * rows + half * size + step * 48, 16), 48)
            other = pl.ds(far_slots[key] * size + pl.multiple_of(step * 48, 16), 48)
            grads[at] = (grads[at].astype(f32) + far[other].astype(f32)).astype(bf16)
            return carry

        lax.fori_loop(0, size // 48, add, 0)

    for which in range(2):
        pull(0, 0, which).start()
    seat.wait()
    for copy in intake:
        copy.wait()

    def step(chip, carry):
        @pl.when(chip == 0)
        def _():
            across[0].wait_recv()

        @pl.when(chip == 1)
        def _():
            sends[2, 0].wait_recv()
            sends[6, 0].start()
            sends[4, 1].wait_recv()
            sends[6, 1].start()
            sends[2, 1].wait_recv()
            across[1].start()
            sends[4, 0].wait_recv()
            across[2].start()
            across[1].wait_recv()

        @pl.when(chip == 2)
        def _():
            sends[6, 0].wait_recv()
            sends[6, 1].wait_recv()
            across[3].start()
            across[2].wait_recv()

        @pl.when(chip == 3)
        def _():
            across[3].wait_recv()

        slot = chip % 2
        for which in range(2):
            pull(chip, slot, which).wait()

        @pl.when(chip < 3)
        def _():
            for which in range(2):
                pull(chip + 1, 1 - slot, which).start()

        @pl.when(chip > 0)
        def _():
            for copy in saves(chip - 1):
                copy.wait()

        base = pl.multiple_of(chip * pair, pair)
        at = pl.ds(base, pair)
        logits = lax.dot_general(
            held[at], router_ref[...], (((1,), (1,)), ((), ())), preferred_element_type=f32
        )
        apart = []
        for which in range(2):
            block = group_of(2 * chip + which)
            picks = pick_ref[pl.ds(pl.multiple_of(block * rows, rows), rows)]
            apart.append(
                jnp.sum(
                    logits[which * rows : (which + 1) * rows] * picks, axis=-1, keepdims=True
                )
            )
        weight = 1.0 / (1.0 + jnp.exp(jnp.concatenate(apart, axis=0)))
        loads = pl.ds(pl.multiple_of(slot * pair, pair), pair)
        tile = width
        wide = 1024
        partial_dense = jnp.zeros((pair, 128), f32)

        def units(number, total):
            cut = pl.ds(pl.multiple_of(number * tile, tile), tile)
            contract = (((1,), (1,)), ((), ()))
            gate = lax.dot_general(
                held[at], gate_ref[cut], contract, preferred_element_type=f32
            )
            up = lax.dot_general(held[at], up_ref[cut], contract, preferred_element_type=f32)
            sigmoid = 1.0 / (1.0 + jnp.exp(-gate))
            active = gate * sigmoid
            value = (active * up).astype(bf16)
            exact = value.astype(f32)
            plain = pulled[loads, cut]
            hidden[:, cut] = value
            scaled[:, cut] = (weight * exact).astype(bf16)
            inner = weight * plain
            grad_gate[:, cut] = (inner * up * (sigmoid * (1.0 + gate * (1.0 - sigmoid)))).astype(
                bf16
            )
            grad_up[:, cut] = (inner * active).astype(bf16)
            both = exact * plain
            for start in range(0, tile, 128):
                total = total + both[:, start : start + 128]
            return total

        partial_dense = lax.fori_loop(0, width // tile, units, partial_dense)
        ones = jnp.ones((8, 128), f32)
        for which in range(2):
            dense[2 * chip + which] = lax.dot_general(
                ones,
                partial_dense[which * rows : (which + 1) * rows],
                (((1,), (1,)), ((), ())),
                precision=highest,
                preferred_element_type=f32,
            )

        @pl.when(chip == 1)
        def _():
            join(0)

        @pl.when(chip == 2)
        def _():
            join(1)
            hops["x2"].start()

        @pl.when(chip == 3)
        def _():
            join(2)
            hops["y4"].start()

        def columns(number, carry):
            cut = pl.ds(pl.multiple_of(number * wide, wide), wide)
            made[:, cut] = jnp.dot(
                hidden[...], down_ref[:, cut], preferred_element_type=f32
            ).astype(bf16)
            grads[at, cut] = (
                jnp.dot(grad_gate[...], gate_ref[:, cut], preferred_element_type=f32)
                + jnp.dot(grad_up[...], up_ref[:, cut], preferred_element_type=f32)
            ).astype(bf16)
            return carry

        lax.fori_loop(0, depth // wide, columns, 0)
        across_sum(chip).start()
        for copy in saves(chip):
            copy.start()
        return carry

    lax.fori_loop(0, 4, step, 0)
    join(3)
    hops["x6"].start()
    hops["y6"].start()
    for mask in range(1, 8):
        dense_hop(mask).start()
    add_far(0, 0, "x2")
    add_far(0, 1, "y4")
    add_far(4, 0, "x6")
    hops["then_y"].start()
    add_far(2, 1, "y6")
    hops["then_x"].start()
    total = dense[0]
    for mask in range(1, 8):
        dense_hop(mask).wait_recv()
        total = total + dense_far[mask]
    for copy in saves(3):
        copy.wait()
    pick = (lax.broadcasted_iota(jnp.int32, (8, 128), 0) == 0).astype(f32)
    column = lax.dot_general(
        total, pick, (((0,), (0,)), ((), ())), precision=highest, preferred_element_type=f32
    )
    upper = column.astype(bf16)
    lower = (column - upper.astype(f32)).astype(bf16)
    lane = lax.broadcasted_iota(jnp.int32, column.shape, 1)
    dense_hold[...] = jnp.where(lane == 0, upper, jnp.where(lane == 1, lower, 0.0)).astype(bf16)
    add_far(0, 0, "then_y")
    add_far(0, 1, "then_x")
    tail = pltpu.make_async_copy(dense_hold, grad_out.at[:, pl.ds(depth, 128)], load_sem.at[0])
    tail.start()
    last = pltpu.make_async_copy(
        whole(grads, 0, rows), grad_out.at[:, pl.ds(0, depth)], load_sem.at[2]
    )
    last.start()
    for copy in list(sends.values()) + list(across.values()) + list(hops.values()):
        copy.wait_send()
    for chip in range(4):
        across_sum(chip).wait_send()
    for mask in range(1, 8):
        dense_hop(mask).wait_send()
    last.wait()
    tail.wait()


def ffn_call(own, slopes, picks, router, gate, up, down):
    rows, depth = own.shape
    width = gate.shape[0]
    vmem = pl.BlockSpec(memory_space=pltpu.VMEM)
    return pl.pallas_call(
        partial(ffn_kernel, rows),
        out_shape=[
            jax.ShapeDtypeStruct((8, rows, depth), bf16),
            jax.ShapeDtypeStruct((8, rows, width), bf16),
            jax.ShapeDtypeStruct((8, rows, width), bf16),
            jax.ShapeDtypeStruct((8, rows, width), bf16),
            jax.ShapeDtypeStruct((8, rows, depth), bf16),
            jax.ShapeDtypeStruct((rows, depth + 128), bf16),
        ],
        in_specs=[ANY, ANY, vmem, vmem, ANY, ANY, ANY],
        out_specs=[ANY] * 6,
        scratch_shapes=[
            pltpu.VMEM((width, depth), bf16),
            pltpu.VMEM((width, depth), bf16),
            pltpu.VMEM((width, depth), bf16),
            pltpu.VMEM((8 * rows, depth), bf16),
            pltpu.VMEM((4 * rows, width), f32),
            pltpu.VMEM((2 * rows, width), bf16),
            pltpu.VMEM((2 * rows, width), bf16),
            pltpu.VMEM((2 * rows, width), bf16),
            pltpu.VMEM((2 * rows, width), bf16),
            pltpu.VMEM((2 * rows, depth), bf16),
            pltpu.VMEM((8 * rows, depth), bf16),
            pltpu.VMEM((4 * rows, depth), bf16),
            pltpu.VMEM((3 * rows, depth), bf16),
            pltpu.VMEM((8, 8, rows), f32),
            pltpu.VMEM((8, 8, rows), f32),
            pltpu.VMEM((rows, 128), bf16),
            pltpu.SemaphoreType.DMA((6,)),
            pltpu.SemaphoreType.DMA((6,)),
            pltpu.SemaphoreType.DMA((8,)),
            pltpu.SemaphoreType.DMA((8,)),
            pltpu.SemaphoreType.DMA((6,)),
            pltpu.SemaphoreType.DMA((6,)),
            pltpu.SemaphoreType.DMA((8,)),
            pltpu.SemaphoreType.DMA((8,)),
            pltpu.SemaphoreType.DMA((3,)),
            pltpu.SemaphoreType.DMA((10,)),
            pltpu.SemaphoreType.DMA((3,)),
        ],
        compiler_params=pltpu.CompilerParams(
            collective_id=2, has_side_effects=True, vmem_limit_bytes=61 * 1024 * 1024
        ),
        name="ffn",
    )(own, slopes, picks, router, gate, up, down)


class ChipSums:
    def __init__(self, remote, blocks, near, far, sems, rows):
        self.blocks, self.near, self.far, self.rows = blocks, near, far, rows
        self.remote = remote
        self.near_send, self.near_recv, self.sum_send, self.sum_recv = sems
        self.hops = {}
        size = rows // 2
        for slot, (key, block, half, mask) in enumerate(
            (
                ("x2", 2, 0, 2),
                ("x6", 6, 0, 2),
                ("y4", 4, 1, 4),
                ("y6", 6, 1, 4),
                ("then_y", 4, 0, 4),
                ("then_x", 2, 1, 2),
            )
        ):
            self.hops[key] = (
                remote(
                    halves(blocks, block, rows, half),
                    far.at[pl.ds(slot * size, size)],
                    self.sum_send.at[slot],
                    self.sum_recv.at[slot],
                    mask,
                ),
                slot * size,
            )

    def across(self, chip):
        return self.remote(
            whole(self.blocks, 2 * chip + 1, self.rows),
            whole(self.near, chip, self.rows),
            self.near_send.at[chip],
            self.near_recv.at[chip],
            1,
        )

    def add(self, start, other, other_start, count):
        piece = 48 if count % 48 == 0 else 32

        def one(step, carry):
            at = pl.ds(pl.multiple_of(start + step * piece, 16), piece)
            have = pl.ds(pl.multiple_of(other_start + step * piece, 16), piece)
            self.blocks[at] = (self.blocks[at].astype(f32) + other[have].astype(f32)).astype(bf16)
            return carry

        lax.fori_loop(0, count // piece, one, 0)

    def join(self, chip):
        self.across(chip).wait_recv()
        self.add(2 * chip * self.rows, self.near, chip * self.rows, self.rows)

    def begin(self, key):
        self.hops[key][0].start()

    def settle(self, chip):
        self.join(chip)

        @pl.when(chip == 1)
        def _():
            self.begin("x2")

        @pl.when(chip == 2)
        def _():
            self.begin("y4")

        @pl.when(chip == 3)
        def _():
            self.begin("x6")
            self.begin("y6")

    def add_far(self, block, half, key):
        size = self.rows // 2
        copy, place = self.hops[key]
        copy.wait_recv()
        self.add(block * self.rows + half * size, self.far, place, size)

    def cross(self):
        self.add_far(4, 0, "x6")
        self.begin("then_y")
        self.add_far(2, 1, "y6")
        self.begin("then_x")
        self.add_far(0, 0, "x2")
        self.add_far(0, 1, "y4")

    def close(self):
        self.add_far(0, 0, "then_y")
        self.add_far(0, 1, "then_x")

    def drain(self):
        for copy, place in self.hops.values():
            copy.wait_send()
        for chip in range(4):
            self.across(chip).wait_send()


def turned_pair(index, other, bits):
    result = index
    for bit in bits:
        on = (other // bit) % 2
        result = result + on * bit * (1 - 2 * ((index // bit) % 2))
    return result


def back_kernel(
    grad_in,
    rows_in,
    place_ref,
    cos_far,
    sin_far,
    cos_near,
    sin_near,
    weight_ref,
    query_in,
    key_in,
    value_in,
    mixture_in,
    query_weight,
    back_out,
    key_out,
    value_out,
    output_sum,
    query_part,
    query_out,
    grad_ref,
    rows_ref,
    query_ref,
    key_ref,
    value_ref,
    mixture_ref,
    grad_hold,
    query_hold,
    back_hold,
    weights,
    key_part,
    value_part,
    key_got,
    value_got,
    key_pass,
    value_pass,
    total_hold,
    result_hold,
    output_blocks,
    output_near,
    output_far,
    query_blocks,
    output_near_send,
    output_near_recv,
    output_sum_send,
    output_sum_recv,
    query_save,
    got_send,
    got_recv,
    pass_send,
    pass_recv,
    load_sem,
    intake_sem,
):
    group = lax.axis_index("dp")
    mine = lax.axis_index("expert")
    experts = 4
    side = mine // 2
    edge = ((mine + 1) % experts) // 2 == 0
    bits = (1, 2, 4)
    peers = {mask: (flips(group, mask, bits), mine) for mask in (1, 2, 4)}
    intake = [
        pltpu.make_async_copy(source, target, intake_sem.at[number])
        for number, (source, target) in enumerate(
            (
                (grad_in, grad_ref),
                (mixture_in, mixture_ref),
                (query_in, query_ref),
                (key_in, key_ref),
                (value_in, value_ref),
                (rows_in, rows_ref),
            )
        )
    ]
    for copy in intake:
        copy.start()
    barrier(
        [peers[mask] for mask in (1, 2, 4)]
        + [(group, (mine + step) % experts) for step in range(1, experts)]
    )

    def remote(source, target, send, recv, mask):
        return pltpu.make_async_remote_copy(
            src_ref=source,
            dst_ref=target,
            send_sem=send,
            recv_sem=recv,
            device_id=peers[mask],
            device_id_type=MESH,
        )

    rows_all, depth = grad_ref.shape
    tokens = key_ref.shape[0]
    capacity = rows_all // experts
    seq_len = tokens // experts
    tile = 256
    contract = (((1,), (1,)), ((), ()))
    stack = (((0,), (0,)), ((), ()))
    scale = HEAD ** (-0.5)
    outputs = ChipSums(
        remote,
        output_blocks,
        output_near,
        output_far,
        (output_near_send, output_near_recv, output_sum_send, output_sum_recv),
        tile,
    )
    def owner_of(number):
        near_end = 2 - side
        far_end = 3 - 3 * side
        return jnp.where(
            number == 0,
            jnp.where(edge, near_end, far_end),
            jnp.where(
                number == 1,
                jnp.where(edge, far_end, near_end),
                jnp.where(number == 2, 1 + 4 * side - mine, mine),
            ),
        )

    def chip_of(owner):
        return turned_pair(owner, group // 2, (1, 2))

    def load(step):
        at = pl.multiple_of((2 * owner_of(step // 2) + step % 2) * tile, tile)
        return pltpu.make_async_copy(
            weight_ref.at[pl.ds(at, tile)], weights.at[step % 2], load_sem.at[step % 2]
        )

    def part_at(owner):
        return pl.ds(pl.multiple_of(owner * tokens, tokens), tokens)

    def give(owner):
        return [
            pltpu.make_async_remote_copy(
                src_ref=part.at[part_at(owner)],
                dst_ref=got.at[part_at(mine)],
                send_sem=got_send.at[owner, number],
                recv_sem=got_recv.at[mine, number],
                device_id=(group, owner),
                device_id_type=MESH,
            )
            for number, (part, got) in enumerate(
                ((key_part, key_got), (value_part, value_got))
            )
        ]

    def got_from(source):
        return [
            pltpu.make_async_remote_copy(
                src_ref=part.at[part_at(source)],
                dst_ref=got.at[part_at(source)],
                send_sem=got_send.at[source, number],
                recv_sem=got_recv.at[source, number],
                device_id=(group, source),
                device_id_type=MESH,
            )
            for number, (part, got) in enumerate(
                ((key_part, key_got), (value_part, value_got))
            )
        ]

    def hand_on(target):
        return [
            pltpu.make_async_remote_copy(
                src_ref=part.at[part_at(2 - side)],
                dst_ref=pile,
                send_sem=pass_send.at[number],
                recv_sem=pass_recv.at[number],
                device_id=(group, target),
                device_id_type=MESH,
            )
            for number, (part, pile) in enumerate(
                ((key_part, key_pass), (value_part, value_pass))
            )
        ]

    load(0).start()
    for copy in intake:
        copy.wait()
    block_slices = blocks_of(experts, rows_all, tokens, tile)
    spots = lax.broadcasted_iota(jnp.int32, (rows_all, seq_len), 1)

    def one(step, carry):
        owner = owner_of(step // 2)
        parity = step % 2
        number = 2 * owner + parity
        chip = chip_of(owner)
        load(step).wait()

        @pl.when(step < 7)
        def _():
            load(step + 1).start()

        columns = pl.ds(pl.multiple_of(number * tile, tile), tile)
        block = turned_pair(number, group, bits)
        block_at = pl.ds(pl.multiple_of(block * tile, tile), tile)
        grad_hold[...] = (
            lax.dot_general(
                grad_ref[...], weights[parity], contract, preferred_element_type=f32
            )
            .astype(bf16)
            .astype(f32)
        )
        output_blocks[block_at] = lax.dot_general(
            mixture_ref[:, columns], grad_ref[...], stack, preferred_element_type=f32
        ).astype(bf16)

        @pl.when((parity == 1) & (step > 1))
        def _():
            outputs.settle(chip_of(owner_of(step // 2 - 1)))

        query_hold[...] = query_ref[:, columns].astype(f32)
        keys_tile = key_ref[:, columns]
        values_tile = value_ref[:, columns]
        queries = [query_hold[rows, cut].astype(bf16) for rows, keys, cut in block_slices]
        grads = [grad_hold[rows, cut].astype(bf16) for rows, keys, cut in block_slices]
        scores = jnp.concatenate(
            [
                lax.dot_general(query, keys_tile[keys, cut], contract, preferred_element_type=f32)
                for query, (rows, keys, cut) in zip(queries, block_slices)
            ],
            axis=0,
        )
        grad_probs = jnp.concatenate(
            [
                lax.dot_general(grad, values_tile[keys, cut], contract, preferred_element_type=f32)
                for grad, (rows, keys, cut) in zip(grads, block_slices)
            ],
            axis=0,
        )
        seen = spots <= place_ref[...]
        probs = softmax_all(scores, jnp.concatenate([seen] * (tile // HEAD), axis=0))
        inner = jnp.sum(probs * grad_probs, axis=-1, keepdims=True)
        slopes = probs * (grad_probs - inner)
        for count, (rows, keys, cut) in enumerate(block_slices):
            own = slice(count * capacity, (count + 1) * capacity)
            slope = slopes[own].astype(bf16)
            token_at = pl.ds(
                pl.multiple_of(owner * tokens + keys.start, seq_len), seq_len
            )
            lanes = pl.ds(pl.multiple_of(parity * tile + cut.start, HEAD), HEAD)
            value_part[token_at, lanes] = lax.dot_general(
                probs[own].astype(bf16), grads[count], stack, preferred_element_type=f32
            ).astype(bf16)
            key_part[token_at, lanes] = (
                lax.dot_general(slope, queries[count], stack, preferred_element_type=f32) * scale
            ).astype(bf16)
            back_hold[rows, cut] = (
                jnp.dot(slope, keys_tile[keys, cut], preferred_element_type=f32) * scale
            )
        for head in range(tile // HEAD):
            cut = slice(head * HEAD, (head + 1) * HEAD)
            lanes = pl.ds(pl.multiple_of(number * tile + head * HEAD, HEAD), HEAD)
            query_out[:, lanes] = turn(back_hold[:, cut], cos_far[...], -sin_far[...]).astype(bf16)

        @pl.when(parity == 1)
        def _():
            outputs.across(chip).start()

            @pl.when((step == 1) & edge)
            def _():
                for copy in hand_on(1 + side):
                    copy.start()

            @pl.when(((step == 1) | (step == 5)) & jnp.logical_not(edge))
            def _():
                for copy in give(owner):
                    copy.start()

        return carry

    lax.fori_loop(0, 8, one, 0)

    def keep(number):
        at = pl.ds(pl.multiple_of(number * tile, tile), tile)
        return pltpu.make_async_copy(query_blocks.at[at], query_part.at[at], query_save.at[number])

    def project(number, carry):
        at = pl.ds(pl.multiple_of(number * tile, tile), tile)
        query_blocks[at] = lax.dot_general(
            rows_ref[:, at], query_out[...], stack, preferred_element_type=f32
        ).astype(bf16)
        keep(number).start()
        return carry

    lax.fori_loop(0, 8, project, 0)
    outputs.settle(chip_of(mine))

    def stream(step):
        at = pl.multiple_of(step * tile, tile)
        return pltpu.make_async_copy(
            query_weight.at[pl.ds(at, tile)], weights.at[step % 2], load_sem.at[step % 2]
        )

    stream(0).start()

    def rows_back(step, carry):
        stream(step).wait()

        @pl.when(step < depth // tile - 1)
        def _():
            stream(step + 1).start()

        cut = pl.ds(pl.multiple_of(step * tile, tile), tile)
        back_out[:, cut] = lax.dot_general(
            query_out[...], weights[step % 2], contract, preferred_element_type=f32
        ).astype(bf16)
        return carry

    @pl.when(edge)
    def _():
        for copy in hand_on(1 + side):
            copy.wait_send()
        for owner in (3 - 3 * side, 1 + 4 * side - mine):
            for copy in give(owner):
                copy.start()

    lax.fori_loop(0, depth // tile, rows_back, 0)
    piece = 32

    @pl.when(jnp.logical_not(edge))
    def _():
        for (part, pile), copy in zip(
            ((key_part, key_pass), (value_part, value_pass)), hand_on(1 + side)
        ):
            copy.wait_recv()

            def add(step, carry):
                at = pl.ds(pl.multiple_of((2 - side) * tokens + step * piece, piece), piece)
                other = pl.ds(pl.multiple_of(step * piece, piece), piece)
                part[at] = (part[at].astype(f32) + pile[other].astype(f32)).astype(bf16)
                return carry

            lax.fori_loop(0, tokens // piece, add, 0)
        for copy in give(2 - side):
            copy.start()

    def deliver(sums, result):
        half_tile = tile // 2
        for half in range(2):

            def one(step, carry):
                at = pl.ds(pl.multiple_of(step * piece, piece), piece)
                source = pl.ds(pl.multiple_of(half * half_tile + step * piece, piece), piece)
                result_hold[at] = sums.blocks[source].astype(f32)
                return carry

            lax.fori_loop(0, half_tile // piece, one, 0)
            copy = pltpu.make_async_copy(
                result_hold, result.at[pl.ds(half * half_tile, half_tile)], load_sem.at[0]
            )
            copy.start()
            copy.wait()

    outputs.cross()
    outputs.close()
    deliver(outputs, output_sum)

    def expected(source):
        far_end = (mine + 2) % experts
        middle = ((mine + 1) % experts) // 2 == 1
        return jnp.logical_not(middle & (source == far_end))

    def gather(number, part, got):
        def first(step, carry):
            at = pl.ds(pl.multiple_of(mine * tokens + step * piece, piece), piece)
            where = pl.ds(pl.multiple_of(step * piece, piece), piece)
            total_hold[where] = part[at].astype(f32)
            return carry

        lax.fori_loop(0, tokens // piece, first, 0)
        for hop in range(1, experts):
            source = (mine + hop) % experts

            @pl.when(expected(source))
            def _():
                got_from(source)[number].wait_recv()

                def add(step, carry):
                    at = pl.ds(pl.multiple_of(source * tokens + step * piece, piece), piece)
                    where = pl.ds(pl.multiple_of(step * piece, piece), piece)
                    total_hold[where] = total_hold[where] + got[at].astype(f32)
                    return carry

                lax.fori_loop(0, tokens // piece, add, 0)

    gather(1, value_part, value_got)
    value_out[...] = total_hold[...].astype(bf16)
    gather(0, key_part, key_got)
    for head in range(key_out.shape[1] // HEAD):
        cut = slice(head * HEAD, (head + 1) * HEAD)
        key_out[:, cut] = turn(total_hold[:, cut], cos_near[...], -sin_near[...]).astype(bf16)

    @pl.when(jnp.logical_not(edge))
    def _():
        for copy in give(2 - side):
            copy.wait_send()

    for owner in (3 - 3 * side, 1 + 4 * side - mine):
        for copy in give(owner):
            copy.wait_send()
    outputs.drain()

    def kept(number, carry):
        keep(number).wait()
        return carry

    lax.fori_loop(0, 8, kept, 0)


def back_call(
    grad_rows, rows_flat, places, far, near, output_w, query, key, value, mixture, query_w
):
    rows, depth = grad_rows.shape
    tokens, heads_width = key.shape
    own = heads_width // 4
    tile = 256
    vmem = pl.BlockSpec(memory_space=pltpu.VMEM)

    def dma(*shape):
        return pltpu.SemaphoreType.DMA(shape)

    def blocks(count):
        return pltpu.VMEM((count * tile, depth), bf16)

    return pl.pallas_call(
        back_kernel,
        out_shape=[
            jax.ShapeDtypeStruct((rows, depth), bf16),
            jax.ShapeDtypeStruct((tokens, own), bf16),
            jax.ShapeDtypeStruct((tokens, own), bf16),
            jax.ShapeDtypeStruct((tile, depth), f32),
            jax.ShapeDtypeStruct((depth, heads_width), bf16),
        ],
        in_specs=[ANY] * 2 + [vmem] * 5 + [ANY] * 6,
        out_specs=[vmem] * 3 + [ANY] * 2,
        scratch_shapes=[
            pltpu.VMEM((rows, heads_width), bf16),
            pltpu.VMEM((rows, depth), bf16),
            pltpu.VMEM((rows, depth), bf16),
            pltpu.VMEM((rows, heads_width), bf16),
            pltpu.VMEM((tokens, heads_width), bf16),
            pltpu.VMEM((tokens, heads_width), bf16),
            pltpu.VMEM((rows, heads_width), bf16),
            pltpu.VMEM((rows, tile), f32),
            pltpu.VMEM((rows, tile), f32),
            pltpu.VMEM((rows, tile), f32),
            pltpu.VMEM((2, tile, depth), bf16),
            pltpu.VMEM((4 * tokens, own), bf16),
            pltpu.VMEM((4 * tokens, own), bf16),
            pltpu.VMEM((4 * tokens, own), bf16),
            pltpu.VMEM((4 * tokens, own), bf16),
            pltpu.VMEM((tokens, own), bf16),
            pltpu.VMEM((tokens, own), bf16),
            pltpu.VMEM((tokens, own), f32),
            pltpu.VMEM((tile // 2, depth), f32),
            blocks(8),
            blocks(4),
            blocks(3),
            blocks(8),
            dma(4),
            dma(4),
            dma(6),
            dma(6),
            dma(8),
            dma(4, 2),
            dma(4, 2),
            dma(2),
            dma(2),
            dma(2),
            dma(6),
        ],
        compiler_params=pltpu.CompilerParams(
            collective_id=3, has_side_effects=True, vmem_limit_bytes=61 * 1024 * 1024
        ),
        cost_estimate=pl.CostEstimate(
            flops=60_000_000_000, bytes_accessed=200_000_000, transcendentals=0
        ),
        name="attend_back_sums",
    )(
        grad_rows,
        rows_flat,
        places,
        *far,
        *near,
        output_w,
        query,
        key,
        value,
        mixture,
        query_w,
    )


def start_kernel(
    home,
    attn_gain,
    moe_gain,
    attn_router,
    moe_router,
    attn_choice,
    moe_choice,
    lengths,
    cos_home,
    sin_home,
    given,
    value_shard,
    key_shard,
    query_shard,
    output_shard,
    small_full,
    told_full,
    table_out,
    place_out,
    cos_far,
    sin_far,
    attn_table,
    moe_table,
    normed_out,
    rows_out,
    query_out,
    key_out,
    value_out,
    mixture_out,
    branch_out,
    value_own,
    key_own,
    query_full,
    output_full,
    given_out,
    inputs,
    small_own,
    told_own,
    small_hold,
    normed,
    rows_hold,
    query_hold,
    query_low,
    keys,
    values,
    chances,
    mixture,
    branch,
    given_hold,
    value_stage,
    key_stage,
    query_stage,
    output_stage,
    value_buf,
    key_buf,
    query_buf,
    output_buf,
    load_sem,
    far_send,
    far_recv,
    near_send,
    near_recv,
    home_send,
    home_recv,
    small_send,
    small_recv,
    told_send,
    told_recv,
    heads_send,
    heads_recv,
    given_send,
    given_recv,
    save_sem,
):
    group = lax.axis_index("dp")
    mine = lax.axis_index("expert")
    experts = 4
    bits = (1, 2, 4)
    peers = {mask: (flips(group, mask, bits), mine) for mask in range(1, 8)}
    others = [(mine + hop) % experts for hop in range(1, experts)]
    seq_len, depth = home.shape
    expert_rows = rows_out.shape[0]
    capacity = expert_rows // experts
    tokens = experts * seq_len
    extent = key_shard.shape[0]
    half_extent = extent // 2
    own_width = value_buf.shape[1]
    heads_width = key_buf.shape[1]
    tile = 256
    shards = (value_shard, key_shard, query_shard, output_shard)
    stages = (value_stage, key_stage, query_stage, output_stage)
    buffers = (value_buf, key_buf, query_buf, output_buf)
    loads = []
    for which in range(4):
        source = shards[which]
        if which == 0:
            source = source.at[:, pl.ds(pl.multiple_of(mine * own_width, own_width), own_width)]
        loads.append(pltpu.make_async_copy(source, stages[which], load_sem.at[which]))
    seat = pltpu.make_async_copy(home, inputs.at[mine], load_sem.at[4])
    for copy in loads:
        copy.start()
    seat.start()

    small_hold[...] = jnp.zeros_like(small_hold)
    small_hold[0:1] = attn_gain[...]
    small_hold[1:2] = moe_gain[...]
    small_hold[2 : 2 + experts] = attn_router[...]
    small_hold[2 + experts : 2 + 2 * experts] = moe_router[...]
    small_own[...] = small_hold[...].astype(bf16)
    lane = lax.broadcasted_iota(jnp.int32, (experts, seq_len), 1)
    live = lane < lengths[...]
    told_own[0:experts] = jnp.where(live, moe_choice[0], -1).astype(f32)
    told_own[experts : 2 * experts] = jnp.where(live, moe_choice[1], -1).astype(f32)
    barrier([peers[mask] for mask in range(1, 8)] + [(group, other) for other in others])

    def remote(source, target, send, recv, device):
        return pltpu.make_async_remote_copy(
            src_ref=source,
            dst_ref=target,
            send_sem=send,
            recv_sem=recv,
            device_id=device,
            device_id_type=MESH,
        )

    small_at = pl.ds(pl.multiple_of(group * extent, extent), extent)
    told_at = pl.ds(pl.multiple_of(group * 2 * experts, 2 * experts), 2 * experts)
    smalls = []
    for mask in range(1, 8):
        smalls.append(
            remote(
                small_own,
                small_full.at[:, small_at],
                small_send.at[mask],
                small_recv.at[mask],
                peers[mask],
            )
        )
        smalls.append(
            remote(
                told_own,
                told_full.at[told_at],
                told_send.at[mask],
                told_recv.at[mask],
                peers[mask],
            )
        )
    homes = [
        remote(home, inputs.at[mine], home_send.at[hop], home_recv.at[hop], (group, other))
        for hop, other in enumerate(others)
    ]
    for copy in smalls + homes:
        copy.start()
    small_full[:, small_at] = small_own[...]
    told_full[told_at] = told_own[...]

    def piece(which, mask, half):
        start = flips(group, mask, bits) * extent + half * half_extent
        return buffers[which].at[pl.ds(pl.multiple_of(start, half_extent), half_extent)]

    def block(which, mask):
        start = flips(group, mask, bits) * extent
        return buffers[which].at[pl.ds(pl.multiple_of(start, extent), extent)]

    far = {}
    near = {}
    for which in range(4):
        for slot, (mask, half, towards) in enumerate(
            ((0, 0, 2), (0, 1, 2), (0, 1, 4), (0, 0, 4), (2, 0, 4), (4, 1, 2))
        ):
            far[which, slot] = remote(
                piece(which, mask, half),
                piece(which, mask, half),
                far_send.at[which, slot],
                far_recv.at[which, slot],
                peers[towards],
            )
        for chip in range(4):
            near[which, chip] = remote(
                block(which, 2 * chip),
                block(which, 2 * chip),
                near_send.at[which, chip],
                near_recv.at[which, chip],
                peers[1],
            )

    def convert(which):
        loads[which].wait()
        count = 32

        def one(step, carry):
            at = pl.ds(pl.multiple_of(step * count, count), count)
            to = pl.ds(pl.multiple_of(group * extent + step * count, count), count)
            buffers[which][to] = stages[which][at].astype(bf16)
            return carry

        lax.fori_loop(0, extent // count, one, 0)

    def leave(which):
        for slot in (0, 2, 1, 3):
            far[which, slot].start()
        near[which, 0].start()

    def pass_on(which):
        far[which, 0].wait_recv()
        far[which, 4].start()
        far[which, 2].wait_recv()
        far[which, 5].start()

    def spread(which):
        far[which, 1].wait_recv()
        near[which, 1].start()
        far[which, 3].wait_recv()
        near[which, 2].start()
        far[which, 4].wait_recv()
        far[which, 5].wait_recv()
        near[which, 3].start()

    def complete(which):
        for chip in range(4):
            near[which, chip].wait_recv()

    convert(0)
    leave(0)
    convert(1)
    leave(1)

    chosen = ((attn_choice[0] == mine) | (attn_choice[1] == mine)) & live
    picked = chosen.astype(f32)
    early = lax.broadcasted_iota(jnp.int32, (seq_len, seq_len), 0)
    late = lax.broadcasted_iota(jnp.int32, (seq_len, seq_len), 1)
    until = (early <= late).astype(f32)
    seats = lax.broadcasted_iota(jnp.int32, (capacity, seq_len), 0).astype(f32) + 1.0
    spot = lax.broadcasted_iota(jnp.int32, (capacity, seq_len), 1).astype(f32)

    def seated(taken):
        slot_of = jnp.dot(taken, until, preferred_element_type=f32)
        return [
            ((slot_of[row : row + 1] == seats) & (taken[row : row + 1] > 0.0)).astype(f32)
            for row in range(experts)
        ]

    tables = seated(picked)
    row_of = lax.broadcasted_iota(jnp.int32, (experts, seq_len), 0)

    def own_row(value):
        return jnp.sum(jnp.where(row_of == mine, value, 0), axis=0, keepdims=True)

    own_live = lane < own_row(jnp.broadcast_to(lengths[...], (experts, seq_len)))
    for choice, table_ref in ((attn_choice, attn_table), (moe_choice, moe_table)):
        goes = ((own_row(choice[0]) == row_of) | (own_row(choice[1]) == row_of)) & own_live
        table_ref[...] = jnp.concatenate(seated(goes.astype(f32)), axis=0).astype(bf16)
    for other in range(experts):
        given_hold[other] = jnp.dot(
            moe_table[other * capacity : (other + 1) * capacity],
            given[...],
            preferred_element_type=f32,
        ).astype(bf16)
    empty = jnp.zeros((capacity, seq_len), f32)
    table_out[...] = jnp.concatenate(
        [
            jnp.concatenate(
                [tables[seq] if seq == other else empty for other in range(experts)], axis=1
            )
            for seq in range(experts)
        ],
        axis=0,
    ).astype(bf16)
    place_out[...] = jnp.concatenate(
        [jnp.sum(table * spot, axis=1, keepdims=True) for table in tables], axis=0
    ).astype(jnp.int32)
    stacked = jnp.concatenate(tables, axis=0)
    vacant = 1.0 - jnp.sum(stacked, axis=1, keepdims=True)
    cos_far[...] = vacant + jnp.dot(
        stacked, cos_home[...], precision=highest, preferred_element_type=f32
    )
    sin_far[...] = jnp.dot(stacked, sin_home[...], precision=highest, preferred_element_type=f32)

    pass_on(0)
    convert(2)
    pass_on(1)
    leave(2)
    convert(3)
    spread(0)
    complete(0)
    spread(1)

    seat.wait()
    for copy in smalls:
        copy.wait_recv()
    gain = small_full[0:1].astype(f32)
    for hop in range(experts):
        source = (mine + experts - hop) % experts
        if hop > 0:
            homes[hop - 1].wait_recv()
        count = 32

        def one(step, carry):
            at = pl.ds(pl.multiple_of(step * count, count), count)
            to = pl.ds(pl.multiple_of(source * seq_len + step * count, count), count)
            value = inputs[source, at].astype(f32)
            normed[to] = (value * norm_scale(value) * gain).astype(bf16)
            return carry

        lax.fori_loop(0, seq_len // count, one, 0)
    own_at = pl.ds(pl.multiple_of(mine * own_width, own_width), own_width)
    values[:, own_at] = jnp.dot(
        normed[...], value_buf[...], preferred_element_type=f32
    ).astype(bf16)
    heads = [
        remote(
            values.at[:, own_at],
            values.at[:, own_at],
            heads_send.at[hop],
            heads_recv.at[hop],
            (group, other),
        )
        for hop, other in enumerate(others)
    ]
    for copy in heads:
        copy.start()
    rows_hold[...] = jnp.dot(table_out[...], normed[...], preferred_element_type=f32).astype(bf16)
    saves = [
        pltpu.make_async_copy(normed, normed_out, save_sem.at[0]),
        pltpu.make_async_copy(rows_hold, rows_out, save_sem.at[1]),
        pltpu.make_async_copy(value_buf, value_own, save_sem.at[2]),
    ]
    for copy in saves:
        copy.start()

    def save(source, target, number):
        copy = pltpu.make_async_copy(source, target, save_sem.at[number])
        copy.start()
        saves.append(copy)

    complete(1)
    save(key_buf.at[:, own_at], key_own, 3)

    def make_keys(step, carry):
        cut = pl.ds(pl.multiple_of(step * tile, tile), tile)
        made = jnp.dot(normed[...], key_buf[:, cut], preferred_element_type=f32)
        for head in range(tile // HEAD):
            lanes = pl.ds(pl.multiple_of(step * tile + head * HEAD, HEAD), HEAD)
            part = made[:, head * HEAD : (head + 1) * HEAD]
            for seq in range(experts):
                rows = slice(seq * seq_len, (seq + 1) * seq_len)
                keys[rows, lanes] = turn(part[rows], cos_home[...], sin_home[...]).astype(bf16)
        return carry

    lax.fori_loop(0, heads_width // tile, make_keys, 0)
    save(keys, key_out, 4)
    pass_on(2)
    leave(3)
    spread(2)
    complete(2)
    save(query_buf, query_full, 5)

    blocks = blocks_of(experts, expert_rows, tokens, tile)
    contract = (((1,), (1,)), ((), ()))
    spots = lax.broadcasted_iota(jnp.int32, (expert_rows, seq_len), 1)
    span_rows = len(blocks) * capacity

    def make_chances(step, carry):
        cut = pl.ds(pl.multiple_of(step * tile, tile), tile)
        made = jnp.dot(rows_hold[...], query_buf[:, cut], preferred_element_type=f32)
        for head in range(tile // HEAD):
            part = slice(head * HEAD, (head + 1) * HEAD)
            query_hold[:, part] = turn(made[:, part], cos_far[...], sin_far[...])
        query_low[:, cut] = query_hold[...].astype(bf16)
        tile_keys = keys[:, cut]
        scores = jnp.concatenate(
            [
                lax.dot_general(
                    query_hold[rows, lanes].astype(bf16),
                    tile_keys[spans, lanes],
                    contract,
                    preferred_element_type=f32,
                )
                for rows, spans, lanes in blocks
            ],
            axis=0,
        )
        seen = spots <= place_out[...]
        probs = softmax_all(scores, jnp.concatenate([seen] * (tile // HEAD), axis=0))
        chances[pl.ds(pl.multiple_of(step * span_rows, 64), span_rows)] = probs.astype(bf16)
        return carry

    lax.fori_loop(0, heads_width // tile, make_chances, 0)
    save(query_low, query_out, 6)
    pass_on(3)
    for copy in heads:
        copy.wait_recv()
    givens = [
        remote(
            given_hold.at[other],
            given_out.at[mine],
            given_send.at[hop],
            given_recv.at[hop],
            (group, other),
        )
        for hop, other in enumerate(others)
    ]
    for copy in givens:
        copy.start()
    save(given_hold.at[mine], given_out.at[mine], 11)
    save(values, value_out, 7)

    def mix(step, carry):
        cut = pl.ds(pl.multiple_of(step * tile, tile), tile)
        tile_values = values[:, cut]
        probs = chances[pl.ds(pl.multiple_of(step * span_rows, 64), span_rows)].astype(f32)
        for count, (rows, spans, lanes) in enumerate(blocks):
            query_hold[rows, lanes] = jnp.dot(
                probs[count * capacity : (count + 1) * capacity].astype(bf16),
                tile_values[spans, lanes],
                preferred_element_type=f32,
            )
        mixture[:, cut] = query_hold[...].astype(bf16)
        return carry

    lax.fori_loop(0, heads_width // tile, mix, 0)
    save(mixture, mixture_out, 8)
    spread(3)
    complete(3)
    save(output_buf, output_full, 9)

    def project(step, carry):
        cut = pl.ds(pl.multiple_of(step * tile, tile), tile)
        branch[:, cut] = jnp.dot(
            mixture[...], output_buf[:, cut], preferred_element_type=f32
        ).astype(bf16)
        return carry

    lax.fori_loop(0, depth // tile, project, 0)
    save(branch, branch_out, 10)
    for copy in givens:
        copy.wait_recv()
    for copy in smalls + homes + heads + givens + list(far.values()) + list(near.values()):
        copy.wait_send()
    for copy in saves:
        copy.wait()


def start_call(
    home,
    attn_gain,
    moe_gain,
    attn_router,
    moe_router,
    attn_choice,
    moe_choice,
    lengths,
    near,
    given,
    value_weight,
    key_weight,
    query_weight,
    output_weight,
):
    experts = 4
    groups = 8
    seq_len, depth = home.shape
    extent, heads_width = key_weight.shape
    capacity = 2 * seq_len // experts + 8
    rows = experts * capacity
    tokens = experts * seq_len
    own_width = heads_width // experts
    small_room = -(-(2 + 2 * experts) // 16) * 16
    vmem = pl.BlockSpec(memory_space=pltpu.VMEM)

    def shaped(*shape, kind=bf16):
        return jax.ShapeDtypeStruct(shape, kind)

    def dma(*shape):
        return pltpu.SemaphoreType.DMA(shape)

    return pl.pallas_call(
        start_kernel,
        out_shape=[
            shaped(small_room, depth),
            shaped(groups * 2 * experts, seq_len, kind=f32),
            shaped(rows, tokens),
            shaped(rows, 1, kind=jnp.int32),
            shaped(rows, HEAD, kind=f32),
            shaped(rows, HEAD, kind=f32),
            shaped(rows, seq_len),
            shaped(rows, seq_len),
            shaped(tokens, depth),
            shaped(rows, depth),
            shaped(rows, heads_width),
            shaped(tokens, heads_width),
            shaped(tokens, heads_width),
            shaped(rows, heads_width),
            shaped(rows, depth),
            shaped(depth, own_width),
            shaped(depth, own_width),
            shaped(depth, heads_width),
            shaped(heads_width, depth),
            shaped(experts, capacity, depth),
        ],
        in_specs=[ANY] + [vmem] * 10 + [ANY] * 4,
        out_specs=[vmem] * 8 + [ANY] * 12,
        scratch_shapes=[
            pltpu.VMEM((experts, seq_len, depth), bf16),
            pltpu.VMEM((small_room, extent), bf16),
            pltpu.VMEM((2 * experts, seq_len), f32),
            pltpu.VMEM((small_room, extent), f32),
            pltpu.VMEM((tokens, depth), bf16),
            pltpu.VMEM((rows, depth), bf16),
            pltpu.VMEM((rows, 256), f32),
            pltpu.VMEM((rows, heads_width), bf16),
            pltpu.VMEM((tokens, heads_width), bf16),
            pltpu.VMEM((tokens, heads_width), bf16),
            pltpu.VMEM((rows * heads_width // HEAD, seq_len), bf16),
            pltpu.VMEM((rows, heads_width), bf16),
            pltpu.VMEM((rows, depth), bf16),
            pltpu.VMEM((experts, capacity, depth), bf16),
            pltpu.VMEM((extent, own_width), f32),
            pltpu.VMEM((extent, heads_width), f32),
            pltpu.VMEM((extent, heads_width), f32),
            pltpu.VMEM((extent, depth), f32),
            pltpu.VMEM((depth, own_width), bf16),
            pltpu.VMEM((depth, heads_width), bf16),
            pltpu.VMEM((depth, heads_width), bf16),
            pltpu.VMEM((heads_width, depth), bf16),
            dma(5),
            dma(4, 6),
            dma(4, 6),
            dma(4, 4),
            dma(4, 4),
            dma(3),
            dma(3),
            dma(8),
            dma(8),
            dma(8),
            dma(8),
            dma(3),
            dma(3),
            dma(3),
            dma(3),
            dma(12),
        ],
        compiler_params=pltpu.CompilerParams(
            collective_id=4, has_side_effects=True, vmem_limit_bytes=61 * 1024 * 1024
        ),
        cost_estimate=pl.CostEstimate(
            flops=100_000_000_000, bytes_accessed=300_000_000, transcendentals=0
        ),
        name="attend_start",
    )(
        home,
        attn_gain,
        moe_gain,
        attn_router,
        moe_router,
        attn_choice,
        moe_choice,
        lengths,
        *near,
        given,
        value_weight,
        key_weight,
        query_weight,
        output_weight,
    )


def start_plain(
    home,
    attn_gain,
    moe_gain,
    attn_router,
    moe_router,
    attn_choice,
    moe_choice,
    lengths,
    near,
    given,
    value_weight,
    key_weight,
    query_weight,
    output_weight,
):
    experts = lax.axis_size("expert")
    mine = lax.axis_index("expert")
    seq_len, depth = home.shape
    heads_width = key_weight.shape[1]
    own_width = heads_width // experts
    capacity = 2 * seq_len // experts + 8
    rows = experts * capacity
    kinds = 2 + 2 * experts
    small_own = jnp.concatenate(
        [
            attn_gain,
            moe_gain,
            attn_router,
            moe_router,
            jnp.zeros((-kinds % 16, attn_gain.shape[1]), f32),
        ]
    ).astype(bf16)
    places = jnp.arange(seq_len, dtype=jnp.int32)
    live = places[None] < lengths
    told = jnp.where(live, moe_choice, -1).astype(f32).reshape(2 * experts, seq_len)
    key_full, value_full, query_full, output_full, small_full, told_full, inputs = gather_all(
        [
            key_weight.astype(bf16),
            value_weight.astype(bf16),
            query_weight.astype(bf16),
            output_weight.astype(bf16),
            small_own,
            told,
        ],
        (2, 2, 2, 2, 1, 1),
        (0, 0, 0, 0, 1, 0),
        home,
    )

    def tables_of(choice):
        return jax.vmap(partial(route_table, experts=experts, capacity=capacity))(
            choice.transpose(1, 2, 0), lengths[:, 0]
        )

    attn_all, moe_all = tables_of(attn_choice), tables_of(moe_choice)
    group_table = lax.dynamic_index_in_dim(attn_all, mine, 1, keepdims=False)
    own_attn = lax.dynamic_index_in_dim(attn_all, mine, 0, keepdims=False).astype(bf16)
    own_moe = lax.dynamic_index_in_dim(moe_all, mine, 0, keepdims=False).astype(bf16)
    row_places = jnp.sum(jnp.where(group_table, places, 0), axis=-1).reshape(rows, 1)
    same = jnp.eye(experts, dtype=bool)[:, None, :, None]
    table = (group_table[:, :, None, :] & same).astype(bf16).reshape(rows, experts * seq_len)
    far = signed_tables(row_places[:, 0])
    all_near = tuple(jnp.tile(part, (experts, 1)) for part in near)
    normed, rows_flat, queries, keys, values, mixture = attend(
        experts,
        inputs.reshape(experts * seq_len, depth),
        small_full,
        table,
        row_places,
        far,
        all_near,
        query_full,
        key_full,
        value_full,
    )
    branch = jnp.dot(mixture, output_full, preferred_element_type=f32).astype(bf16)
    given_rows = jnp.einsum("ect,td->ecd", own_moe, given, preferred_element_type=f32)

    def own_heads(weight):
        return lax.dynamic_slice_in_dim(weight, mine * own_width, own_width, 1)

    return (
        small_full,
        told_full,
        table,
        row_places,
        *far,
        own_attn.reshape(rows, seq_len),
        own_moe.reshape(rows, seq_len),
        normed,
        rows_flat,
        queries,
        keys,
        values,
        mixture,
        branch,
        own_heads(value_full),
        own_heads(key_full),
        query_full,
        output_full,
        exchange(given_rows.astype(bf16)),
    )


def last_kernel(
    rows_in,
    table_in,
    key_in,
    value_in,
    grad_keys_in,
    grad_values_in,
    normed_in,
    home_out,
    key_out,
    value_out,
    rows_back,
    table_ref,
    key_own,
    value_own,
    grad_keys,
    grad_values,
    normed_ref,
    intake_sem,
    part,
    got,
    pile,
    blocks,
    near,
    far,
    swapped,
    near_send,
    near_recv,
    sum_send,
    sum_recv,
    got_send,
    got_recv,
    pass_send,
    pass_recv,
    swap_send,
    swap_recv,
):
    group = lax.axis_index("dp")
    mine = lax.axis_index("expert")
    experts = 4
    side = mine // 2
    edge = ((mine + 1) % experts) // 2 == 0
    bits = (1, 2, 4)
    peers = {mask: (flips(group, mask, bits), mine) for mask in (1, 2, 4)}
    others = [(mine + hop) % experts for hop in range(1, experts)]
    intake = [
        pltpu.make_async_copy(source, target, intake_sem.at[number])
        for number, (source, target) in enumerate(
            (
                (rows_in, rows_back),
                (table_in, table_ref),
                (grad_keys_in, grad_keys),
                (grad_values_in, grad_values),
                (key_in, key_own),
                (value_in, value_own),
                (normed_in, normed_ref),
            )
        )
    ]
    for copy in intake:
        copy.start()
    barrier([peers[mask] for mask in (1, 2, 4)] + [(group, other) for other in others])

    def send_to(device, source, target, send, recv):
        return pltpu.make_async_remote_copy(
            src_ref=source,
            dst_ref=target,
            send_sem=send,
            recv_sem=recv,
            device_id=device,
            device_id_type=MESH,
        )

    def remote(source, target, send, recv, mask):
        return send_to(peers[mask], source, target, send, recv)

    seq_len, depth = home_out.shape
    own_width = grad_keys.shape[1]
    tile = depth // 8
    contract = (((1,), (1,)), ((), ()))
    stack = (((0,), (0,)), ((), ()))
    sums = ChipSums(
        remote, blocks, near, far, (near_send, near_recv, sum_send, sum_recv), tile
    )

    def owner_of(number):
        near_end = 2 - side
        far_end = 3 - 3 * side
        return jnp.where(
            number == 0,
            jnp.where(edge, near_end, far_end),
            jnp.where(
                number == 1,
                jnp.where(edge, far_end, near_end),
                jnp.where(number == 2, 1 + 4 * side - mine, mine),
            ),
        )

    def give(owner):
        return send_to(
            (group, owner), part.at[owner], got.at[mine], got_send.at[owner], got_recv.at[mine]
        )

    def got_from(source):
        return send_to(
            (group, source),
            part.at[source],
            got.at[source],
            got_send.at[source],
            got_recv.at[source],
        )

    hand_on = send_to(
        (group, 1 + side), part.at[2 - side], pile, pass_send.at[0], pass_recv.at[0]
    )

    for copy in intake[:-1]:
        copy.wait()

    def one(step, carry):
        owner = owner_of(step)
        at = pl.ds(pl.multiple_of(owner * seq_len, seq_len), seq_len)
        part[owner] = (
            lax.dot_general(
                table_ref[:, at], rows_back[...], stack, preferred_element_type=f32
            )
            + lax.dot_general(
                grad_keys[at], key_own[...], contract, preferred_element_type=f32
            )
            + lax.dot_general(
                grad_values[at], value_own[...], contract, preferred_element_type=f32
            )
        ).astype(bf16)

        @pl.when((step == 0) & edge)
        def _():
            hand_on.start()

        @pl.when(((step == 0) | (step == 2)) & jnp.logical_not(edge))
        def _():
            give(owner).start()

        return carry

    lax.fori_loop(0, experts, one, 0)

    def project(block, carry):
        number = turned_pair(block, group, bits)
        columns = pl.ds(pl.multiple_of(number * tile, tile), tile)
        block_at = pl.ds(pl.multiple_of(block * tile, tile), tile)
        for half, value in enumerate((grad_keys, grad_values)):
            blocks[block_at, half * own_width : (half + 1) * own_width] = lax.dot_general(
                normed_ref[:, columns], value[...], stack, preferred_element_type=f32
            ).astype(bf16)

        @pl.when(block % 2 == 1)
        def _():
            sums.across(block // 2).start()

        return carry

    intake[-1].wait()
    lax.fori_loop(0, 8, project, 0)
    piece = 32

    @pl.when(edge)
    def _():
        hand_on.wait_send()
        for owner in (3 - 3 * side, 1 + 4 * side - mine):
            give(owner).start()

    def add_rows(target, start, source, other_start, count):
        def add(step, carry):
            at = pl.ds(pl.multiple_of(start + step * piece, piece), piece)
            have = pl.ds(pl.multiple_of(other_start + step * piece, piece), piece)
            target[at] = (target[at].astype(f32) + source[have].astype(f32)).astype(target.dtype)
            return carry

        lax.fori_loop(0, count // piece, add, 0)

    for chip in range(4):
        sums.settle(chip)

    @pl.when(jnp.logical_not(edge))
    def _():
        hand_on.wait_recv()
        add_rows(part.at[2 - side], 0, pile, 0, seq_len)
        give(2 - side).start()

    sums.cross()
    sums.close()
    share = tile // experts
    swaps = [
        send_to(
            (group, other),
            blocks.at[pl.ds(pl.multiple_of(other * share, share), share)],
            swapped.at[mine],
            swap_send.at[hop],
            swap_recv.at[hop],
        )
        for hop, other in enumerate(others)
    ]
    for copy in swaps:
        copy.start()

    def hand_out(source, value):
        at = pl.ds(pl.multiple_of(source * own_width, own_width), own_width)
        key_out[:, at] = value[:, :own_width].astype(f32)
        value_out[:, at] = value[:, own_width:].astype(f32)

    hand_out(mine, blocks[pl.ds(pl.multiple_of(mine * share, share), share)])
    for hop in range(1, experts):
        source = (mine + experts - hop) % experts
        swaps[hop - 1].wait_recv()
        hand_out(source, swapped[source])

    home_out[...] = part[mine].astype(f32)
    for hop in range(1, experts):
        source = (mine + hop) % experts
        middle = ((mine + 1) % experts) // 2 == 1

        @pl.when(jnp.logical_not(middle & (source == (mine + 2) % experts)))
        def _():
            got_from(source).wait_recv()

            def add(step, carry):
                at = pl.ds(pl.multiple_of(step * piece, piece), piece)
                home_out[at] = home_out[at] + got[source, at].astype(f32)
                return carry

            lax.fori_loop(0, seq_len // piece, add, 0)

    @pl.when(jnp.logical_not(edge))
    def _():
        give(2 - side).wait_send()

    for owner in (3 - 3 * side, 1 + 4 * side - mine):
        give(owner).wait_send()
    for copy in swaps:
        copy.wait_send()
    sums.drain()


def last_call(rows_back, table, key_own, value_own, grad_keys, grad_values, normed):
    rows = rows_back.shape[0]
    tokens, own = grad_keys.shape
    depth = normed.shape[1]
    experts = 4
    heads_width = own * experts
    seq_len = tokens // experts
    tile = depth // 8
    share = tile // experts
    vmem = pl.BlockSpec(memory_space=pltpu.VMEM)

    def dma(*shape):
        return pltpu.SemaphoreType.DMA(shape)

    def blocks(count):
        return pltpu.VMEM((count * tile, 2 * own), bf16)

    return pl.pallas_call(
        last_kernel,
        out_shape=[
            jax.ShapeDtypeStruct((seq_len, depth), f32),
            jax.ShapeDtypeStruct((share, heads_width), f32),
            jax.ShapeDtypeStruct((share, heads_width), f32),
        ],
        in_specs=[ANY] * 7,
        out_specs=[vmem] * 3,
        scratch_shapes=[
            pltpu.VMEM((rows, depth), bf16),
            pltpu.VMEM((rows, tokens), bf16),
            pltpu.VMEM((depth, own), bf16),
            pltpu.VMEM((depth, own), bf16),
            pltpu.VMEM((tokens, own), bf16),
            pltpu.VMEM((tokens, own), bf16),
            pltpu.VMEM((tokens, depth), bf16),
            dma(7),
            pltpu.VMEM((experts, seq_len, depth), bf16),
            pltpu.VMEM((experts, seq_len, depth), bf16),
            pltpu.VMEM((seq_len, depth), bf16),
            blocks(8),
            blocks(4),
            blocks(3),
            pltpu.VMEM((experts, share, 2 * own), bf16),
            dma(4),
            dma(4),
            dma(6),
            dma(6),
            dma(4),
            dma(4),
            dma(1),
            dma(1),
            dma(3),
            dma(3),
        ],
        compiler_params=pltpu.CompilerParams(
            collective_id=5, has_side_effects=True, vmem_limit_bytes=56 * 1024 * 1024
        ),
        cost_estimate=pl.CostEstimate(
            flops=40_000_000_000, bytes_accessed=150_000_000, transcendentals=0
        ),
        name="attend_last",
    )(rows_back, table, key_own, value_own, grad_keys, grad_values, normed)


def last_plain(rows_back, table, key_own, value_own, grad_keys, grad_values, normed):
    experts = lax.axis_size("expert")
    own_width = grad_keys.shape[1]
    depth = normed.shape[1]
    part = (
        jnp.einsum("rt,rd->td", table, rows_back, preferred_element_type=f32)
        + jnp.einsum("te,de->td", grad_keys, key_own, preferred_element_type=f32)
        + jnp.einsum("te,de->td", grad_values, value_own, preferred_element_type=f32)
    ).astype(bf16)
    home = jnp.sum(exchange(part.reshape(experts, -1, depth)).astype(f32), axis=0)
    both = jnp.einsum(
        "td,te->de",
        normed,
        jnp.concatenate([grad_keys, grad_values], axis=1),
        preferred_element_type=f32,
    ).astype(bf16)
    both = lax.psum_scatter(both, "dp", scatter_dimension=0, tiled=True)
    both = exchange(both.reshape(experts, -1, 2 * own_width))
    both = both.reshape(experts, -1, 2, own_width).transpose(2, 1, 0, 3).astype(f32)
    return home, both[0].reshape(-1, experts * own_width), both[1].reshape(
        -1, experts * own_width
    )


def ffn_plain(own, slopes, picks, router, gate, up, down):
    groups, rows, width = slopes.shape
    depth = own.shape[1]
    held = lax.all_gather(own, "dp", axis=0, tiled=True)
    logits = jnp.einsum("rd,ed->re", held, router, preferred_element_type=f32)
    weight = 1.0 / (1.0 + jnp.exp(jnp.sum(logits * picks, axis=-1, keepdims=True)))
    plain = slopes.reshape(groups * rows, width)
    gate_pre = jnp.einsum("rd,fd->rf", held, gate, preferred_element_type=f32)
    up_pre = jnp.einsum("rd,fd->rf", held, up, preferred_element_type=f32)
    sigmoid = 1.0 / (1.0 + jnp.exp(-gate_pre))
    active = gate_pre * sigmoid
    hidden = (active * up_pre).astype(bf16)
    wide = hidden.astype(f32)
    inner = weight * plain
    grad_gate = (inner * up_pre * (sigmoid * (1.0 + gate_pre * (1.0 - sigmoid)))).astype(bf16)
    grad_up = (inner * active).astype(bf16)
    made = jnp.dot(hidden, down, preferred_element_type=f32).astype(bf16)
    grads = (
        jnp.dot(grad_gate, gate, preferred_element_type=f32)
        + jnp.dot(grad_up, up, preferred_element_type=f32)
    ).astype(bf16)
    grads = lax.psum_scatter(
        grads.reshape(groups, rows, depth), "dp", scatter_dimension=0, tiled=True
    )[0]
    dense = lax.psum_scatter(
        jnp.sum(wide * plain, axis=-1).reshape(groups, rows),
        "dp",
        scatter_dimension=0,
        tiled=True,
    )

    def split(value):
        return value.reshape(groups, rows, value.shape[-1])

    upper = dense[0][:, None].astype(bf16)
    lower = (dense[0][:, None] - upper.astype(f32)).astype(bf16)
    grads = jnp.concatenate([grads, upper, lower, jnp.zeros((rows, 126), bf16)], axis=1)
    scaled = (weight * wide).astype(bf16)
    return (
        split(held),
        split(scaled),
        split(grad_gate),
        split(grad_up),
        split(made),
        grads,
    )


def back_plain(
    grad_rows, rows_flat, places, far, near, output_w, query, key, value, mixture, query_w
):
    experts = lax.axis_size("expert")
    grad_query, keys_part, values_part, output_part = attend_back(
        experts, grad_rows, places, far, output_w, query, key, value, mixture
    )
    output_sum = lax.psum_scatter(output_part, "dp", scatter_dimension=0, tiled=True)
    grad_values = jnp.sum(exchange(values_part).astype(f32), axis=0).astype(bf16)
    grad_keys = jnp.sum(exchange(keys_part).astype(f32), axis=0)
    grad_keys = jnp.concatenate(
        [
            turned_back(grad_keys[:, start : start + HEAD], near)
            for start in range(0, grad_keys.shape[1], HEAD)
        ],
        axis=1,
    ).astype(bf16)
    query_part = jnp.einsum("rd,re->de", rows_flat, grad_query, preferred_element_type=f32)
    rows_back = jnp.einsum("re,de->rd", grad_query, query_w, preferred_element_type=f32)
    return (
        rows_back.astype(bf16),
        grad_keys,
        grad_values,
        output_sum.astype(f32),
        query_part.astype(bf16),
    )


def exchange(value):
    return lax.all_to_all(value, "expert", split_axis=0, concat_axis=0, tiled=True)


def on_device(
    hidden_in,
    out_grad,
    seq_lengths,
    attn_choice,
    moe_choice,
    attn_gain,
    moe_gain,
    attn_router,
    moe_router,
    key_weight,
    value_weight,
    query_weight,
    output_weight,
    gate_weight,
    up_weight,
    down_weight,
):
    experts = lax.axis_size("expert")
    groups = lax.axis_size("dp")
    mine_index = lax.axis_index("expert")
    seq_len = hidden_in.shape[1]
    model_width = hidden_in.shape[2]
    head_width = query_weight.shape[2]
    own_width = head_width // experts
    capacity = 2 * seq_len // experts + 8
    expert_rows = experts * capacity
    total_rows = groups * expert_rows
    score_scale = HEAD ** (-0.5)
    places = jnp.arange(seq_len, dtype=jnp.int32)
    own_length = lax.dynamic_index_in_dim(seq_lengths, mine_index, 0, keepdims=False)
    live_rows = (places < own_length).astype(f32)
    own_attn = lax.dynamic_index_in_dim(attn_choice, mine_index, 0, keepdims=False)
    own_moe = lax.dynamic_index_in_dim(moe_choice, mine_index, 0, keepdims=False)
    kinds = 2 + 2 * experts
    ready = groups == 8 and experts == 4
    near_home = signed_tables(places)
    (
        small_full,
        told_full,
        spread_table,
        row_places,
        cos_far,
        sin_far,
        table_attn,
        table_moe,
        normed_group,
        rows_flat,
        queries,
        keys_all,
        values_all,
        mixture,
        attn_rows,
        value_own,
        key_own,
        query_full,
        output_full,
        given_rows,
    ) = (start_call if ready else start_plain)(
        hidden_in[0],
        attn_gain[None],
        moe_gain[None],
        attn_router.T,
        moe_router.T,
        attn_choice.transpose(2, 0, 1),
        moe_choice.transpose(2, 0, 1),
        seq_lengths[:, None],
        near_home,
        out_grad[0],
        value_weight,
        key_weight,
        query_weight[0],
        output_weight[0],
    )
    far = (cos_far, sin_far)
    near = tuple(jnp.tile(part, (experts, 1)) for part in near_home)
    table_attn = table_attn.reshape(experts, capacity, seq_len)
    table_moe = table_moe.reshape(experts, capacity, seq_len)
    given_all = lax.all_gather(
        given_rows.reshape(expert_rows, model_width), "dp", axis=0, tiled=True
    )
    attn_rows = attn_rows.reshape(experts, capacity, model_width)

    gain_attn = small_full[0].astype(f32)
    gain_moe = small_full[1].astype(f32)
    router_attn = small_full[2 : 2 + experts]
    router_moe = small_full[2 + experts : kinds]
    inputs_f = hidden_in[0].astype(f32)
    scale_one = norm_scale(inputs_f)
    normed_one = (inputs_f * scale_one * gain_attn).astype(bf16)
    attn_logits = jnp.einsum("td,ed->te", normed_one, router_attn, preferred_element_type=f32)
    onehot_attn, shares_attn, dense_attn = router_gates(attn_logits, own_attn, live_rows, experts)

    told = told_full.reshape(groups, 2, experts, seq_len).transpose(1, 0, 2, 3)
    told = told.reshape(2, groups * experts, seq_len).astype(jnp.int32)
    comes = (told[0] == mine_index) | (told[1] == mine_index)
    order = jnp.cumsum(comes.astype(jnp.int32), axis=1) - 1
    slots = jnp.arange(capacity, dtype=jnp.int32)[None, :, None]
    rivals = jnp.sum(
        jnp.where(
            (order[:, None, :] == slots) & comes[:, None, :],
            (told[0] + told[1] - mine_index)[:, None, :],
            0,
        ),
        axis=-1,
    ).reshape(total_rows, 1)
    back_attn = exchange(attn_rows)
    spread_attn = jnp.einsum("ect,ecd->etd", table_attn, back_attn, preferred_element_type=f32)
    attn_sum = jnp.sum(dense_attn.T[:, :, None] * spread_attn, axis=0)
    middle = inputs_f + attn_sum
    scale_two = norm_scale(middle)
    normed_two = (middle * scale_two * gain_moe).astype(bf16)
    moe_logits = jnp.einsum("td,ed->te", normed_two, router_moe, preferred_element_type=f32)
    onehot_moe, shares_moe, dense_moe = router_gates(moe_logits, own_moe, live_rows, experts)
    send_moe = jnp.einsum(
        "ect,td->ecd", table_moe, normed_two, preferred_element_type=f32
    ).astype(bf16)
    rows_moe = exchange(send_moe).reshape(expert_rows, model_width)

    units = gate_weight.shape[2]
    room = -(-units // 256) * 256
    gate_slice = jnp.pad(gate_weight[0].T.astype(bf16), ((0, room - units), (0, 0)))
    up_slice = jnp.pad(up_weight[0].T.astype(bf16), ((0, room - units), (0, 0)))
    down_slice = jnp.pad(down_weight[0].astype(bf16), ((0, room - units), (0, 0)))
    slopes = jnp.einsum("rd,fd->rf", given_all, down_slice, preferred_element_type=f32)
    expert_ids = jnp.arange(16, dtype=jnp.int32)[None, :]
    picks = (expert_ids == rivals).astype(f32) - (
        expert_ids == mine_index
    ).astype(f32)
    router_rows = jnp.pad(router_moe, ((0, 16 - experts), (0, 0)))
    feed = ffn_call if groups == 8 and expert_rows % 96 == 0 else ffn_plain
    ffn_rows, scaled, grad_gate, grad_up, partial_out, grad_ffn = feed(
        rows_moe,
        slopes.reshape(groups, expert_rows, room),
        picks,
        router_rows,
        gate_slice,
        up_slice,
        down_slice,
    )
    back_moe_grad = exchange(grad_ffn.reshape(experts, capacity, model_width + 128))
    summed_out = lax.psum_scatter(partial_out, "dp", scatter_dimension=0, tiled=True)
    ffn_rows = ffn_rows.reshape(total_rows, model_width)
    down_grad = jnp.einsum(
        "rf,rd->fd",
        scaled.reshape(total_rows, room)[:, :units],
        given_all,
        preferred_element_type=f32,
    )[None]
    gate_grad = jnp.einsum(
        "rd,rf->df",
        ffn_rows,
        grad_gate.reshape(total_rows, room)[:, :units],
        preferred_element_type=f32,
    )[None]
    up_grad = jnp.einsum(
        "rd,rf->df",
        ffn_rows,
        grad_up.reshape(total_rows, room)[:, :units],
        preferred_element_type=f32,
    )[None]
    back_moe_grad, down_grad, gate_grad = lax.optimization_barrier(
        (back_moe_grad, down_grad, gate_grad)
    )
    back_dense = jnp.sum(back_moe_grad[:, :, model_width:].astype(f32), axis=-1)
    back_moe_grad = back_moe_grad[:, :, :model_width]

    grad_out = out_grad[0].astype(f32) * live_rows[:, None]
    grad_dense_moe = jnp.sum(table_moe.astype(f32) * back_dense[:, :, None], axis=1).T
    grad_normed_two = jnp.einsum(
        "ect,ecd->td", table_moe, back_moe_grad, preferred_element_type=f32
    )
    grad_logits_moe = gates_backward(grad_dense_moe, onehot_moe, shares_moe, live_rows)
    grad_normed_two = grad_normed_two + jnp.dot(
        grad_logits_moe, router_moe.astype(f32), precision=highest
    )
    moe_router_part = jnp.dot(grad_logits_moe.T, normed_two.astype(f32), precision=highest)
    grad_middle_norm, moe_gain_part = norm_backward(grad_normed_two, middle, scale_two, gain_moe)
    grad_middle = grad_out + grad_middle_norm
    grad_dense_attn = jnp.sum(grad_middle[None] * spread_attn, axis=-1).T
    rows_attn_grad = (dense_attn.T[:, :, None] * grad_middle[None]).astype(bf16)
    send_attn_grad = jnp.einsum(
        "ect,etd->ecd", table_attn, rows_attn_grad, preferred_element_type=f32
    ).astype(bf16)
    recv_attn_grad = exchange(send_attn_grad)
    recv_attn_grad, up_grad, summed_out = lax.optimization_barrier(
        (recv_attn_grad, up_grad, summed_out)
    )

    back_moe = exchange(summed_out[0].reshape(experts, capacity, model_width))
    backward = back_call if ready else back_plain
    rows_back, grad_keys, grad_values, output_out, query_part = backward(
        recv_attn_grad.reshape(expert_rows, model_width),
        rows_flat,
        row_places,
        far,
        near,
        output_full,
        queries,
        keys_all,
        values_all,
        mixture,
        query_full,
    )
    query_out = lax.psum_scatter(query_part, "dp", scatter_dimension=0, tiled=True)
    grad_normed_one, key_grad, value_grad = (last_call if ready else last_plain)(
        rows_back, spread_table, key_own, value_own, grad_keys, grad_values, normed_group
    )
    grad_normed_one, back_moe = lax.optimization_barrier((grad_normed_one, back_moe))
    spread_moe = jnp.einsum("ect,ecd->etd", table_moe, back_moe, preferred_element_type=f32)
    moe_sum = jnp.sum(dense_moe.T[:, :, None] * spread_moe, axis=0)
    block_out = (live_rows[:, None] * (middle + moe_sum)).astype(bf16)[None]
    grad_logits_attn = gates_backward(grad_dense_attn, onehot_attn, shares_attn, live_rows)
    attn_router_part = jnp.dot(grad_logits_attn.T, normed_one.astype(f32), precision=highest)
    grad_normed_one = grad_normed_one + jnp.dot(
        grad_logits_attn, router_attn.astype(f32), precision=highest
    )
    grad_inputs_norm, attn_gain_part = norm_backward(
        grad_normed_one, inputs_f, scale_one, gain_attn
    )
    input_grad = (grad_middle + grad_inputs_norm).astype(bf16)[None]
    smalls = total_small(
        jnp.concatenate(
            [attn_gain_part[None], moe_gain_part[None], attn_router_part, moe_router_part]
        )
    )
    return (
        block_out,
        input_grad,
        smalls[0],
        smalls[1],
        smalls[2 : 2 + experts].T,
        smalls[2 + experts : kinds].T,
        key_grad,
        value_grad,
        query_out.astype(f32)[None],
        output_out[None],
        gate_grad,
        up_grad,
        down_grad,
    )


def solution(mesh):
    placed = (
        P(("dp", "expert"), None, None),
        P(("dp", "expert"), None, None),
        P("dp"),
        P("dp", None, None),
        P("dp", None, None),
        P("dp"),
        P("dp"),
        P("dp", None),
        P("dp", None),
        P("dp", None),
        P("dp", None),
        P("expert", "dp", None),
        P("expert", "dp", None),
        P("expert", None, "dp"),
        P("expert", None, "dp"),
        P("expert", "dp", None),
    )
    return jax.shard_map(
        on_device,
        mesh=mesh,
        in_specs=placed,
        out_specs=(
            P(("dp", "expert"), None, None),
            P(("dp", "expert"), None, None),
            P(("dp", "expert")),
            P(("dp", "expert")),
            P(("dp", "expert"), None),
            P(("dp", "expert"), None),
            P(("dp", "expert"), None),
            P(("dp", "expert"), None),
            P("expert", "dp", None),
            P("expert", "dp", None),
            P("expert", None, "dp"),
            P("expert", None, "dp"),
            P("expert", "dp", None),
        ),
        check_vma=False,
    )
```

```python
from functools import partial

import jax
import jax.numpy as jnp
from jax import lax
from jax.experimental import pallas as pl
from jax.experimental.pallas import tpu as pltpu
from jax.sharding import PartitionSpec as P

HEADS = 16
HEAD = 128
MESH = pl.DeviceIdType.MESH
ANY = pl.BlockSpec(memory_space=pl.ANY)

eps = 1e-06
theta = 10000.0
highest = lax.Precision.HIGHEST
f32 = jnp.float32
bf16 = jnp.bfloat16


def rope_tables(positions, head_size):
    half_size = head_size // 2
    frequency = theta ** (-(jnp.arange(half_size, dtype=f32) * 2.0 / head_size))
    angles = positions.astype(f32)[:, None] * frequency[None, :]
    return (jnp.cos(angles), jnp.sin(angles))


def signed_tables(positions):
    cosine, sine = rope_tables(positions, HEAD)
    return (jnp.concatenate([cosine, cosine], 1), jnp.concatenate([-sine, sine], 1))


def turned_back(value, tables):
    half_size = HEAD // 2
    swapped = jnp.concatenate([value[:, half_size:], value[:, :half_size]], axis=1)
    return value * tables[0] - swapped * tables[1]


def norm_scale(value):
    return lax.rsqrt(jnp.mean(value * value, axis=-1, keepdims=True) + eps)


def norm_backward(grad_normed, value, scale_value, gain_value):
    scaled_grad = grad_normed * gain_value
    gain_part = jnp.sum(grad_normed * value * scale_value, axis=0)
    grad_value = scale_value * scaled_grad - value * scale_value**3 * jnp.mean(
        scaled_grad * value, axis=-1, keepdims=True
    )
    return (grad_value, gain_part)


def softmax_rows(values):
    peak = jnp.max(values, axis=-1, keepdims=True)
    powers = jnp.exp(values - peak)
    return powers / jnp.sum(powers, axis=-1, keepdims=True)


def router_gates(logits, choices, live_rows, experts):
    onehot = (choices[:, :, None] == jnp.arange(experts, dtype=jnp.int32)[None, None, :]).astype(
        f32
    )
    chosen = jnp.sum(logits[:, None, :] * onehot, axis=-1)
    shares = softmax_rows(chosen)
    dense = jnp.sum((shares * live_rows[:, None])[:, :, None] * onehot, axis=1)
    return (onehot, shares, dense)


def gates_backward(grad_dense, onehot, shares, live_rows):
    grad_shares = jnp.sum(grad_dense[:, None, :] * onehot, axis=-1) * live_rows[:, None]
    grad_chosen = shares * (grad_shares - jnp.sum(shares * grad_shares, axis=-1, keepdims=True))
    return jnp.sum(grad_chosen[:, :, None] * onehot, axis=1)


def route_table(choices, length_value, experts, capacity):
    places = jnp.arange(choices.shape[0], dtype=jnp.int32)
    living = (places < length_value).astype(jnp.int32)
    picked = (
        jnp.sum(
            (choices[:, :, None] == jnp.arange(experts, dtype=jnp.int32)[None, None, :]).astype(
                jnp.int32
            ),
            axis=1,
        )
        * living[:, None]
    )
    slot_of = jnp.cumsum(picked, axis=0) - 1
    slot_ids = jnp.arange(capacity, dtype=jnp.int32)
    return (slot_of.T[:, None, :] == slot_ids[None, :, None]) & (picked.T[:, None, :] == 1)


def flip(index, bit):
    return index + bit * (1 - 2 * ((index // bit) % 2))


def flips(index, mask, bits):
    for bit in bits:
        if mask & bit:
            index = flip(index, bit)
    return index


def span(bits):
    masks = [0]
    for bit in bits:
        masks = masks + [mask | bit for mask in masks]
    return masks


def bit_orders(size):
    bits = [1 << k for k in range(size.bit_length() - 1)]
    high = bits[1:]
    return (high + bits[:1], high[::-1] + bits[:1])


def barrier(targets):
    semaphore = pltpu.get_barrier_semaphore()
    for target in targets:
        pl.semaphore_signal(semaphore, inc=1, device_id=target, device_id_type=MESH)
    pl.semaphore_wait(semaphore, len(targets))


def gather_kernel(groups, experts, splits, axes, *refs):
    count = len(splits)
    shards, home = refs[:count], refs[count]
    fulls, home_all = refs[count + 1 : 2 * count + 1], refs[2 * count + 1]
    local_sem, send_sem, recv_sem, home_send, home_recv = refs[2 * count + 2 :]
    group = lax.axis_index("dp")
    mine = lax.axis_index("expert")
    orders = bit_orders(groups)
    bits = sorted(orders[0])
    others = [(mine + step) % experts for step in range(1, experts)]
    barrier([(flip(group, bit), mine) for bit in bits] + [(group, other) for other in others])

    home_copies = []
    for step, other in enumerate(others):
        copy = pltpu.make_async_remote_copy(
            src_ref=home,
            dst_ref=home_all.at[mine],
            send_sem=home_send.at[step],
            recv_sem=home_recv.at[step],
            device_id=(group, other),
            device_id_type=MESH,
        )
        copy.start()
        home_copies.append(copy)

    def part(ref, which, block, half):
        pieces, axis = splits[which], axes[which]
        extent = shards[which].shape[axis]
        size = extent // pieces
        start = half * size if block is None else block * extent + half * size
        if block is not None:
            start = pl.multiple_of(start, size)
        where = pl.ds(start, size)
        return ref.at[where] if axis == 0 else ref.at[:, where]

    stages = {}
    slot = 0
    for which in range(count):
        for half in range(splits[which]):
            order = orders[half]
            for stage, bit in enumerate(order):
                copies = []
                for mask in span(order[:stage]):
                    block = flips(group, mask, bits)
                    target = part(fulls[which], which, block, half)
                    source = part(shards[which], which, None, half) if mask == 0 else target
                    copies.append(
                        pltpu.make_async_remote_copy(
                            src_ref=source,
                            dst_ref=target,
                            send_sem=send_sem.at[slot],
                            recv_sem=recv_sem.at[slot],
                            device_id=(flip(group, bit), mine),
                            device_id_type=MESH,
                        )
                    )
                    slot += 1
                stages[which, half, stage] = copies
    keys = [(which, half) for which in range(count) for half in range(splits[which])]
    for which, half in keys:
        for copy in stages[which, half, 0]:
            copy.start()
    local = [pltpu.make_async_copy(home, home_all.at[mine], local_sem.at[count])]
    for which in range(count):
        extent = shards[which].shape[axes[which]]
        where = pl.ds(pl.multiple_of(group * extent, extent), extent)
        target = fulls[which].at[where] if axes[which] == 0 else fulls[which].at[:, where]
        local.append(pltpu.make_async_copy(shards[which], target, local_sem.at[which]))
    for copy in local:
        copy.start()
    for stage in range(len(bits)):
        for which, half in keys:
            for copy in stages[which, half, stage]:
                copy.wait_recv()
            if stage + 1 < len(bits):
                for copy in stages[which, half, stage + 1]:
                    copy.start()
    for copies in stages.values():
        for copy in copies:
            copy.wait_send()
    for copy in home_copies:
        copy.wait()
    for copy in local:
        copy.wait()


def gather_all(arrays, splits, axes, home):
    groups = lax.axis_size("dp")
    experts = lax.axis_size("expert")
    shapes = []
    for array, axis in zip(arrays, axes):
        shape = list(array.shape)
        shape[axis] *= groups
        shapes.append(jax.ShapeDtypeStruct(tuple(shape), array.dtype))
    shapes.append(jax.ShapeDtypeStruct((experts,) + home.shape, home.dtype))
    slots = sum(splits) * (groups - 1)
    return pl.pallas_call(
        partial(gather_kernel, groups, experts, splits, axes),
        out_shape=shapes,
        in_specs=[ANY] * (len(arrays) + 1),
        out_specs=[ANY] * (len(arrays) + 1),
        scratch_shapes=[
            pltpu.SemaphoreType.DMA((len(arrays) + 1,)),
            pltpu.SemaphoreType.DMA((slots,)),
            pltpu.SemaphoreType.DMA((slots,)),
            pltpu.SemaphoreType.DMA((experts - 1,)),
            pltpu.SemaphoreType.DMA((experts - 1,)),
        ],
        compiler_params=pltpu.CompilerParams(collective_id=0, has_side_effects=True),
        name="gather_all",
    )(*arrays, home)


def total_kernel(groups, experts, parts, total, held, send_sem, recv_sem):
    devices = groups * experts
    me = lax.axis_index("dp") * experts + lax.axis_index("expert")
    semaphore = pltpu.get_barrier_semaphore()

    def greet(step, carry):
        other = (me + step) % devices
        pl.semaphore_signal(
            semaphore,
            inc=1,
            device_id=(other // experts, other % experts),
            device_id_type=MESH,
        )
        return carry

    lax.fori_loop(1, devices, greet, 0)
    pl.semaphore_wait(semaphore, devices - 1)

    share = parts.shape[1] // devices

    def columns(owner):
        return pl.ds(pl.multiple_of((owner * share // 128) * 128, 128), 128)

    def copy_of(step):
        other = (me + step) % devices
        return pltpu.make_async_remote_copy(
            src_ref=parts.at[:, columns(other)],
            dst_ref=held.at[step],
            send_sem=send_sem.at[step],
            recv_sem=recv_sem.at[step],
            device_id=(other // experts, other % experts),
            device_id_type=MESH,
        )

    def send(step, carry):
        copy_of(step).start()
        return carry

    lax.fori_loop(1, devices, send, 0)
    held[0] = parts[:, columns(me)]

    def finish(step, carry):
        copy_of(step).wait()
        return carry

    lax.fori_loop(1, devices, finish, 0)
    total[...] = jnp.sum(held[...], axis=0)


def total_small(rows):
    groups = lax.axis_size("dp")
    experts = lax.axis_size("expert")
    devices = groups * experts
    kinds, width = rows.shape
    share = width // devices
    room = -(-kinds // 8) * 8
    total = pl.pallas_call(
        partial(total_kernel, groups, experts),
        out_shape=jax.ShapeDtypeStruct((room, 128), f32),
        in_specs=[pl.BlockSpec(memory_space=pltpu.VMEM)],
        out_specs=pl.BlockSpec(memory_space=pltpu.VMEM),
        scratch_shapes=[
            pltpu.VMEM((devices, room, 128), f32),
            pltpu.SemaphoreType.DMA((devices,)),
            pltpu.SemaphoreType.DMA((devices,)),
        ],
        compiler_params=pltpu.CompilerParams(collective_id=1, has_side_effects=True),
        name="total_small",
    )(jnp.pad(rows, ((0, room - kinds), (0, 0))))
    place = (lax.axis_index("dp") * experts + lax.axis_index("expert")) % (128 // share)
    return lax.dynamic_slice_in_dim(total, place * share, share, 1)[:kinds]


def turn(value, cosine, sine):
    return value * cosine + pltpu.roll(value, HEAD // 2, 1) * sine


def softmax_all(scores, seen):
    masked = jnp.where(seen, scores * (HEAD ** (-0.5)), -1e30)
    powers = jnp.exp(masked - jnp.max(masked, axis=-1, keepdims=True))
    return powers / jnp.sum(powers, axis=-1, keepdims=True)


def blocks_of(experts, rows, tokens, width):
    capacity, seq_len = rows // experts, tokens // experts
    return [
        (
            slice(seq * capacity, (seq + 1) * capacity),
            slice(seq * seq_len, (seq + 1) * seq_len),
            slice(head * HEAD, (head + 1) * HEAD),
        )
        for head in range(width // HEAD)
        for seq in range(experts)
    ]


def attend_kernel(
    experts,
    inputs_ref,
    small_ref,
    table_ref,
    place_ref,
    cos_far,
    sin_far,
    cos_near,
    sin_near,
    query_weight,
    key_weight,
    value_weight,
    normed_out,
    rows_out,
    query_out,
    key_out,
    value_out,
    mixture_out,
    query_hold,
):
    @pl.when(pl.program_id(0) == 0)
    def _():
        gain = small_ref[0:1].astype(f32)

        def norm_part(step, carry):
            at = pl.ds(pl.multiple_of(step * 32, 32), 32)
            value = inputs_ref[at].astype(f32)
            normed_out[at] = (value * norm_scale(value) * gain).astype(bf16)
            return carry

        lax.fori_loop(0, inputs_ref.shape[0] // 32, norm_part, 0)
        rows_out[...] = jnp.dot(
            table_ref[...], normed_out[...], preferred_element_type=f32
        ).astype(bf16)

    capacity = rows_out.shape[0] // experts
    seq_len = normed_out.shape[0] // experts
    width = key_out.shape[1]
    key = jnp.dot(normed_out[...], key_weight[...], preferred_element_type=f32)
    value_out[...] = jnp.dot(
        normed_out[...], value_weight[...], preferred_element_type=f32
    ).astype(bf16)
    query = jnp.dot(rows_out[...], query_weight[...], preferred_element_type=f32)
    for head in range(width // HEAD):
        cut = slice(head * HEAD, (head + 1) * HEAD)
        key_out[:, cut] = turn(key[:, cut], cos_near[...], sin_near[...]).astype(bf16)
        query_hold[:, cut] = turn(query[:, cut], cos_far[...], sin_far[...])
    query_out[...] = query_hold[...].astype(bf16)
    blocks = blocks_of(experts, rows_out.shape[0], normed_out.shape[0], width)
    contract = (((1,), (1,)), ((), ()))
    scores = jnp.concatenate(
        [
            lax.dot_general(
                query_hold[rows, cut].astype(bf16),
                key_out[keys, cut],
                contract,
                preferred_element_type=f32,
            )
            for rows, keys, cut in blocks
        ],
        axis=0,
    )
    spots = lax.broadcasted_iota(jnp.int32, (rows_out.shape[0], seq_len), 1)
    seen = spots <= place_ref[...]
    probs = softmax_all(scores, jnp.concatenate([seen] * (width // HEAD), axis=0))
    for number, (rows, keys, cut) in enumerate(blocks):
        query_hold[rows, cut] = jnp.dot(
            probs[number * capacity : (number + 1) * capacity].astype(bf16),
            value_out[keys, cut],
            preferred_element_type=f32,
        )
    mixture_out[...] = query_hold[...].astype(bf16)


def attend(experts, inputs, small, table, places, far, near, query_w, key_w, value_w):
    tokens, depth = inputs.shape
    rows = table.shape[0]
    heads_width = query_w.shape[1]
    tile = 256

    def full(shape):
        return pl.BlockSpec(shape, lambda step: (0, 0))

    def cut(height):
        return pl.BlockSpec((height, tile), lambda step: (0, step))

    def shaped(height, width):
        return jax.ShapeDtypeStruct((height, width), bf16)

    return pl.pallas_call(
        partial(attend_kernel, experts),
        grid=(heads_width // tile,),
        out_shape=[
            shaped(tokens, depth),
            shaped(rows, depth),
            shaped(rows, heads_width),
            shaped(tokens, heads_width),
            shaped(tokens, heads_width),
            shaped(rows, heads_width),
        ],
        in_specs=[
            full((tokens, depth)),
            full(small.shape),
            full(table.shape),
            full(places.shape),
            full((rows, HEAD)),
            full((rows, HEAD)),
            full((tokens, HEAD)),
            full((tokens, HEAD)),
            cut(depth),
            cut(depth),
            cut(depth),
        ],
        out_specs=[
            full((tokens, depth)),
            full((rows, depth)),
            cut(rows),
            cut(tokens),
            cut(tokens),
            cut(rows),
        ],
        scratch_shapes=[pltpu.VMEM((rows, tile), f32)],
        compiler_params=pltpu.CompilerParams(vmem_limit_bytes=48 * 1024 * 1024),
        cost_estimate=pl.CostEstimate(
            flops=2 * depth * heads_width * (2 * tokens + rows),
            bytes_accessed=6 * depth * heads_width + 8 * tokens * depth,
            transcendentals=rows * heads_width,
        ),
        name="attend",
    )(inputs, small, table, places, *far, *near, query_w, key_w, value_w)


def attend_back_kernel(
    experts,
    grad_ref,
    place_ref,
    cos_far,
    sin_far,
    weight_ref,
    query_ref,
    key_ref,
    value_ref,
    mixture_ref,
    query_out,
    key_out,
    value_out,
    output_out,
    grad_hold,
    query_hold,
    back_hold,
):
    contract = (((1,), (1,)), ((), ()))
    stack = (((0,), (0,)), ((), ()))
    rows_all = grad_ref.shape[0]
    capacity = rows_all // experts
    width = query_ref.shape[1]
    seq_len = key_ref.shape[0] // experts
    scale = HEAD ** (-0.5)
    grad_hold[...] = (
        lax.dot_general(grad_ref[...], weight_ref[...], contract, preferred_element_type=f32)
        .astype(bf16)
        .astype(f32)
    )
    output_out[...] = lax.dot_general(
        mixture_ref[...], grad_ref[...], stack, preferred_element_type=f32
    ).astype(bf16)
    query_hold[...] = query_ref[...].astype(f32)
    blocks = blocks_of(experts, rows_all, key_ref.shape[0], width)
    queries = [query_hold[rows, cut].astype(bf16) for rows, keys, cut in blocks]
    grads = [grad_hold[rows, cut].astype(bf16) for rows, keys, cut in blocks]
    scores = jnp.concatenate(
        [
            lax.dot_general(query, key_ref[keys, cut], contract, preferred_element_type=f32)
            for query, (rows, keys, cut) in zip(queries, blocks)
        ],
        axis=0,
    )
    grad_probs = jnp.concatenate(
        [
            lax.dot_general(grad, value_ref[keys, cut], contract, preferred_element_type=f32)
            for grad, (rows, keys, cut) in zip(grads, blocks)
        ],
        axis=0,
    )
    spots = lax.broadcasted_iota(jnp.int32, (rows_all, seq_len), 1)
    seen = spots <= place_ref[...]
    probs = softmax_all(scores, jnp.concatenate([seen] * (width // HEAD), axis=0))
    inner = jnp.sum(probs * grad_probs, axis=-1, keepdims=True)
    slopes = probs * (grad_probs - inner)
    for number, (rows, keys, cut) in enumerate(blocks):
        own = slice(number * capacity, (number + 1) * capacity)
        slope = slopes[own].astype(bf16)
        value_out[0, keys, cut] = lax.dot_general(
            probs[own].astype(bf16), grads[number], stack, preferred_element_type=f32
        ).astype(bf16)
        key_out[0, keys, cut] = (
            lax.dot_general(slope, queries[number], stack, preferred_element_type=f32) * scale
        ).astype(bf16)
        back_hold[rows, cut] = (
            jnp.dot(slope, key_ref[keys, cut], preferred_element_type=f32) * scale
        )
    for head in range(width // HEAD):
        cut = slice(head * HEAD, (head + 1) * HEAD)
        query_out[:, cut] = turn(back_hold[:, cut], cos_far[...], -sin_far[...]).astype(bf16)


def attend_back(experts, grad_rows, places, far, output_w, query, key, value, mixture):
    rows, depth = grad_rows.shape
    tokens, heads_width = key.shape
    tile = 256
    own_width = heads_width // experts
    steps = own_width // tile

    def full(shape):
        return pl.BlockSpec(shape, lambda step: (0, 0))

    def cut(height):
        return pl.BlockSpec((height, tile), lambda step: (0, step))

    by_heads = pl.BlockSpec((1, tokens, tile), lambda step: (step // steps, 0, step % steps))
    return pl.pallas_call(
        partial(attend_back_kernel, experts),
        grid=(heads_width // tile,),
        out_shape=[
            jax.ShapeDtypeStruct((rows, heads_width), bf16),
            jax.ShapeDtypeStruct((experts, tokens, own_width), bf16),
            jax.ShapeDtypeStruct((experts, tokens, own_width), bf16),
            jax.ShapeDtypeStruct((heads_width, depth), bf16),
        ],
        in_specs=[
            full((rows, depth)),
            full(places.shape),
            full((rows, HEAD)),
            full((rows, HEAD)),
            pl.BlockSpec((tile, depth), lambda step: (step, 0)),
            cut(rows),
            cut(tokens),
            cut(tokens),
            cut(rows),
        ],
        out_specs=[
            cut(rows),
            by_heads,
            by_heads,
            pl.BlockSpec((tile, depth), lambda step: (step, 0)),
        ],
        scratch_shapes=[pltpu.VMEM((rows, tile), f32)] * 3,
        compiler_params=pltpu.CompilerParams(vmem_limit_bytes=48 * 1024 * 1024),
        cost_estimate=pl.CostEstimate(
            flops=4 * rows * depth * heads_width,
            bytes_accessed=4 * depth * heads_width + 8 * tokens * heads_width,
            transcendentals=rows * heads_width,
        ),
        name="attend_back",
    )(grad_rows, places, *far, output_w, query, key, value, mixture)


def halves(ref, block, rows, half):
    size = rows // 2
    return ref.at[pl.ds(pl.multiple_of(block * rows + half * size, size), size)]


def whole(ref, block, rows):
    return ref.at[pl.ds(pl.multiple_of(block * rows, rows), rows)]


def ffn_kernel(
    rows,
    own_ref,
    slope_ref,
    pick_ref,
    router_ref,
    gate_in,
    up_in,
    down_in,
    rows_out,
    hidden_out,
    grad_gate_out,
    grad_up_out,
    out_out,
    grad_out,
    gate_ref,
    up_ref,
    down_ref,
    held,
    pulled,
    hidden,
    scaled,
    grad_gate,
    grad_up,
    made,
    grads,
    near,
    far,
    dense,
    dense_far,
    dense_hold,
    far_send,
    far_recv,
    across_send,
    across_recv,
    near_send,
    near_recv,
    sum_send,
    sum_recv,
    dense_send,
    dense_recv,
    load_sem,
    seat_sem,
    save_sem,
    intake_sem,
):
    group = lax.axis_index("dp")
    mine = lax.axis_index("expert")
    depth = held.shape[1]
    width = hidden.shape[1]
    part = rows // 2
    pair = 2 * part
    split = -(-part // 32) * 16
    bits = (1, 2, 4)
    peers = {mask: (flips(group, mask, bits), mine) for mask in range(1, 8)}
    intake = [
        pltpu.make_async_copy(source, target, intake_sem.at[number])
        for number, (source, target) in enumerate(
            ((gate_in, gate_ref), (up_in, up_ref), (down_in, down_ref))
        )
    ]
    for copy in intake:
        copy.start()
    barrier([peers[mask] for mask in range(1, 8)])

    def remote(source, target, send, recv, mask):
        return pltpu.make_async_remote_copy(
            src_ref=source,
            dst_ref=target,
            send_sem=send,
            recv_sem=recv,
            device_id=peers[mask],
            device_id_type=MESH,
        )

    def cut_of(half):
        return (0, split) if half == 0 else (split, part - split)

    def seat_of(batch, block):
        return pl.ds(pl.multiple_of((batch * 8 + block) * part, 16), part)

    def some(batch, block, half):
        start, size = cut_of(half)
        return held.at[pl.ds((batch * 8 + block) * part + start, size)]

    sends = {}
    across = {}
    for batch in range(2):
        for slot, (mask, half) in enumerate(((2, 0), (4, 1), (2, 1), (4, 0))):
            start, size = cut_of(half)
            sends[batch, mask, half] = remote(
                own_ref.at[pl.ds(batch * part + start, size)],
                some(batch, mask, half),
                far_send.at[batch, slot],
                far_recv.at[batch, slot],
                mask,
            )
        sends[batch, 6, 0] = remote(
            some(batch, 2, 0),
            some(batch, 6, 0),
            far_send.at[batch, 4],
            far_recv.at[batch, 4],
            4,
        )
        sends[batch, 6, 1] = remote(
            some(batch, 4, 1),
            some(batch, 6, 1),
            far_send.at[batch, 5],
            far_recv.at[batch, 5],
            2,
        )
        for chip in range(4):
            across[batch, chip] = remote(
                own_ref.at[pl.ds(batch * part, part)]
                if chip == 0
                else held.at[seat_of(batch, 2 * chip)],
                held.at[seat_of(batch, 2 * chip + 1)],
                across_send.at[batch, chip],
                across_recv.at[batch, chip],
                1,
            )

    def leave(batch):
        for mask, half in ((2, 0), (4, 1), (2, 1), (4, 0)):
            sends[batch, mask, half].start()

    def pass_on(batch):
        sends[batch, 2, 0].wait_recv()
        sends[batch, 6, 0].start()
        sends[batch, 4, 1].wait_recv()
        sends[batch, 6, 1].start()
        sends[batch, 2, 1].wait_recv()
        across[batch, 1].start()
        sends[batch, 4, 0].wait_recv()
        across[batch, 2].start()

    def finish(batch):
        sends[batch, 6, 0].wait_recv()
        sends[batch, 6, 1].wait_recv()
        across[batch, 3].start()

    leave(0)
    across[0, 0].start()
    across[1, 0].start()
    seats = [
        pltpu.make_async_copy(
            own_ref.at[pl.ds(batch * part, part)], held.at[seat_of(batch, 0)], seat_sem.at[batch]
        )
        for batch in range(2)
    ]
    for seat in seats:
        seat.start()

    def group_of(index):
        result = group
        for bit in bits:
            on = (index // bit) % 2
            turned = bit * (1 - 2 * ((group // bit) % 2))
            result = result + on * turned
        return result

    def rows_of(step, which):
        return group_of(2 * (step % 4) + which), pl.ds(
            pl.multiple_of((step // 4) * part, 16), part
        )

    def pull(step, which):
        block, at = rows_of(step, which)
        slot = 2 * (step % 2) + which
        return pltpu.make_async_copy(
            slope_ref.at[block, at],
            pulled.at[pl.ds(pl.multiple_of(slot * part, 16), part)],
            load_sem.at[which],
        )

    def saves(step):
        copies = []
        for which in range(2):
            block, at = rows_of(step, which)
            own = pl.ds(which * part, part)
            for number, (source, target) in enumerate(
                (
                    (held.at[seat_of(step // 4, 2 * (step % 4) + which)], rows_out),
                    (scaled.at[own], hidden_out),
                    (grad_gate.at[own], grad_gate_out),
                    (grad_up.at[own], grad_up_out),
                    (made.at[own], out_out),
                )
            ):
                copies.append(
                    pltpu.make_async_copy(
                        source, target.at[block, at], save_sem.at[5 * which + number]
                    )
                )
        return copies

    sums = [
        ChipSums(
            remote,
            grads.at[batch],
            near.at[batch],
            far.at[batch],
            (
                near_send.at[batch],
                near_recv.at[batch],
                sum_send.at[batch],
                sum_recv.at[batch],
            ),
            part,
        )
        for batch in range(2)
    ]

    def dense_hop(mask):
        return remote(
            dense.at[mask],
            dense_far.at[mask],
            dense_send.at[mask],
            dense_recv.at[mask],
            mask,
        )

    for which in range(2):
        pull(0, which).start()
    for seat in seats:
        seat.wait()
    for copy in intake:
        copy.wait()

    def one(step, carry):
        batch = step // 4
        chip = step % 4

        @pl.when(step == 0)
        def _():
            across[0, 0].wait_recv()

        @pl.when(step == 1)
        def _():
            pass_on(0)
            across[0, 1].wait_recv()

        @pl.when(step == 2)
        def _():
            finish(0)
            leave(1)
            across[0, 2].wait_recv()

        @pl.when(step == 3)
        def _():
            across[0, 3].wait_recv()

        @pl.when(step == 4)
        def _():
            across[1, 0].wait_recv()

        @pl.when(step == 5)
        def _():
            pass_on(1)
            across[1, 1].wait_recv()

        @pl.when(step == 6)
        def _():
            finish(1)
            across[1, 2].wait_recv()

        @pl.when(step == 7)
        def _():
            across[1, 3].wait_recv()

        for which in range(2):
            pull(step, which).wait()

        @pl.when(step < 7)
        def _():
            for which in range(2):
                pull(step + 1, which).start()

        @pl.when(step > 0)
        def _():
            for copy in saves(step - 1):
                copy.wait()

        at = pl.ds(pl.multiple_of((batch * 8 + 2 * chip) * part, pair), pair)
        grads_at = pl.ds(pl.multiple_of(2 * chip * part, pair), pair)
        loads = pl.ds(pl.multiple_of((step % 2) * pair, pair), pair)
        logits = lax.dot_general(
            held[at], router_ref[...], (((1,), (1,)), ((), ())), preferred_element_type=f32
        )
        apart = []
        for which in range(2):
            block = group_of(2 * chip + which)
            picks = pick_ref[pl.ds(pl.multiple_of(block * rows + batch * part, 8), part)]
            apart.append(
                jnp.sum(
                    logits[which * part : (which + 1) * part] * picks, axis=-1, keepdims=True
                )
            )
        weight = 1.0 / (1.0 + jnp.exp(jnp.concatenate(apart, axis=0)))
        tile = width
        wide = 1024
        partial_dense = jnp.zeros((pair, 128), f32)

        def units(number, total):
            cut = pl.ds(pl.multiple_of(number * tile, tile), tile)
            contract = (((1,), (1,)), ((), ()))
            gate = lax.dot_general(
                held[at], gate_ref[cut], contract, preferred_element_type=f32
            )
            up = lax.dot_general(held[at], up_ref[cut], contract, preferred_element_type=f32)
            sigmoid = 1.0 / (1.0 + jnp.exp(-gate))
            active = gate * sigmoid
            value = (active * up).astype(bf16)
            exact = value.astype(f32)
            plain = pulled[loads, cut]
            hidden[:, cut] = value
            scaled[:, cut] = (weight * exact).astype(bf16)
            inner = weight * plain
            grad_gate[:, cut] = (inner * up * (sigmoid * (1.0 + gate * (1.0 - sigmoid)))).astype(
                bf16
            )
            grad_up[:, cut] = (inner * active).astype(bf16)
            both = exact * plain
            for start in range(0, tile, 128):
                total = total + both[:, start : start + 128]
            return total

        partial_dense = lax.fori_loop(0, width // tile, units, partial_dense)
        ones = jnp.ones((8, 128), f32)
        for which in range(2):
            dense[2 * chip + which, pl.ds(pl.multiple_of(batch * 8, 8), 8)] = lax.dot_general(
                ones,
                partial_dense[which * part : (which + 1) * part],
                (((1,), (1,)), ((), ())),
                precision=highest,
                preferred_element_type=f32,
            )

        for number in range(2):

            @pl.when((step > 4 * number) & (step <= 4 * number + 4))
            def _():
                sums[number].settle((step - 1) % 4)

        def columns(number, carry):
            cut = pl.ds(pl.multiple_of(number * wide, wide), wide)
            made[:, cut] = jnp.dot(
                hidden[...], down_ref[:, cut], preferred_element_type=f32
            ).astype(bf16)
            grads[batch, grads_at, cut] = (
                jnp.dot(grad_gate[...], gate_ref[:, cut], preferred_element_type=f32)
                + jnp.dot(grad_up[...], up_ref[:, cut], preferred_element_type=f32)
            ).astype(bf16)
            return carry

        lax.fori_loop(0, depth // wide, columns, 0)
        for number in range(2):

            @pl.when(batch == number)
            def _():
                sums[number].across(chip).start()

        for copy in saves(step):
            copy.start()

        @pl.when(step == 6)
        def _():
            sums[0].cross()

        return carry

    lax.fori_loop(0, 8, one, 0)
    sums[1].settle(3)
    for mask in range(1, 8):
        dense_hop(mask).start()
    sums[0].close()
    total = dense[0]
    for mask in range(1, 8):
        dense_hop(mask).wait_recv()
        total = total + dense_far[mask]
    for copy in saves(7):
        copy.wait()
    pick = (lax.broadcasted_iota(jnp.int32, (8, 128), 0) == 0).astype(f32)
    column = jnp.concatenate(
        [
            lax.dot_general(
                total[batch * 8 : (batch + 1) * 8],
                pick,
                (((0,), (0,)), ((), ())),
                precision=highest,
                preferred_element_type=f32,
            )
            for batch in range(2)
        ],
        axis=0,
    )
    upper = column.astype(bf16)
    lower = (column - upper.astype(f32)).astype(bf16)
    lane = lax.broadcasted_iota(jnp.int32, column.shape, 1)
    dense_hold[...] = jnp.where(lane == 0, upper, jnp.where(lane == 1, lower, 0.0)).astype(bf16)
    last = [pltpu.make_async_copy(dense_hold, grad_out.at[:, pl.ds(depth, 128)], load_sem.at[0])]
    for batch in range(2):
        last.append(
            pltpu.make_async_copy(
                grads.at[batch, pl.ds(0, part)],
                grad_out.at[pl.ds(batch * part, part), pl.ds(0, depth)],
                seat_sem.at[batch],
            )
        )
    last[0].start()
    last[1].start()
    sums[1].cross()
    sums[1].close()
    last[2].start()
    for copy in list(sends.values()) + list(across.values()):
        copy.wait_send()
    for batch in range(2):
        sums[batch].drain()
    for mask in range(1, 8):
        dense_hop(mask).wait_send()
    for copy in last:
        copy.wait()


def ffn_call(own, slopes, picks, router, gate, up, down):
    rows, depth = own.shape
    width = gate.shape[0]
    vmem = pl.BlockSpec(memory_space=pltpu.VMEM)
    return pl.pallas_call(
        partial(ffn_kernel, rows),
        out_shape=[
            jax.ShapeDtypeStruct((8, rows, depth), bf16),
            jax.ShapeDtypeStruct((8, rows, width), bf16),
            jax.ShapeDtypeStruct((8, rows, width), bf16),
            jax.ShapeDtypeStruct((8, rows, width), bf16),
            jax.ShapeDtypeStruct((8, rows, depth), bf16),
            jax.ShapeDtypeStruct((rows, depth + 128), bf16),
        ],
        in_specs=[ANY, ANY, vmem, vmem, ANY, ANY, ANY],
        out_specs=[ANY] * 6,
        scratch_shapes=[
            pltpu.VMEM((width, depth), bf16),
            pltpu.VMEM((width, depth), bf16),
            pltpu.VMEM((width, depth), bf16),
            pltpu.VMEM((8 * rows, depth), bf16),
            pltpu.VMEM((2 * rows, width), f32),
            pltpu.VMEM((rows, width), bf16),
            pltpu.VMEM((rows, width), bf16),
            pltpu.VMEM((rows, width), bf16),
            pltpu.VMEM((rows, width), bf16),
            pltpu.VMEM((rows, depth), bf16),
            pltpu.VMEM((2, 4 * rows, depth), bf16),
            pltpu.VMEM((2, 2 * rows, depth), bf16),
            pltpu.VMEM((2, 3 * rows // 2, depth), bf16),
            pltpu.VMEM((8, 16, rows // 2), f32),
            pltpu.VMEM((8, 16, rows // 2), f32),
            pltpu.VMEM((rows, 128), bf16),
            pltpu.SemaphoreType.DMA((2, 6)),
            pltpu.SemaphoreType.DMA((2, 6)),
            pltpu.SemaphoreType.DMA((2, 4)),
            pltpu.SemaphoreType.DMA((2, 4)),
            pltpu.SemaphoreType.DMA((2, 4)),
            pltpu.SemaphoreType.DMA((2, 4)),
            pltpu.SemaphoreType.DMA((2, 6)),
            pltpu.SemaphoreType.DMA((2, 6)),
            pltpu.SemaphoreType.DMA((8,)),
            pltpu.SemaphoreType.DMA((8,)),
            pltpu.SemaphoreType.DMA((2,)),
            pltpu.SemaphoreType.DMA((2,)),
            pltpu.SemaphoreType.DMA((10,)),
            pltpu.SemaphoreType.DMA((3,)),
        ],
        compiler_params=pltpu.CompilerParams(
            collective_id=2, has_side_effects=True, vmem_limit_bytes=61 * 1024 * 1024
        ),
        name="ffn",
    )(own, slopes, picks, router, gate, up, down)


class ChipSums:
    def __init__(self, remote, blocks, near, far, sems, rows):
        self.blocks, self.near, self.far, self.rows = blocks, near, far, rows
        self.remote = remote
        self.near_send, self.near_recv, self.sum_send, self.sum_recv = sems
        self.hops = {}
        self.split = -(-rows // 32) * 16
        place = 0
        for slot, (key, block, half, mask) in enumerate(
            (
                ("x2", 2, 0, 2),
                ("x6", 6, 0, 2),
                ("y4", 4, 1, 4),
                ("y6", 6, 1, 4),
                ("then_y", 4, 0, 4),
                ("then_x", 2, 1, 2),
            )
        ):
            start, size = self.half(half)
            self.hops[key] = (
                remote(
                    blocks.at[pl.ds(block * rows + start, size)],
                    far.at[pl.ds(place, size)],
                    self.sum_send.at[slot],
                    self.sum_recv.at[slot],
                    mask,
                ),
                place,
            )
            place += size

    def half(self, number):
        return (0, self.split) if number == 0 else (self.split, self.rows - self.split)

    def across(self, chip):
        return self.remote(
            whole(self.blocks, 2 * chip + 1, self.rows),
            whole(self.near, chip, self.rows),
            self.near_send.at[chip],
            self.near_recv.at[chip],
            1,
        )

    def add(self, start, other, other_start, count):
        piece = next(size for size in (48, 32, 16) if count % size == 0)

        def one(step, carry):
            at = pl.ds(pl.multiple_of(start + step * piece, 16), piece)
            have = pl.ds(pl.multiple_of(other_start + step * piece, 16), piece)
            self.blocks[at] = (self.blocks[at].astype(f32) + other[have].astype(f32)).astype(bf16)
            return carry

        lax.fori_loop(0, count // piece, one, 0)

    def join(self, chip):
        self.across(chip).wait_recv()
        self.add(2 * chip * self.rows, self.near, chip * self.rows, self.rows)

    def begin(self, key):
        self.hops[key][0].start()

    def settle(self, chip):
        self.join(chip)

        @pl.when(chip == 1)
        def _():
            self.begin("x2")

        @pl.when(chip == 2)
        def _():
            self.begin("y4")

        @pl.when(chip == 3)
        def _():
            self.begin("x6")
            self.begin("y6")

    def add_far(self, block, half, key):
        start, size = self.half(half)
        copy, place = self.hops[key]
        copy.wait_recv()
        self.add(block * self.rows + start, self.far, place, size)

    def cross(self):
        self.add_far(4, 0, "x6")
        self.begin("then_y")
        self.add_far(2, 1, "y6")
        self.begin("then_x")
        self.add_far(0, 0, "x2")
        self.add_far(0, 1, "y4")

    def close(self):
        self.add_far(0, 0, "then_y")
        self.add_far(0, 1, "then_x")

    def drain(self):
        for copy, place in self.hops.values():
            copy.wait_send()
        for chip in range(4):
            self.across(chip).wait_send()


def turned_pair(index, other, bits):
    result = index
    for bit in bits:
        on = (other // bit) % 2
        result = result + on * bit * (1 - 2 * ((index // bit) % 2))
    return result


def back_kernel(
    grad_in,
    rows_in,
    place_ref,
    cos_far,
    sin_far,
    cos_near,
    sin_near,
    weight_ref,
    query_in,
    key_in,
    value_in,
    mixture_in,
    query_weight,
    back_out,
    key_out,
    value_out,
    output_sum,
    query_part,
    query_out,
    grad_ref,
    rows_ref,
    query_ref,
    key_ref,
    value_ref,
    mixture_ref,
    grad_hold,
    query_hold,
    back_hold,
    weights,
    key_part,
    value_part,
    key_got,
    value_got,
    key_pass,
    value_pass,
    total_hold,
    result_hold,
    output_blocks,
    output_near,
    output_far,
    query_blocks,
    output_near_send,
    output_near_recv,
    output_sum_send,
    output_sum_recv,
    query_save,
    got_send,
    got_recv,
    pass_send,
    pass_recv,
    load_sem,
    intake_sem,
):
    group = lax.axis_index("dp")
    mine = lax.axis_index("expert")
    experts = 4
    side = mine // 2
    edge = ((mine + 1) % experts) // 2 == 0
    bits = (1, 2, 4)
    peers = {mask: (flips(group, mask, bits), mine) for mask in (1, 2, 4)}
    intake = [
        pltpu.make_async_copy(source, target, intake_sem.at[number])
        for number, (source, target) in enumerate(
            (
                (grad_in, grad_ref),
                (mixture_in, mixture_ref),
                (query_in, query_ref),
                (key_in, key_ref),
                (value_in, value_ref),
                (rows_in, rows_ref),
            )
        )
    ]
    for copy in intake:
        copy.start()
    barrier(
        [peers[mask] for mask in (1, 2, 4)]
        + [(group, (mine + step) % experts) for step in range(1, experts)]
    )

    def remote(source, target, send, recv, mask):
        return pltpu.make_async_remote_copy(
            src_ref=source,
            dst_ref=target,
            send_sem=send,
            recv_sem=recv,
            device_id=peers[mask],
            device_id_type=MESH,
        )

    rows_all, depth = grad_ref.shape
    tokens = key_ref.shape[0]
    capacity = rows_all // experts
    seq_len = tokens // experts
    tile = 256
    contract = (((1,), (1,)), ((), ()))
    stack = (((0,), (0,)), ((), ()))
    scale = HEAD ** (-0.5)
    outputs = ChipSums(
        remote,
        output_blocks,
        output_near,
        output_far,
        (output_near_send, output_near_recv, output_sum_send, output_sum_recv),
        tile,
    )
    def owner_of(number):
        near_end = 2 - side
        far_end = 3 - 3 * side
        return jnp.where(
            number == 0,
            jnp.where(edge, near_end, far_end),
            jnp.where(
                number == 1,
                jnp.where(edge, far_end, near_end),
                jnp.where(number == 2, 1 + 4 * side - mine, mine),
            ),
        )

    def chip_of(owner):
        return turned_pair(owner, group // 2, (1, 2))

    def load(step):
        at = pl.multiple_of((2 * owner_of(step // 2) + step % 2) * tile, tile)
        return pltpu.make_async_copy(
            weight_ref.at[pl.ds(at, tile)], weights.at[step % 2], load_sem.at[step % 2]
        )

    def part_at(owner):
        return pl.ds(pl.multiple_of(owner * tokens, tokens), tokens)

    def give(owner):
        return [
            pltpu.make_async_remote_copy(
                src_ref=part.at[part_at(owner)],
                dst_ref=got.at[part_at(mine)],
                send_sem=got_send.at[owner, number],
                recv_sem=got_recv.at[mine, number],
                device_id=(group, owner),
                device_id_type=MESH,
            )
            for number, (part, got) in enumerate(
                ((key_part, key_got), (value_part, value_got))
            )
        ]

    def got_from(source):
        return [
            pltpu.make_async_remote_copy(
                src_ref=part.at[part_at(source)],
                dst_ref=got.at[part_at(source)],
                send_sem=got_send.at[source, number],
                recv_sem=got_recv.at[source, number],
                device_id=(group, source),
                device_id_type=MESH,
            )
            for number, (part, got) in enumerate(
                ((key_part, key_got), (value_part, value_got))
            )
        ]

    def hand_on(target):
        return [
            pltpu.make_async_remote_copy(
                src_ref=part.at[part_at(2 - side)],
                dst_ref=pile,
                send_sem=pass_send.at[number],
                recv_sem=pass_recv.at[number],
                device_id=(group, target),
                device_id_type=MESH,
            )
            for number, (part, pile) in enumerate(
                ((key_part, key_pass), (value_part, value_pass))
            )
        ]

    load(0).start()
    for copy in intake:
        copy.wait()
    block_slices = blocks_of(experts, rows_all, tokens, tile)
    spots = lax.broadcasted_iota(jnp.int32, (rows_all, seq_len), 1)

    def one(step, carry):
        owner = owner_of(step // 2)
        parity = step % 2
        number = 2 * owner + parity
        chip = chip_of(owner)
        load(step).wait()

        @pl.when(step < 7)
        def _():
            load(step + 1).start()

        columns = pl.ds(pl.multiple_of(number * tile, tile), tile)
        block = turned_pair(number, group, bits)
        block_at = pl.ds(pl.multiple_of(block * tile, tile), tile)
        grad_hold[...] = (
            lax.dot_general(
                grad_ref[...], weights[parity], contract, preferred_element_type=f32
            )
            .astype(bf16)
            .astype(f32)
        )
        output_blocks[block_at] = lax.dot_general(
            mixture_ref[:, columns], grad_ref[...], stack, preferred_element_type=f32
        ).astype(bf16)

        @pl.when((parity == 1) & (step > 1))
        def _():
            outputs.settle(chip_of(owner_of(step // 2 - 1)))

        query_hold[...] = query_ref[:, columns].astype(f32)
        keys_tile = key_ref[:, columns]
        values_tile = value_ref[:, columns]
        queries = [query_hold[rows, cut].astype(bf16) for rows, keys, cut in block_slices]
        grads = [grad_hold[rows, cut].astype(bf16) for rows, keys, cut in block_slices]
        scores = jnp.concatenate(
            [
                lax.dot_general(query, keys_tile[keys, cut], contract, preferred_element_type=f32)
                for query, (rows, keys, cut) in zip(queries, block_slices)
            ],
            axis=0,
        )
        grad_probs = jnp.concatenate(
            [
                lax.dot_general(grad, values_tile[keys, cut], contract, preferred_element_type=f32)
                for grad, (rows, keys, cut) in zip(grads, block_slices)
            ],
            axis=0,
        )
        seen = spots <= place_ref[...]
        probs = softmax_all(scores, jnp.concatenate([seen] * (tile // HEAD), axis=0))
        inner = jnp.sum(probs * grad_probs, axis=-1, keepdims=True)
        slopes = probs * (grad_probs - inner)
        for count, (rows, keys, cut) in enumerate(block_slices):
            own = slice(count * capacity, (count + 1) * capacity)
            slope = slopes[own].astype(bf16)
            token_at = pl.ds(
                pl.multiple_of(owner * tokens + keys.start, seq_len), seq_len
            )
            lanes = pl.ds(pl.multiple_of(parity * tile + cut.start, HEAD), HEAD)
            value_part[token_at, lanes] = lax.dot_general(
                probs[own].astype(bf16), grads[count], stack, preferred_element_type=f32
            ).astype(bf16)
            key_part[token_at, lanes] = (
                lax.dot_general(slope, queries[count], stack, preferred_element_type=f32) * scale
            ).astype(bf16)
            back_hold[rows, cut] = (
                jnp.dot(slope, keys_tile[keys, cut], preferred_element_type=f32) * scale
            )
        for head in range(tile // HEAD):
            cut = slice(head * HEAD, (head + 1) * HEAD)
            lanes = pl.ds(pl.multiple_of(number * tile + head * HEAD, HEAD), HEAD)
            query_out[:, lanes] = turn(back_hold[:, cut], cos_far[...], -sin_far[...]).astype(bf16)

        @pl.when(parity == 1)
        def _():
            outputs.across(chip).start()

            @pl.when((step == 1) & edge)
            def _():
                for copy in hand_on(1 + side):
                    copy.start()

            @pl.when(((step == 1) | (step == 5)) & jnp.logical_not(edge))
            def _():
                for copy in give(owner):
                    copy.start()

        return carry

    lax.fori_loop(0, 8, one, 0)

    def keep(number):
        at = pl.ds(pl.multiple_of(number * tile, tile), tile)
        return pltpu.make_async_copy(query_blocks.at[at], query_part.at[at], query_save.at[number])

    def project(number, carry):
        at = pl.ds(pl.multiple_of(number * tile, tile), tile)
        query_blocks[at] = lax.dot_general(
            rows_ref[:, at], query_out[...], stack, preferred_element_type=f32
        ).astype(bf16)
        keep(number).start()
        return carry

    lax.fori_loop(0, 8, project, 0)
    outputs.settle(chip_of(mine))

    def stream(step):
        at = pl.multiple_of(step * tile, tile)
        return pltpu.make_async_copy(
            query_weight.at[pl.ds(at, tile)], weights.at[step % 2], load_sem.at[step % 2]
        )

    stream(0).start()

    def rows_back(step, carry):
        stream(step).wait()

        @pl.when(step < depth // tile - 1)
        def _():
            stream(step + 1).start()

        cut = pl.ds(pl.multiple_of(step * tile, tile), tile)
        back_out[:, cut] = lax.dot_general(
            query_out[...], weights[step % 2], contract, preferred_element_type=f32
        ).astype(bf16)
        return carry

    @pl.when(edge)
    def _():
        for copy in hand_on(1 + side):
            copy.wait_send()
        for owner in (3 - 3 * side, 1 + 4 * side - mine):
            for copy in give(owner):
                copy.start()

    lax.fori_loop(0, depth // tile, rows_back, 0)
    piece = 32

    @pl.when(jnp.logical_not(edge))
    def _():
        for (part, pile), copy in zip(
            ((key_part, key_pass), (value_part, value_pass)), hand_on(1 + side)
        ):
            copy.wait_recv()

            def add(step, carry):
                at = pl.ds(pl.multiple_of((2 - side) * tokens + step * piece, piece), piece)
                other = pl.ds(pl.multiple_of(step * piece, piece), piece)
                part[at] = (part[at].astype(f32) + pile[other].astype(f32)).astype(bf16)
                return carry

            lax.fori_loop(0, tokens // piece, add, 0)
        for copy in give(2 - side):
            copy.start()

    def deliver(sums, result):
        half_tile = tile // 2
        for half in range(2):

            def one(step, carry):
                at = pl.ds(pl.multiple_of(step * piece, piece), piece)
                source = pl.ds(pl.multiple_of(half * half_tile + step * piece, piece), piece)
                result_hold[at] = sums.blocks[source].astype(f32)
                return carry

            lax.fori_loop(0, half_tile // piece, one, 0)
            copy = pltpu.make_async_copy(
                result_hold, result.at[pl.ds(half * half_tile, half_tile)], load_sem.at[0]
            )
            copy.start()
            copy.wait()

    outputs.cross()
    outputs.close()
    deliver(outputs, output_sum)

    def expected(source):
        far_end = (mine + 2) % experts
        middle = ((mine + 1) % experts) // 2 == 1
        return jnp.logical_not(middle & (source == far_end))

    def gather(number, part, got):
        def first(step, carry):
            at = pl.ds(pl.multiple_of(mine * tokens + step * piece, piece), piece)
            where = pl.ds(pl.multiple_of(step * piece, piece), piece)
            total_hold[where] = part[at].astype(f32)
            return carry

        lax.fori_loop(0, tokens // piece, first, 0)
        for hop in range(1, experts):
            source = (mine + hop) % experts

            @pl.when(expected(source))
            def _():
                got_from(source)[number].wait_recv()

                def add(step, carry):
                    at = pl.ds(pl.multiple_of(source * tokens + step * piece, piece), piece)
                    where = pl.ds(pl.multiple_of(step * piece, piece), piece)
                    total_hold[where] = total_hold[where] + got[at].astype(f32)
                    return carry

                lax.fori_loop(0, tokens // piece, add, 0)

    gather(1, value_part, value_got)
    value_out[...] = total_hold[...].astype(bf16)
    gather(0, key_part, key_got)
    for head in range(key_out.shape[1] // HEAD):
        cut = slice(head * HEAD, (head + 1) * HEAD)
        key_out[:, cut] = turn(total_hold[:, cut], cos_near[...], -sin_near[...]).astype(bf16)

    @pl.when(jnp.logical_not(edge))
    def _():
        for copy in give(2 - side):
            copy.wait_send()

    for owner in (3 - 3 * side, 1 + 4 * side - mine):
        for copy in give(owner):
            copy.wait_send()
    outputs.drain()

    def kept(number, carry):
        keep(number).wait()
        return carry

    lax.fori_loop(0, 8, kept, 0)


def back_call(
    grad_rows, rows_flat, places, far, near, output_w, query, key, value, mixture, query_w
):
    rows, depth = grad_rows.shape
    tokens, heads_width = key.shape
    own = heads_width // 4
    tile = 256
    vmem = pl.BlockSpec(memory_space=pltpu.VMEM)

    def dma(*shape):
        return pltpu.SemaphoreType.DMA(shape)

    def blocks(count):
        return pltpu.VMEM((count * tile, depth), bf16)

    return pl.pallas_call(
        back_kernel,
        out_shape=[
            jax.ShapeDtypeStruct((rows, depth), bf16),
            jax.ShapeDtypeStruct((tokens, own), bf16),
            jax.ShapeDtypeStruct((tokens, own), bf16),
            jax.ShapeDtypeStruct((tile, depth), f32),
            jax.ShapeDtypeStruct((depth, heads_width), bf16),
        ],
        in_specs=[ANY] * 2 + [vmem] * 5 + [ANY] * 6,
        out_specs=[vmem] * 3 + [ANY] * 2,
        scratch_shapes=[
            pltpu.VMEM((rows, heads_width), bf16),
            pltpu.VMEM((rows, depth), bf16),
            pltpu.VMEM((rows, depth), bf16),
            pltpu.VMEM((rows, heads_width), bf16),
            pltpu.VMEM((tokens, heads_width), bf16),
            pltpu.VMEM((tokens, heads_width), bf16),
            pltpu.VMEM((rows, heads_width), bf16),
            pltpu.VMEM((rows, tile), f32),
            pltpu.VMEM((rows, tile), f32),
            pltpu.VMEM((rows, tile), f32),
            pltpu.VMEM((2, tile, depth), bf16),
            pltpu.VMEM((4 * tokens, own), bf16),
            pltpu.VMEM((4 * tokens, own), bf16),
            pltpu.VMEM((4 * tokens, own), bf16),
            pltpu.VMEM((4 * tokens, own), bf16),
            pltpu.VMEM((tokens, own), bf16),
            pltpu.VMEM((tokens, own), bf16),
            pltpu.VMEM((tokens, own), f32),
            pltpu.VMEM((tile // 2, depth), f32),
            blocks(8),
            blocks(4),
            blocks(3),
            blocks(8),
            dma(4),
            dma(4),
            dma(6),
            dma(6),
            dma(8),
            dma(4, 2),
            dma(4, 2),
            dma(2),
            dma(2),
            dma(2),
            dma(6),
        ],
        compiler_params=pltpu.CompilerParams(
            collective_id=3, has_side_effects=True, vmem_limit_bytes=61 * 1024 * 1024
        ),
        cost_estimate=pl.CostEstimate(
            flops=60_000_000_000, bytes_accessed=200_000_000, transcendentals=0
        ),
        name="attend_back_sums",
    )(
        grad_rows,
        rows_flat,
        places,
        *far,
        *near,
        output_w,
        query,
        key,
        value,
        mixture,
        query_w,
    )


def start_kernel(
    home,
    attn_gain,
    moe_gain,
    attn_router,
    moe_router,
    attn_choice,
    moe_choice,
    lengths,
    cos_home,
    sin_home,
    given,
    value_shard,
    key_shard,
    query_shard,
    output_shard,
    small_full,
    told_full,
    table_out,
    place_out,
    cos_far,
    sin_far,
    attn_table,
    moe_table,
    normed_out,
    rows_out,
    query_out,
    key_out,
    value_out,
    mixture_out,
    branch_out,
    value_own,
    key_own,
    query_full,
    output_full,
    given_out,
    inputs,
    small_own,
    told_own,
    small_hold,
    normed,
    rows_hold,
    query_hold,
    query_low,
    keys,
    values,
    chances,
    mixture,
    branch,
    given_hold,
    value_stage,
    key_stage,
    query_stage,
    output_stage,
    value_buf,
    key_buf,
    query_buf,
    output_buf,
    load_sem,
    far_send,
    far_recv,
    near_send,
    near_recv,
    home_send,
    home_recv,
    small_send,
    small_recv,
    told_send,
    told_recv,
    heads_send,
    heads_recv,
    given_send,
    given_recv,
    save_sem,
):
    group = lax.axis_index("dp")
    mine = lax.axis_index("expert")
    experts = 4
    bits = (1, 2, 4)
    peers = {mask: (flips(group, mask, bits), mine) for mask in range(1, 8)}
    others = [(mine + hop) % experts for hop in range(1, experts)]
    seq_len, depth = home.shape
    expert_rows = rows_out.shape[0]
    capacity = expert_rows // experts
    tokens = experts * seq_len
    extent = key_shard.shape[0]
    half_extent = extent // 2
    own_width = value_buf.shape[1]
    heads_width = key_buf.shape[1]
    tile = 256
    shards = (value_shard, key_shard, query_shard, output_shard)
    stages = (value_stage, key_stage, query_stage, output_stage)
    buffers = (value_buf, key_buf, query_buf, output_buf)
    loads = []
    for which in range(4):
        source = shards[which]
        if which == 0:
            source = source.at[:, pl.ds(pl.multiple_of(mine * own_width, own_width), own_width)]
        loads.append(pltpu.make_async_copy(source, stages[which], load_sem.at[which]))
    seat = pltpu.make_async_copy(home, inputs.at[mine], load_sem.at[4])
    for copy in loads:
        copy.start()
    seat.start()

    small_hold[...] = jnp.zeros_like(small_hold)
    small_hold[0:1] = attn_gain[...]
    small_hold[1:2] = moe_gain[...]
    small_hold[2 : 2 + experts] = attn_router[...]
    small_hold[2 + experts : 2 + 2 * experts] = moe_router[...]
    small_own[...] = small_hold[...].astype(bf16)
    lane = lax.broadcasted_iota(jnp.int32, (experts, seq_len), 1)
    live = lane < lengths[...]
    told_own[0:experts] = jnp.where(live, moe_choice[0], -1).astype(f32)
    told_own[experts : 2 * experts] = jnp.where(live, moe_choice[1], -1).astype(f32)
    barrier([peers[mask] for mask in range(1, 8)] + [(group, other) for other in others])

    def remote(source, target, send, recv, device):
        return pltpu.make_async_remote_copy(
            src_ref=source,
            dst_ref=target,
            send_sem=send,
            recv_sem=recv,
            device_id=device,
            device_id_type=MESH,
        )

    small_at = pl.ds(pl.multiple_of(group * extent, extent), extent)
    told_at = pl.ds(pl.multiple_of(group * 2 * experts, 2 * experts), 2 * experts)
    smalls = []
    for mask in range(1, 8):
        smalls.append(
            remote(
                small_own,
                small_full.at[:, small_at],
                small_send.at[mask],
                small_recv.at[mask],
                peers[mask],
            )
        )
        smalls.append(
            remote(
                told_own,
                told_full.at[told_at],
                told_send.at[mask],
                told_recv.at[mask],
                peers[mask],
            )
        )
    homes = [
        remote(home, inputs.at[mine], home_send.at[hop], home_recv.at[hop], (group, other))
        for hop, other in enumerate(others)
    ]
    for copy in smalls + homes:
        copy.start()
    small_full[:, small_at] = small_own[...]
    told_full[told_at] = told_own[...]

    def piece(which, mask, half):
        start = flips(group, mask, bits) * extent + half * half_extent
        return buffers[which].at[pl.ds(pl.multiple_of(start, half_extent), half_extent)]

    def block(which, mask):
        start = flips(group, mask, bits) * extent
        return buffers[which].at[pl.ds(pl.multiple_of(start, extent), extent)]

    far = {}
    near = {}
    for which in range(4):
        for slot, (mask, half, towards) in enumerate(
            ((0, 0, 2), (0, 1, 2), (0, 1, 4), (0, 0, 4), (2, 0, 4), (4, 1, 2))
        ):
            far[which, slot] = remote(
                piece(which, mask, half),
                piece(which, mask, half),
                far_send.at[which, slot],
                far_recv.at[which, slot],
                peers[towards],
            )
        for chip in range(4):
            near[which, chip] = remote(
                block(which, 2 * chip),
                block(which, 2 * chip),
                near_send.at[which, chip],
                near_recv.at[which, chip],
                peers[1],
            )

    def convert(which):
        loads[which].wait()
        count = 32

        def one(step, carry):
            at = pl.ds(pl.multiple_of(step * count, count), count)
            to = pl.ds(pl.multiple_of(group * extent + step * count, count), count)
            buffers[which][to] = stages[which][at].astype(bf16)
            return carry

        lax.fori_loop(0, extent // count, one, 0)

    def leave(which):
        for slot in (0, 2, 1, 3):
            far[which, slot].start()
        near[which, 0].start()

    def pass_on(which):
        far[which, 0].wait_recv()
        far[which, 4].start()
        far[which, 2].wait_recv()
        far[which, 5].start()

    def spread(which):
        far[which, 1].wait_recv()
        near[which, 1].start()
        far[which, 3].wait_recv()
        near[which, 2].start()
        far[which, 4].wait_recv()
        far[which, 5].wait_recv()
        near[which, 3].start()

    def complete(which):
        for chip in range(4):
            near[which, chip].wait_recv()

    convert(0)
    leave(0)
    convert(1)
    leave(1)

    chosen = ((attn_choice[0] == mine) | (attn_choice[1] == mine)) & live
    picked = chosen.astype(f32)
    early = lax.broadcasted_iota(jnp.int32, (seq_len, seq_len), 0)
    late = lax.broadcasted_iota(jnp.int32, (seq_len, seq_len), 1)
    until = (early <= late).astype(f32)
    seats = lax.broadcasted_iota(jnp.int32, (capacity, seq_len), 0).astype(f32) + 1.0
    spot = lax.broadcasted_iota(jnp.int32, (capacity, seq_len), 1).astype(f32)

    def seated(taken):
        slot_of = jnp.dot(taken, until, preferred_element_type=f32)
        return [
            ((slot_of[row : row + 1] == seats) & (taken[row : row + 1] > 0.0)).astype(f32)
            for row in range(experts)
        ]

    tables = seated(picked)
    row_of = lax.broadcasted_iota(jnp.int32, (experts, seq_len), 0)

    def own_row(value):
        return jnp.sum(jnp.where(row_of == mine, value, 0), axis=0, keepdims=True)

    own_live = lane < own_row(jnp.broadcast_to(lengths[...], (experts, seq_len)))
    for choice, table_ref in ((attn_choice, attn_table), (moe_choice, moe_table)):
        goes = ((own_row(choice[0]) == row_of) | (own_row(choice[1]) == row_of)) & own_live
        table_ref[...] = jnp.concatenate(seated(goes.astype(f32)), axis=0).astype(bf16)
    for other in range(experts):
        given_hold[other] = jnp.dot(
            moe_table[other * capacity : (other + 1) * capacity],
            given[...],
            preferred_element_type=f32,
        ).astype(bf16)
    empty = jnp.zeros((capacity, seq_len), f32)
    table_out[...] = jnp.concatenate(
        [
            jnp.concatenate(
                [tables[seq] if seq == other else empty for other in range(experts)], axis=1
            )
            for seq in range(experts)
        ],
        axis=0,
    ).astype(bf16)
    place_out[...] = jnp.concatenate(
        [jnp.sum(table * spot, axis=1, keepdims=True) for table in tables], axis=0
    ).astype(jnp.int32)
    stacked = jnp.concatenate(tables, axis=0)
    vacant = 1.0 - jnp.sum(stacked, axis=1, keepdims=True)
    cos_far[...] = vacant + jnp.dot(
        stacked, cos_home[...], precision=highest, preferred_element_type=f32
    )
    sin_far[...] = jnp.dot(stacked, sin_home[...], precision=highest, preferred_element_type=f32)

    pass_on(0)
    convert(2)
    pass_on(1)
    leave(2)
    convert(3)
    spread(0)
    complete(0)
    spread(1)

    seat.wait()
    for copy in smalls:
        copy.wait_recv()
    gain = small_full[0:1].astype(f32)
    for hop in range(experts):
        source = (mine + experts - hop) % experts
        if hop > 0:
            homes[hop - 1].wait_recv()
        count = 32

        def one(step, carry):
            at = pl.ds(pl.multiple_of(step * count, count), count)
            to = pl.ds(pl.multiple_of(source * seq_len + step * count, count), count)
            value = inputs[source, at].astype(f32)
            normed[to] = (value * norm_scale(value) * gain).astype(bf16)
            return carry

        lax.fori_loop(0, seq_len // count, one, 0)
    own_at = pl.ds(pl.multiple_of(mine * own_width, own_width), own_width)
    values[:, own_at] = jnp.dot(
        normed[...], value_buf[...], preferred_element_type=f32
    ).astype(bf16)
    heads = [
        remote(
            values.at[:, own_at],
            values.at[:, own_at],
            heads_send.at[hop],
            heads_recv.at[hop],
            (group, other),
        )
        for hop, other in enumerate(others)
    ]
    for copy in heads:
        copy.start()
    rows_hold[...] = jnp.dot(table_out[...], normed[...], preferred_element_type=f32).astype(bf16)
    saves = [
        pltpu.make_async_copy(normed, normed_out, save_sem.at[0]),
        pltpu.make_async_copy(rows_hold, rows_out, save_sem.at[1]),
        pltpu.make_async_copy(value_buf, value_own, save_sem.at[2]),
    ]
    for copy in saves:
        copy.start()

    def save(source, target, number):
        copy = pltpu.make_async_copy(source, target, save_sem.at[number])
        copy.start()
        saves.append(copy)

    complete(1)
    save(key_buf.at[:, own_at], key_own, 3)

    def make_keys(step, carry):
        cut = pl.ds(pl.multiple_of(step * tile, tile), tile)
        made = jnp.dot(normed[...], key_buf[:, cut], preferred_element_type=f32)
        for head in range(tile // HEAD):
            lanes = pl.ds(pl.multiple_of(step * tile + head * HEAD, HEAD), HEAD)
            part = made[:, head * HEAD : (head + 1) * HEAD]
            for seq in range(experts):
                rows = slice(seq * seq_len, (seq + 1) * seq_len)
                keys[rows, lanes] = turn(part[rows], cos_home[...], sin_home[...]).astype(bf16)
        return carry

    lax.fori_loop(0, heads_width // tile, make_keys, 0)
    save(keys, key_out, 4)
    pass_on(2)
    leave(3)
    spread(2)
    complete(2)
    save(query_buf, query_full, 5)

    blocks = blocks_of(experts, expert_rows, tokens, tile)
    contract = (((1,), (1,)), ((), ()))
    spots = lax.broadcasted_iota(jnp.int32, (expert_rows, seq_len), 1)
    span_rows = len(blocks) * capacity

    def make_chances(step, carry):
        cut = pl.ds(pl.multiple_of(step * tile, tile), tile)
        made = jnp.dot(rows_hold[...], query_buf[:, cut], preferred_element_type=f32)
        for head in range(tile // HEAD):
            part = slice(head * HEAD, (head + 1) * HEAD)
            query_hold[:, part] = turn(made[:, part], cos_far[...], sin_far[...])
        query_low[:, cut] = query_hold[...].astype(bf16)
        tile_keys = keys[:, cut]
        scores = jnp.concatenate(
            [
                lax.dot_general(
                    query_hold[rows, lanes].astype(bf16),
                    tile_keys[spans, lanes],
                    contract,
                    preferred_element_type=f32,
                )
                for rows, spans, lanes in blocks
            ],
            axis=0,
        )
        seen = spots <= place_out[...]
        probs = softmax_all(scores, jnp.concatenate([seen] * (tile // HEAD), axis=0))
        chances[pl.ds(pl.multiple_of(step * span_rows, 64), span_rows)] = probs.astype(bf16)
        return carry

    lax.fori_loop(0, heads_width // tile, make_chances, 0)
    save(query_low, query_out, 6)
    pass_on(3)
    for copy in heads:
        copy.wait_recv()
    givens = [
        remote(
            given_hold.at[other],
            given_out.at[mine],
            given_send.at[hop],
            given_recv.at[hop],
            (group, other),
        )
        for hop, other in enumerate(others)
    ]
    for copy in givens:
        copy.start()
    save(given_hold.at[mine], given_out.at[mine], 11)
    save(values, value_out, 7)

    def mix(step, carry):
        cut = pl.ds(pl.multiple_of(step * tile, tile), tile)
        tile_values = values[:, cut]
        probs = chances[pl.ds(pl.multiple_of(step * span_rows, 64), span_rows)].astype(f32)
        for count, (rows, spans, lanes) in enumerate(blocks):
            query_hold[rows, lanes] = jnp.dot(
                probs[count * capacity : (count + 1) * capacity].astype(bf16),
                tile_values[spans, lanes],
                preferred_element_type=f32,
            )
        mixture[:, cut] = query_hold[...].astype(bf16)
        return carry

    lax.fori_loop(0, heads_width // tile, mix, 0)
    save(mixture, mixture_out, 8)
    spread(3)
    complete(3)
    save(output_buf, output_full, 9)

    def project(step, carry):
        cut = pl.ds(pl.multiple_of(step * tile, tile), tile)
        branch[:, cut] = jnp.dot(
            mixture[...], output_buf[:, cut], preferred_element_type=f32
        ).astype(bf16)
        return carry

    lax.fori_loop(0, depth // tile, project, 0)
    save(branch, branch_out, 10)
    for copy in givens:
        copy.wait_recv()
    for copy in smalls + homes + heads + givens + list(far.values()) + list(near.values()):
        copy.wait_send()
    for copy in saves:
        copy.wait()


def start_call(
    home,
    attn_gain,
    moe_gain,
    attn_router,
    moe_router,
    attn_choice,
    moe_choice,
    lengths,
    near,
    given,
    value_weight,
    key_weight,
    query_weight,
    output_weight,
):
    experts = 4
    groups = 8
    seq_len, depth = home.shape
    extent, heads_width = key_weight.shape
    capacity = 2 * seq_len // experts + 8
    rows = experts * capacity
    tokens = experts * seq_len
    own_width = heads_width // experts
    small_room = -(-(2 + 2 * experts) // 16) * 16
    vmem = pl.BlockSpec(memory_space=pltpu.VMEM)

    def shaped(*shape, kind=bf16):
        return jax.ShapeDtypeStruct(shape, kind)

    def dma(*shape):
        return pltpu.SemaphoreType.DMA(shape)

    return pl.pallas_call(
        start_kernel,
        out_shape=[
            shaped(small_room, depth),
            shaped(groups * 2 * experts, seq_len, kind=f32),
            shaped(rows, tokens),
            shaped(rows, 1, kind=jnp.int32),
            shaped(rows, HEAD, kind=f32),
            shaped(rows, HEAD, kind=f32),
            shaped(rows, seq_len),
            shaped(rows, seq_len),
            shaped(tokens, depth),
            shaped(rows, depth),
            shaped(rows, heads_width),
            shaped(tokens, heads_width),
            shaped(tokens, heads_width),
            shaped(rows, heads_width),
            shaped(rows, depth),
            shaped(depth, own_width),
            shaped(depth, own_width),
            shaped(depth, heads_width),
            shaped(heads_width, depth),
            shaped(experts, capacity, depth),
        ],
        in_specs=[ANY] + [vmem] * 10 + [ANY] * 4,
        out_specs=[vmem] * 8 + [ANY] * 12,
        scratch_shapes=[
            pltpu.VMEM((experts, seq_len, depth), bf16),
            pltpu.VMEM((small_room, extent), bf16),
            pltpu.VMEM((2 * experts, seq_len), f32),
            pltpu.VMEM((small_room, extent), f32),
            pltpu.VMEM((tokens, depth), bf16),
            pltpu.VMEM((rows, depth), bf16),
            pltpu.VMEM((rows, 256), f32),
            pltpu.VMEM((rows, heads_width), bf16),
            pltpu.VMEM((tokens, heads_width), bf16),
            pltpu.VMEM((tokens, heads_width), bf16),
            pltpu.VMEM((rows * heads_width // HEAD, seq_len), bf16),
            pltpu.VMEM((rows, heads_width), bf16),
            pltpu.VMEM((rows, depth), bf16),
            pltpu.VMEM((experts, capacity, depth), bf16),
            pltpu.VMEM((extent, own_width), f32),
            pltpu.VMEM((extent, heads_width), f32),
            pltpu.VMEM((extent, heads_width), f32),
            pltpu.VMEM((extent, depth), f32),
            pltpu.VMEM((depth, own_width), bf16),
            pltpu.VMEM((depth, heads_width), bf16),
            pltpu.VMEM((depth, heads_width), bf16),
            pltpu.VMEM((heads_width, depth), bf16),
            dma(5),
            dma(4, 6),
            dma(4, 6),
            dma(4, 4),
            dma(4, 4),
            dma(3),
            dma(3),
            dma(8),
            dma(8),
            dma(8),
            dma(8),
            dma(3),
            dma(3),
            dma(3),
            dma(3),
            dma(12),
        ],
        compiler_params=pltpu.CompilerParams(
            collective_id=4, has_side_effects=True, vmem_limit_bytes=61 * 1024 * 1024
        ),
        cost_estimate=pl.CostEstimate(
            flops=100_000_000_000, bytes_accessed=300_000_000, transcendentals=0
        ),
        name="attend_start",
    )(
        home,
        attn_gain,
        moe_gain,
        attn_router,
        moe_router,
        attn_choice,
        moe_choice,
        lengths,
        *near,
        given,
        value_weight,
        key_weight,
        query_weight,
        output_weight,
    )


def start_plain(
    home,
    attn_gain,
    moe_gain,
    attn_router,
    moe_router,
    attn_choice,
    moe_choice,
    lengths,
    near,
    given,
    value_weight,
    key_weight,
    query_weight,
    output_weight,
):
    experts = lax.axis_size("expert")
    mine = lax.axis_index("expert")
    seq_len, depth = home.shape
    heads_width = key_weight.shape[1]
    own_width = heads_width // experts
    capacity = 2 * seq_len // experts + 8
    rows = experts * capacity
    kinds = 2 + 2 * experts
    small_own = jnp.concatenate(
        [
            attn_gain,
            moe_gain,
            attn_router,
            moe_router,
            jnp.zeros((-kinds % 16, attn_gain.shape[1]), f32),
        ]
    ).astype(bf16)
    places = jnp.arange(seq_len, dtype=jnp.int32)
    live = places[None] < lengths
    told = jnp.where(live, moe_choice, -1).astype(f32).reshape(2 * experts, seq_len)
    key_full, value_full, query_full, output_full, small_full, told_full, inputs = gather_all(
        [
            key_weight.astype(bf16),
            value_weight.astype(bf16),
            query_weight.astype(bf16),
            output_weight.astype(bf16),
            small_own,
            told,
        ],
        (2, 2, 2, 2, 1, 1),
        (0, 0, 0, 0, 1, 0),
        home,
    )

    def tables_of(choice):
        return jax.vmap(partial(route_table, experts=experts, capacity=capacity))(
            choice.transpose(1, 2, 0), lengths[:, 0]
        )

    attn_all, moe_all = tables_of(attn_choice), tables_of(moe_choice)
    group_table = lax.dynamic_index_in_dim(attn_all, mine, 1, keepdims=False)
    own_attn = lax.dynamic_index_in_dim(attn_all, mine, 0, keepdims=False).astype(bf16)
    own_moe = lax.dynamic_index_in_dim(moe_all, mine, 0, keepdims=False).astype(bf16)
    row_places = jnp.sum(jnp.where(group_table, places, 0), axis=-1).reshape(rows, 1)
    same = jnp.eye(experts, dtype=bool)[:, None, :, None]
    table = (group_table[:, :, None, :] & same).astype(bf16).reshape(rows, experts * seq_len)
    far = signed_tables(row_places[:, 0])
    all_near = tuple(jnp.tile(part, (experts, 1)) for part in near)
    normed, rows_flat, queries, keys, values, mixture = attend(
        experts,
        inputs.reshape(experts * seq_len, depth),
        small_full,
        table,
        row_places,
        far,
        all_near,
        query_full,
        key_full,
        value_full,
    )
    branch = jnp.dot(mixture, output_full, preferred_element_type=f32).astype(bf16)
    given_rows = jnp.einsum("ect,td->ecd", own_moe, given, preferred_element_type=f32)

    def own_heads(weight):
        return lax.dynamic_slice_in_dim(weight, mine * own_width, own_width, 1)

    return (
        small_full,
        told_full,
        table,
        row_places,
        *far,
        own_attn.reshape(rows, seq_len),
        own_moe.reshape(rows, seq_len),
        normed,
        rows_flat,
        queries,
        keys,
        values,
        mixture,
        branch,
        own_heads(value_full),
        own_heads(key_full),
        query_full,
        output_full,
        exchange(given_rows.astype(bf16)),
    )


def last_kernel(
    rows_in,
    table_in,
    key_in,
    value_in,
    grad_keys_in,
    grad_values_in,
    normed_in,
    home_out,
    key_out,
    value_out,
    rows_back,
    table_ref,
    key_own,
    value_own,
    grad_keys,
    grad_values,
    normed_ref,
    intake_sem,
    part,
    got,
    pile,
    blocks,
    near,
    far,
    swapped,
    near_send,
    near_recv,
    sum_send,
    sum_recv,
    got_send,
    got_recv,
    pass_send,
    pass_recv,
    swap_send,
    swap_recv,
):
    group = lax.axis_index("dp")
    mine = lax.axis_index("expert")
    experts = 4
    side = mine // 2
    edge = ((mine + 1) % experts) // 2 == 0
    bits = (1, 2, 4)
    peers = {mask: (flips(group, mask, bits), mine) for mask in (1, 2, 4)}
    others = [(mine + hop) % experts for hop in range(1, experts)]
    intake = [
        pltpu.make_async_copy(source, target, intake_sem.at[number])
        for number, (source, target) in enumerate(
            (
                (rows_in, rows_back),
                (table_in, table_ref),
                (grad_keys_in, grad_keys),
                (grad_values_in, grad_values),
                (key_in, key_own),
                (value_in, value_own),
                (normed_in, normed_ref),
            )
        )
    ]
    for copy in intake:
        copy.start()
    barrier([peers[mask] for mask in (1, 2, 4)] + [(group, other) for other in others])

    def send_to(device, source, target, send, recv):
        return pltpu.make_async_remote_copy(
            src_ref=source,
            dst_ref=target,
            send_sem=send,
            recv_sem=recv,
            device_id=device,
            device_id_type=MESH,
        )

    def remote(source, target, send, recv, mask):
        return send_to(peers[mask], source, target, send, recv)

    seq_len, depth = home_out.shape
    own_width = grad_keys.shape[1]
    tile = depth // 8
    contract = (((1,), (1,)), ((), ()))
    stack = (((0,), (0,)), ((), ()))
    sums = ChipSums(
        remote, blocks, near, far, (near_send, near_recv, sum_send, sum_recv), tile
    )

    def owner_of(number):
        near_end = 2 - side
        far_end = 3 - 3 * side
        return jnp.where(
            number == 0,
            jnp.where(edge, near_end, far_end),
            jnp.where(
                number == 1,
                jnp.where(edge, far_end, near_end),
                jnp.where(number == 2, 1 + 4 * side - mine, mine),
            ),
        )

    def give(owner):
        return send_to(
            (group, owner), part.at[owner], got.at[mine], got_send.at[owner], got_recv.at[mine]
        )

    def got_from(source):
        return send_to(
            (group, source),
            part.at[source],
            got.at[source],
            got_send.at[source],
            got_recv.at[source],
        )

    hand_on = send_to(
        (group, 1 + side), part.at[2 - side], pile, pass_send.at[0], pass_recv.at[0]
    )

    for copy in intake[:-1]:
        copy.wait()

    def one(step, carry):
        owner = owner_of(step)
        at = pl.ds(pl.multiple_of(owner * seq_len, seq_len), seq_len)
        part[owner] = (
            lax.dot_general(
                table_ref[:, at], rows_back[...], stack, preferred_element_type=f32
            )
            + lax.dot_general(
                grad_keys[at], key_own[...], contract, preferred_element_type=f32
            )
            + lax.dot_general(
                grad_values[at], value_own[...], contract, preferred_element_type=f32
            )
        ).astype(bf16)

        @pl.when((step == 0) & edge)
        def _():
            hand_on.start()

        @pl.when(((step == 0) | (step == 2)) & jnp.logical_not(edge))
        def _():
            give(owner).start()

        return carry

    lax.fori_loop(0, experts, one, 0)

    def project(block, carry):
        number = turned_pair(block, group, bits)
        columns = pl.ds(pl.multiple_of(number * tile, tile), tile)
        block_at = pl.ds(pl.multiple_of(block * tile, tile), tile)
        for half, value in enumerate((grad_keys, grad_values)):
            blocks[block_at, half * own_width : (half + 1) * own_width] = lax.dot_general(
                normed_ref[:, columns], value[...], stack, preferred_element_type=f32
            ).astype(bf16)

        @pl.when(block % 2 == 1)
        def _():
            sums.across(block // 2).start()

        return carry

    intake[-1].wait()
    lax.fori_loop(0, 8, project, 0)
    piece = 32

    @pl.when(edge)
    def _():
        hand_on.wait_send()
        for owner in (3 - 3 * side, 1 + 4 * side - mine):
            give(owner).start()

    def add_rows(target, start, source, other_start, count):
        def add(step, carry):
            at = pl.ds(pl.multiple_of(start + step * piece, piece), piece)
            have = pl.ds(pl.multiple_of(other_start + step * piece, piece), piece)
            target[at] = (target[at].astype(f32) + source[have].astype(f32)).astype(target.dtype)
            return carry

        lax.fori_loop(0, count // piece, add, 0)

    for chip in range(4):
        sums.settle(chip)

    @pl.when(jnp.logical_not(edge))
    def _():
        hand_on.wait_recv()
        add_rows(part.at[2 - side], 0, pile, 0, seq_len)
        give(2 - side).start()

    sums.cross()
    sums.close()
    share = tile // experts
    swaps = [
        send_to(
            (group, other),
            blocks.at[pl.ds(pl.multiple_of(other * share, share), share)],
            swapped.at[mine],
            swap_send.at[hop],
            swap_recv.at[hop],
        )
        for hop, other in enumerate(others)
    ]
    for copy in swaps:
        copy.start()

    def hand_out(source, value):
        at = pl.ds(pl.multiple_of(source * own_width, own_width), own_width)
        key_out[:, at] = value[:, :own_width].astype(f32)
        value_out[:, at] = value[:, own_width:].astype(f32)

    hand_out(mine, blocks[pl.ds(pl.multiple_of(mine * share, share), share)])
    for hop in range(1, experts):
        source = (mine + experts - hop) % experts
        swaps[hop - 1].wait_recv()
        hand_out(source, swapped[source])

    home_out[...] = part[mine].astype(f32)
    for hop in range(1, experts):
        source = (mine + hop) % experts
        middle = ((mine + 1) % experts) // 2 == 1

        @pl.when(jnp.logical_not(middle & (source == (mine + 2) % experts)))
        def _():
            got_from(source).wait_recv()

            def add(step, carry):
                at = pl.ds(pl.multiple_of(step * piece, piece), piece)
                home_out[at] = home_out[at] + got[source, at].astype(f32)
                return carry

            lax.fori_loop(0, seq_len // piece, add, 0)

    @pl.when(jnp.logical_not(edge))
    def _():
        give(2 - side).wait_send()

    for owner in (3 - 3 * side, 1 + 4 * side - mine):
        give(owner).wait_send()
    for copy in swaps:
        copy.wait_send()
    sums.drain()


def last_call(rows_back, table, key_own, value_own, grad_keys, grad_values, normed):
    rows = rows_back.shape[0]
    tokens, own = grad_keys.shape
    depth = normed.shape[1]
    experts = 4
    heads_width = own * experts
    seq_len = tokens // experts
    tile = depth // 8
    share = tile // experts
    vmem = pl.BlockSpec(memory_space=pltpu.VMEM)

    def dma(*shape):
        return pltpu.SemaphoreType.DMA(shape)

    def blocks(count):
        return pltpu.VMEM((count * tile, 2 * own), bf16)

    return pl.pallas_call(
        last_kernel,
        out_shape=[
            jax.ShapeDtypeStruct((seq_len, depth), f32),
            jax.ShapeDtypeStruct((share, heads_width), f32),
            jax.ShapeDtypeStruct((share, heads_width), f32),
        ],
        in_specs=[ANY] * 7,
        out_specs=[vmem] * 3,
        scratch_shapes=[
            pltpu.VMEM((rows, depth), bf16),
            pltpu.VMEM((rows, tokens), bf16),
            pltpu.VMEM((depth, own), bf16),
            pltpu.VMEM((depth, own), bf16),
            pltpu.VMEM((tokens, own), bf16),
            pltpu.VMEM((tokens, own), bf16),
            pltpu.VMEM((tokens, depth), bf16),
            dma(7),
            pltpu.VMEM((experts, seq_len, depth), bf16),
            pltpu.VMEM((experts, seq_len, depth), bf16),
            pltpu.VMEM((seq_len, depth), bf16),
            blocks(8),
            blocks(4),
            blocks(3),
            pltpu.VMEM((experts, share, 2 * own), bf16),
            dma(4),
            dma(4),
            dma(6),
            dma(6),
            dma(4),
            dma(4),
            dma(1),
            dma(1),
            dma(3),
            dma(3),
        ],
        compiler_params=pltpu.CompilerParams(
            collective_id=5, has_side_effects=True, vmem_limit_bytes=56 * 1024 * 1024
        ),
        cost_estimate=pl.CostEstimate(
            flops=40_000_000_000, bytes_accessed=150_000_000, transcendentals=0
        ),
        name="attend_last",
    )(rows_back, table, key_own, value_own, grad_keys, grad_values, normed)


def last_plain(rows_back, table, key_own, value_own, grad_keys, grad_values, normed):
    experts = lax.axis_size("expert")
    own_width = grad_keys.shape[1]
    depth = normed.shape[1]
    part = (
        jnp.einsum("rt,rd->td", table, rows_back, preferred_element_type=f32)
        + jnp.einsum("te,de->td", grad_keys, key_own, preferred_element_type=f32)
        + jnp.einsum("te,de->td", grad_values, value_own, preferred_element_type=f32)
    ).astype(bf16)
    home = jnp.sum(exchange(part.reshape(experts, -1, depth)).astype(f32), axis=0)
    both = jnp.einsum(
        "td,te->de",
        normed,
        jnp.concatenate([grad_keys, grad_values], axis=1),
        preferred_element_type=f32,
    ).astype(bf16)
    both = lax.psum_scatter(both, "dp", scatter_dimension=0, tiled=True)
    both = exchange(both.reshape(experts, -1, 2 * own_width))
    both = both.reshape(experts, -1, 2, own_width).transpose(2, 1, 0, 3).astype(f32)
    return home, both[0].reshape(-1, experts * own_width), both[1].reshape(
        -1, experts * own_width
    )


def ffn_plain(own, slopes, picks, router, gate, up, down):
    groups, rows, width = slopes.shape
    depth = own.shape[1]
    held = lax.all_gather(own, "dp", axis=0, tiled=True)
    logits = jnp.einsum("rd,ed->re", held, router, preferred_element_type=f32)
    weight = 1.0 / (1.0 + jnp.exp(jnp.sum(logits * picks, axis=-1, keepdims=True)))
    plain = slopes.reshape(groups * rows, width)
    gate_pre = jnp.einsum("rd,fd->rf", held, gate, preferred_element_type=f32)
    up_pre = jnp.einsum("rd,fd->rf", held, up, preferred_element_type=f32)
    sigmoid = 1.0 / (1.0 + jnp.exp(-gate_pre))
    active = gate_pre * sigmoid
    hidden = (active * up_pre).astype(bf16)
    wide = hidden.astype(f32)
    inner = weight * plain
    grad_gate = (inner * up_pre * (sigmoid * (1.0 + gate_pre * (1.0 - sigmoid)))).astype(bf16)
    grad_up = (inner * active).astype(bf16)
    made = jnp.dot(hidden, down, preferred_element_type=f32).astype(bf16)
    grads = (
        jnp.dot(grad_gate, gate, preferred_element_type=f32)
        + jnp.dot(grad_up, up, preferred_element_type=f32)
    ).astype(bf16)
    grads = lax.psum_scatter(
        grads.reshape(groups, rows, depth), "dp", scatter_dimension=0, tiled=True
    )[0]
    dense = lax.psum_scatter(
        jnp.sum(wide * plain, axis=-1).reshape(groups, rows),
        "dp",
        scatter_dimension=0,
        tiled=True,
    )

    def split(value):
        return value.reshape(groups, rows, value.shape[-1])

    upper = dense[0][:, None].astype(bf16)
    lower = (dense[0][:, None] - upper.astype(f32)).astype(bf16)
    grads = jnp.concatenate([grads, upper, lower, jnp.zeros((rows, 126), bf16)], axis=1)
    scaled = (weight * wide).astype(bf16)
    return (
        split(held),
        split(scaled),
        split(grad_gate),
        split(grad_up),
        split(made),
        grads,
    )


def back_plain(
    grad_rows, rows_flat, places, far, near, output_w, query, key, value, mixture, query_w
):
    experts = lax.axis_size("expert")
    grad_query, keys_part, values_part, output_part = attend_back(
        experts, grad_rows, places, far, output_w, query, key, value, mixture
    )
    output_sum = lax.psum_scatter(output_part, "dp", scatter_dimension=0, tiled=True)
    grad_values = jnp.sum(exchange(values_part).astype(f32), axis=0).astype(bf16)
    grad_keys = jnp.sum(exchange(keys_part).astype(f32), axis=0)
    grad_keys = jnp.concatenate(
        [
            turned_back(grad_keys[:, start : start + HEAD], near)
            for start in range(0, grad_keys.shape[1], HEAD)
        ],
        axis=1,
    ).astype(bf16)
    query_part = jnp.einsum("rd,re->de", rows_flat, grad_query, preferred_element_type=f32)
    rows_back = jnp.einsum("re,de->rd", grad_query, query_w, preferred_element_type=f32)
    return (
        rows_back.astype(bf16),
        grad_keys,
        grad_values,
        output_sum.astype(f32),
        query_part.astype(bf16),
    )


def exchange(value):
    return lax.all_to_all(value, "expert", split_axis=0, concat_axis=0, tiled=True)


def on_device(
    hidden_in,
    out_grad,
    seq_lengths,
    attn_choice,
    moe_choice,
    attn_gain,
    moe_gain,
    attn_router,
    moe_router,
    key_weight,
    value_weight,
    query_weight,
    output_weight,
    gate_weight,
    up_weight,
    down_weight,
):
    experts = lax.axis_size("expert")
    groups = lax.axis_size("dp")
    mine_index = lax.axis_index("expert")
    seq_len = hidden_in.shape[1]
    model_width = hidden_in.shape[2]
    head_width = query_weight.shape[2]
    own_width = head_width // experts
    capacity = 2 * seq_len // experts + 8
    expert_rows = experts * capacity
    total_rows = groups * expert_rows
    score_scale = HEAD ** (-0.5)
    places = jnp.arange(seq_len, dtype=jnp.int32)
    own_length = lax.dynamic_index_in_dim(seq_lengths, mine_index, 0, keepdims=False)
    live_rows = (places < own_length).astype(f32)
    own_attn = lax.dynamic_index_in_dim(attn_choice, mine_index, 0, keepdims=False)
    own_moe = lax.dynamic_index_in_dim(moe_choice, mine_index, 0, keepdims=False)
    kinds = 2 + 2 * experts
    ready = groups == 8 and experts == 4
    near_home = signed_tables(places)
    (
        small_full,
        told_full,
        spread_table,
        row_places,
        cos_far,
        sin_far,
        table_attn,
        table_moe,
        normed_group,
        rows_flat,
        queries,
        keys_all,
        values_all,
        mixture,
        attn_rows,
        value_own,
        key_own,
        query_full,
        output_full,
        given_rows,
    ) = (start_call if ready else start_plain)(
        hidden_in[0],
        attn_gain[None],
        moe_gain[None],
        attn_router.T,
        moe_router.T,
        attn_choice.transpose(2, 0, 1),
        moe_choice.transpose(2, 0, 1),
        seq_lengths[:, None],
        near_home,
        out_grad[0],
        value_weight,
        key_weight,
        query_weight[0],
        output_weight[0],
    )
    far = (cos_far, sin_far)
    near = tuple(jnp.tile(part, (experts, 1)) for part in near_home)
    table_attn = table_attn.reshape(experts, capacity, seq_len)
    table_moe = table_moe.reshape(experts, capacity, seq_len)
    given_all = lax.all_gather(
        given_rows.reshape(expert_rows, model_width), "dp", axis=0, tiled=True
    )
    attn_rows = attn_rows.reshape(experts, capacity, model_width)

    gain_attn = small_full[0].astype(f32)
    gain_moe = small_full[1].astype(f32)
    router_attn = small_full[2 : 2 + experts]
    router_moe = small_full[2 + experts : kinds]
    inputs_f = hidden_in[0].astype(f32)
    scale_one = norm_scale(inputs_f)
    normed_one = (inputs_f * scale_one * gain_attn).astype(bf16)
    attn_logits = jnp.einsum("td,ed->te", normed_one, router_attn, preferred_element_type=f32)
    onehot_attn, shares_attn, dense_attn = router_gates(attn_logits, own_attn, live_rows, experts)

    told = told_full.reshape(groups, 2, experts, seq_len).transpose(1, 0, 2, 3)
    told = told.reshape(2, groups * experts, seq_len).astype(jnp.int32)
    comes = (told[0] == mine_index) | (told[1] == mine_index)
    order = jnp.cumsum(comes.astype(jnp.int32), axis=1) - 1
    slots = jnp.arange(capacity, dtype=jnp.int32)[None, :, None]
    rivals = jnp.sum(
        jnp.where(
            (order[:, None, :] == slots) & comes[:, None, :],
            (told[0] + told[1] - mine_index)[:, None, :],
            0,
        ),
        axis=-1,
    ).reshape(total_rows, 1)
    back_attn = exchange(attn_rows)
    spread_attn = jnp.einsum("ect,ecd->etd", table_attn, back_attn, preferred_element_type=f32)
    attn_sum = jnp.sum(dense_attn.T[:, :, None] * spread_attn, axis=0)
    middle = inputs_f + attn_sum
    scale_two = norm_scale(middle)
    normed_two = (middle * scale_two * gain_moe).astype(bf16)
    moe_logits = jnp.einsum("td,ed->te", normed_two, router_moe, preferred_element_type=f32)
    onehot_moe, shares_moe, dense_moe = router_gates(moe_logits, own_moe, live_rows, experts)
    send_moe = jnp.einsum(
        "ect,td->ecd", table_moe, normed_two, preferred_element_type=f32
    ).astype(bf16)
    rows_moe = exchange(send_moe).reshape(expert_rows, model_width)

    units = gate_weight.shape[2]
    room = -(-units // 256) * 256
    gate_slice = jnp.pad(gate_weight[0].T.astype(bf16), ((0, room - units), (0, 0)))
    up_slice = jnp.pad(up_weight[0].T.astype(bf16), ((0, room - units), (0, 0)))
    down_slice = jnp.pad(down_weight[0].astype(bf16), ((0, room - units), (0, 0)))
    slopes = jnp.einsum("rd,fd->rf", given_all, down_slice, preferred_element_type=f32)
    expert_ids = jnp.arange(16, dtype=jnp.int32)[None, :]
    picks = (expert_ids == rivals).astype(f32) - (
        expert_ids == mine_index
    ).astype(f32)
    router_rows = jnp.pad(router_moe, ((0, 16 - experts), (0, 0)))
    feed = ffn_call if groups == 8 and expert_rows % 96 == 0 else ffn_plain
    ffn_rows, scaled, grad_gate, grad_up, partial_out, grad_ffn = feed(
        rows_moe,
        slopes.reshape(groups, expert_rows, room),
        picks,
        router_rows,
        gate_slice,
        up_slice,
        down_slice,
    )
    back_moe_grad = exchange(grad_ffn.reshape(experts, capacity, model_width + 128))
    summed_out = lax.psum_scatter(partial_out, "dp", scatter_dimension=0, tiled=True)
    ffn_rows = ffn_rows.reshape(total_rows, model_width)
    down_grad = jnp.einsum(
        "rf,rd->fd",
        scaled.reshape(total_rows, room)[:, :units],
        given_all,
        preferred_element_type=f32,
    )[None]
    gate_grad = jnp.einsum(
        "rd,rf->df",
        ffn_rows,
        grad_gate.reshape(total_rows, room)[:, :units],
        preferred_element_type=f32,
    )[None]
    up_grad = jnp.einsum(
        "rd,rf->df",
        ffn_rows,
        grad_up.reshape(total_rows, room)[:, :units],
        preferred_element_type=f32,
    )[None]
    back_moe_grad, down_grad, gate_grad = lax.optimization_barrier(
        (back_moe_grad, down_grad, gate_grad)
    )
    back_dense = jnp.sum(back_moe_grad[:, :, model_width:].astype(f32), axis=-1)
    back_moe_grad = back_moe_grad[:, :, :model_width]

    grad_out = out_grad[0].astype(f32) * live_rows[:, None]
    grad_dense_moe = jnp.sum(table_moe.astype(f32) * back_dense[:, :, None], axis=1).T
    grad_normed_two = jnp.einsum(
        "ect,ecd->td", table_moe, back_moe_grad, preferred_element_type=f32
    )
    grad_logits_moe = gates_backward(grad_dense_moe, onehot_moe, shares_moe, live_rows)
    grad_normed_two = grad_normed_two + jnp.dot(
        grad_logits_moe, router_moe.astype(f32), precision=highest
    )
    moe_router_part = jnp.dot(grad_logits_moe.T, normed_two.astype(f32), precision=highest)
    grad_middle_norm, moe_gain_part = norm_backward(grad_normed_two, middle, scale_two, gain_moe)
    grad_middle = grad_out + grad_middle_norm
    grad_dense_attn = jnp.sum(grad_middle[None] * spread_attn, axis=-1).T
    rows_attn_grad = (dense_attn.T[:, :, None] * grad_middle[None]).astype(bf16)
    send_attn_grad = jnp.einsum(
        "ect,etd->ecd", table_attn, rows_attn_grad, preferred_element_type=f32
    ).astype(bf16)
    recv_attn_grad = exchange(send_attn_grad)
    recv_attn_grad, up_grad, summed_out = lax.optimization_barrier(
        (recv_attn_grad, up_grad, summed_out)
    )

    backward = back_call if ready else back_plain
    rows_back, grad_keys, grad_values, output_out, query_part = backward(
        recv_attn_grad.reshape(expert_rows, model_width),
        rows_flat,
        row_places,
        far,
        near,
        output_full,
        queries,
        keys_all,
        values_all,
        mixture,
        query_full,
    )
    query_out = lax.psum_scatter(query_part, "dp", scatter_dimension=0, tiled=True)
    grad_normed_one, key_grad, value_grad = (last_call if ready else last_plain)(
        rows_back, spread_table, key_own, value_own, grad_keys, grad_values, normed_group
    )
    grad_normed_one, summed_out = lax.optimization_barrier((grad_normed_one, summed_out))
    back_moe = exchange(summed_out[0].reshape(experts, capacity, model_width))
    spread_moe = jnp.einsum("ect,ecd->etd", table_moe, back_moe, preferred_element_type=f32)
    moe_sum = jnp.sum(dense_moe.T[:, :, None] * spread_moe, axis=0)
    block_out = (live_rows[:, None] * (middle + moe_sum)).astype(bf16)[None]
    grad_logits_attn = gates_backward(grad_dense_attn, onehot_attn, shares_attn, live_rows)
    attn_router_part = jnp.dot(grad_logits_attn.T, normed_one.astype(f32), precision=highest)
    grad_normed_one = grad_normed_one + jnp.dot(
        grad_logits_attn, router_attn.astype(f32), precision=highest
    )
    grad_inputs_norm, attn_gain_part = norm_backward(
        grad_normed_one, inputs_f, scale_one, gain_attn
    )
    input_grad = (grad_middle + grad_inputs_norm).astype(bf16)[None]
    smalls = total_small(
        jnp.concatenate(
            [attn_gain_part[None], moe_gain_part[None], attn_router_part, moe_router_part]
        )
    )
    return (
        block_out,
        input_grad,
        smalls[0],
        smalls[1],
        smalls[2 : 2 + experts].T,
        smalls[2 + experts : kinds].T,
        key_grad,
        value_grad,
        query_out.astype(f32)[None],
        output_out[None],
        gate_grad,
        up_grad,
        down_grad,
    )


def solution(mesh):
    placed = (
        P(("dp", "expert"), None, None),
        P(("dp", "expert"), None, None),
        P("dp"),
        P("dp", None, None),
        P("dp", None, None),
        P("dp"),
        P("dp"),
        P("dp", None),
        P("dp", None),
        P("dp", None),
        P("dp", None),
        P("expert", "dp", None),
        P("expert", "dp", None),
        P("expert", None, "dp"),
        P("expert", None, "dp"),
        P("expert", "dp", None),
    )
    return jax.shard_map(
        on_device,
        mesh=mesh,
        in_specs=placed,
        out_specs=(
            P(("dp", "expert"), None, None),
            P(("dp", "expert"), None, None),
            P(("dp", "expert")),
            P(("dp", "expert")),
            P(("dp", "expert"), None),
            P(("dp", "expert"), None),
            P(("dp", "expert"), None),
            P(("dp", "expert"), None),
            P("expert", "dp", None),
            P("expert", "dp", None),
            P("expert", None, "dp"),
            P("expert", None, "dp"),
            P("expert", "dp", None),
        ),
        check_vma=False,
    )
```
